32 devices in a mesh: seq: 16 (over z, y, x), head: 2 (over core).
Axes of the slice: x: 2, y: 2, z: 4, core: 2. Of those that a mesh axis runs over, the one named last changes fastest.
Arguments:
- block_input: bfloat16 [8192, 768], P('seq', 'head'), may hold values from -6 to 6
- starts: int32 [8192], P('seq'), may hold values from 0 to 1, as said below
- decay_rate: float32 [12, 8192], P('head', 'seq'), may hold values from 0 to 1
- norm1_gain: float32 [768], replicated, may hold values from 0.5 to 1.5
- norm1_bias: float32 [768], replicated, may hold values from -1.5 to 1.5
- q_weight: bfloat16 [768, 768], P(None, 'head'), may hold values from -0.21875 to 0.21875
- k_weight: bfloat16 [768, 768], P(None, 'head'), may hold values from -0.21875 to 0.21875
- v_weight: bfloat16 [768, 768], P(None, 'head'), may hold values from -0.21875 to 0.21875
- shift_kernel: bfloat16 [64, 768], P(None, 'head'), may hold values from -0.75 to 0.75
- out_weight: bfloat16 [768, 768], P(None, 'head'), may hold values from -0.3125 to 0.3125
- norm2_gain: float32 [768], replicated, may hold values from 0.5 to 1.5
- norm2_bias: float32 [768], replicated, may hold values from -1.5 to 1.5
- up_weight: bfloat16 [768, 3072], P(None, 'head'), may hold values from -0.21875 to 0.21875
- down_weight: bfloat16 [768, 3072], P(None, 'head'), may hold values from -0.109375 to 0.109375
- out_grad: bfloat16 [8192, 768], P('seq', 'head'), may hold values from -6 to 6
Outputs:
- block_output: bfloat16 [8192, 768], P('seq', 'head')
- input_grad: bfloat16 [8192, 768], P('seq', 'head')
- norm1_gain_grad: float32 [768], replicated
- norm1_bias_grad: float32 [768], replicated
- q_weight_grad: float32 [768, 768], P('seq', 'head')
- k_weight_grad: float32 [768, 768], P('seq', 'head')
- v_weight_grad: float32 [768, 768], P('seq', 'head')
- shift_kernel_grad: float32 [64, 768], P(None, 'head')
- out_weight_grad: float32 [768, 768], P('seq', 'head')
- norm2_gain_grad: float32 [768], replicated
- norm2_bias_grad: float32 [768], replicated
- up_weight_grad: float32 [768, 3072], P('seq', 'head')
- down_weight_grad: float32 [768, 3072], P('seq', 'head')
The draws below stay inside these ranges and needn't reach their ends.
Inputs may be any that keep to these rules, and one draw needn't show every extreme that they name: `starts`: the first token is 1.
All inputs are finite; a program needn't handle non-finite values.
Results may differ from the reference program's by a relative error of at most 0.017.
Values may be sent and summed in bfloat16 or wider, within the bound.
No kernel may reach another device: no remote copies, remote signals or barrier semaphores. Data moves between devices by JAX's collectives and lax.ppermute only.
A program may use at most 192 MiB of HBM per device.

```python
from functools import partial
import jax
import jax.numpy as jnp
from jax import lax

D = 768
HEAD_TOTAL = 12
DH = 64
FF = 3072
STATE = 64
TOK_DEV = 512
TOKEN_TOTAL = 8192


def draw_starts(key, part):
    key_sequence = jax.random.split(key, 5)
    device_count = TOKEN_TOTAL // TOK_DEV
    position = jnp.arange(TOKEN_TOTAL, dtype=jnp.int32)
    device_of = position // TOK_DEV
    local = position - device_of * TOK_DEV
    level = jax.random.randint(key_sequence[0], (device_count,), 0, 10)
    odds = jnp.left_shift(jnp.full((device_count,), max(2, TOK_DEV // 8), jnp.int32), level)
    odds_rows = jnp.repeat(odds, TOK_DEV, total_repeat_length=TOKEN_TOTAL)
    placed = jax.random.randint(key_sequence[1], (TOKEN_TOTAL,), 0, odds_rows) == 0
    edge_dev = jax.random.randint(key_sequence[2], (device_count,), 0, 4) == 0
    near_dev = jax.random.randint(key_sequence[3], (device_count,), 0, 4) == 0
    offset = jax.random.randint(key_sequence[4], (device_count,), 1, max(2, STATE))
    edge_hit = jnp.repeat(edge_dev, TOK_DEV, total_repeat_length=TOKEN_TOTAL) & (local == 0)
    near_hit = jnp.repeat(near_dev, TOK_DEV, total_repeat_length=TOKEN_TOTAL) & (local == jnp.repeat(offset, TOK_DEV, total_repeat_length=TOKEN_TOTAL))
    span = min(8, max(1, device_count // 4)) * TOK_DEV
    bounds = jnp.array([1, device_count // 2, device_count // 2 + 1, device_count - 1], dtype=jnp.int32) * TOK_DEV
    guarded = jnp.any((position[None, :] >= bounds[:, None] - span) & (position[None, :] < bounds[:, None] + TOK_DEV // 2), axis=0)
    chosen = (placed | edge_hit | near_hit) & jnp.logical_not(guarded) | (position == 0)
    return chosen.astype(jnp.int32)


def draw_decay_rate(key, part):
    key_sequence = jax.random.split(key, 7)
    device_count = TOKEN_TOTAL // TOK_DEV
    fast_head = jax.random.randint(key_sequence[0], (HEAD_TOTAL, 1), 0, 2) == 0
    coarse_rate = jnp.exp(jax.random.uniform(key_sequence[4], (HEAD_TOTAL, TOKEN_TOTAL), minval=jnp.log(0.5), maxval=0.0))
    fast_rate = 1.0 / jax.random.uniform(key_sequence[1], (HEAD_TOTAL, 1), minval=30.0, maxval=50.0)
    slow_rate = jnp.exp(jax.random.uniform(key_sequence[2], (HEAD_TOTAL, 1), minval=jnp.log(0.1), maxval=jnp.log(0.5))) / TOKEN_TOTAL
    baseline_rate = jnp.where(fast_head, fast_rate, slow_rate)
    processor_multiplier = jnp.exp(jax.random.uniform(key_sequence[3], (HEAD_TOTAL, device_count, 1), minval=jnp.log(0.5), maxval=jnp.log(2.0)))
    processor_multiplier = jnp.broadcast_to(processor_multiplier, (HEAD_TOTAL, device_count, TOK_DEV)).reshape(HEAD_TOTAL, TOKEN_TOTAL)
    spike_position = jax.random.randint(key_sequence[5], (3,), 0, TOKEN_TOTAL)
    spike_mask = jnp.any(jnp.arange(TOKEN_TOTAL)[None, :] == spike_position[:, None], axis=0).astype(jnp.float32)
    spike_length = -jnp.log(jax.random.uniform(key_sequence[6], (HEAD_TOTAL, TOKEN_TOTAL), minval=0.5, maxval=0.8))
    return (baseline_rate * processor_multiplier * coarse_rate + spike_mask[None, :] * spike_length).astype(jnp.float32)


def shard_levels(rng, shape, pieces, smallest, largest):
    level = 1.0
    for axis_at, parts in pieces:
        steps = jax.random.uniform(jax.random.fold_in(jax.random.fold_in(rng, 6), axis_at), (parts,), jnp.float32, smallest / len(pieces), largest / len(pieces))
        level = level * jnp.repeat(jnp.exp(steps), shape[axis_at] // parts).reshape((-1,) + (1,) * (len(shape) - 1 - axis_at))
    return level


def normal_values(own_key, shape, deviation, most, pieces=(), kind=jnp.bfloat16):
    drawn = jax.random.normal(own_key, shape, jnp.float32) * deviation
    if len(pieces) > 0:
        drawn = shard_levels(own_key, shape, pieces, -0.22, 0.18) * drawn
    return jnp.clip(drawn, min=-most, max=most).astype(kind)


def setup_inputs(seed: int = 0) -> dict:
    key_of = jax.random.split(jax.random.key(seed), 16)
    block_input = normal_values(key_of[0], (TOKEN_TOTAL, D), 1.0, 6.0, ((0, 16), (1, 2)))
    starts = draw_starts(jax.random.fold_in(key_of[15], 71), 0)
    decay_rate = draw_decay_rate(jax.random.fold_in(key_of[15], 71), 0)
    norm1_gain = jnp.clip(1.0 + 0.1 * jax.random.normal(key_of[3], (D,), jnp.float32), 0.5, 1.5)
    norm1_bias = normal_values(key_of[4], (D,), 0.3, 1.5, (), jnp.float32)
    q_weight = normal_values(key_of[5], (D, D), D ** -0.5, 0.21875, ((1, 2),))
    k_weight = normal_values(key_of[6], (D, D), D ** -0.5, 0.21875, ((1, 2),))
    v_weight = normal_values(key_of[7], (D, D), D ** -0.5, 0.21875, ((1, 2),))
    shift_kernel = normal_values(key_of[8], (STATE, D), STATE ** -0.5, 0.75, ((1, 2),))
    out_weight = normal_values(key_of[9], (D, D), (D // 2) ** -0.5, 0.3125, ((1, 2),))
    norm2_gain = jnp.clip(1.0 + 0.1 * jax.random.normal(key_of[10], (D,), jnp.float32), 0.5, 1.5)
    norm2_bias = normal_values(key_of[11], (D,), 0.3, 1.5, (), jnp.float32)
    up_weight = normal_values(key_of[12], (D, FF), D ** -0.5, 0.21875, ((1, 2),))
    down_weight = normal_values(key_of[13], (D, FF), FF ** -0.5, 0.109375, ((1, 2),))
    out_grad = normal_values(key_of[14], (TOKEN_TOTAL, D), 1.0, 6.0, ((0, 16), (1, 2)))
    return {"block_input": block_input, "starts": starts, "decay_rate": decay_rate, "norm1_gain": norm1_gain, "norm1_bias": norm1_bias, "q_weight": q_weight, "k_weight": k_weight, "v_weight": v_weight, "shift_kernel": shift_kernel, "out_weight": out_weight, "norm2_gain": norm2_gain, "norm2_bias": norm2_bias, "up_weight": up_weight, "down_weight": down_weight, "out_grad": out_grad}


@jax.custom_vjp
def low(v):
    return lax.optimization_barrier(v.astype(jnp.bfloat16)).astype(jnp.float32)

@jax.custom_vjp
def low_back(v):
    return v

def low_keep(v):
    return (low(v), None)

def low_pass(kept, grad):
    return (grad,)

def back_keep(v):
    return (v, None)

def back_low(kept, grad):
    return (low(grad),)
low.defvjp(low_keep, low_pass)
low_back.defvjp(back_keep, back_low)
NORM_EPS = 1e-05
RATE_CAP = 0.05
HIGHEST = lax.Precision.HIGHEST

def layer_norm(rows_in, gain_vec, bias_vec):
    center = rows_in - lax.optimization_barrier(jnp.mean(rows_in, axis=-1, keepdims=True))
    spread = lax.optimization_barrier(jnp.mean(center * center, axis=-1, keepdims=True))
    return center * lax.rsqrt(spread + NORM_EPS) * gain_vec + bias_vec

def matmul(left_side, right_side):
    return jnp.dot(left_side, right_side, precision=HIGHEST, preferred_element_type=jnp.float32)

def block_step(params, carry_in, inputs):
    gain_one, bias_one, weight_q, weight_k, weight_v, kernel, weight_out, gain_two, bias_two, weight_up, weight_down = params
    state_in, key_tail = carry_in
    x_block, start_block, dist_block, rate_block = inputs
    length = x_block.shape[0]
    edge_rows = STATE - 1
    normed = low(layer_norm(x_block, gain_one, bias_one))
    query_rows = low(low_back(matmul(normed, weight_q)))
    key_rows = low(low_back(matmul(normed, weight_k)))
    value_rows = low(low_back(matmul(normed, weight_v)))
    padded = jnp.concatenate([key_tail, key_rows], axis=0)
    shifted = jnp.zeros_like(key_rows)
    for tap_index in range(STATE):
        keep_mask = (dist_block >= tap_index).astype(jnp.float32)[:, None]
        shifted = shifted + keep_mask * kernel[tap_index][None, :] * padded[edge_rows - tap_index:edge_rows - tap_index + length]
    gain_in = jnp.sqrt(-jnp.expm1(-2.0 * jnp.minimum(rate_block, RATE_CAP)))
    scaled_key = low(shifted.reshape(length, HEAD_TOTAL, DH) * gain_in[:, :, None])
    query_heads = query_rows.reshape(length, HEAD_TOTAL, DH)
    value_heads = value_rows.reshape(length, HEAD_TOTAL, DH)
    cumulative = jnp.cumsum(rate_block, axis=0).T
    doc_index = jnp.cumsum(start_block, dtype=jnp.int32)
    place_rows = jnp.arange(length, dtype=jnp.int32)
    same_doc = (doc_index[:, None] == doc_index[None, :]) & (place_rows[:, None] >= place_rows[None, :])
    decay_mat = jnp.where(same_doc[None], jnp.exp(jnp.minimum(cumulative[:, None, :] - cumulative[:, :, None], 0.0)), 0.0)
    scores = low_back(jnp.einsum('thd,shd->hts', query_heads, scaled_key, precision=HIGHEST))
    weights_low = low(scores * decay_mat)
    first_w = jnp.where(doc_index[None, :] == 0, jnp.exp(-cumulative), 0.0)
    from_state = jnp.einsum('thd,hde->the', query_heads, state_in, precision=HIGHEST)
    inside = jnp.einsum('hts,shd->thd', weights_low, value_heads, precision=HIGHEST)
    mixed_rows = 0.125 * (inside + first_w.T[:, :, None] * from_state)
    last_w = jnp.where(doc_index[None, :] == doc_index[-1], jnp.exp(cumulative - cumulative[:, -1:]), 0.0)
    block_state = jnp.einsum('shd,she->hde', scaled_key * last_w.T[:, :, None], value_heads, precision=HIGHEST)
    block_gate = jnp.where(doc_index[-1] == 0, jnp.exp(-cumulative[:, -1]), 0.0)
    new_state = block_gate[:, None, None] * state_in + block_state
    attn_in = low(low_back(mixed_rows.reshape(length, D)))
    branch = low_back(jnp.einsum('th,dh->td', attn_in, weight_out, precision=HIGHEST))
    residual = x_block + branch
    normed_two = low(layer_norm(residual, gain_two, bias_two))
    pre_act = low_back(matmul(normed_two, weight_up))
    hidden = low(jax.nn.gelu(pre_act, approximate=True))
    output = residual + jnp.einsum('tf,df->td', hidden, weight_down, precision=HIGHEST)
    return ((new_state, padded[length:]), output)

def reference(block_input, starts, decay_rate, norm1_gain, norm1_bias, q_weight, k_weight, v_weight, shift_kernel, out_weight, norm2_gain, norm2_bias, up_weight, down_weight, out_grad):
    length = 512 if TOK_DEV % 512 == 0 else TOK_DEV
    block_count = TOKEN_TOTAL // length
    position = jnp.arange(TOKEN_TOTAL, dtype=jnp.int32)
    last_start = lax.cummax(jnp.where(starts > 0, position, jnp.zeros_like(position)), axis=0)
    distance = (position - last_start).astype(jnp.int32)
    side_inputs = (starts.reshape(block_count, length), distance.reshape(block_count, length), decay_rate.T.reshape(block_count, length, HEAD_TOTAL))
    params = tuple((weight_item.astype(jnp.float32) for weight_item in (norm1_gain, norm1_bias, q_weight, k_weight, v_weight, shift_kernel, out_weight, norm2_gain, norm2_bias, up_weight, down_weight)))

    def forward(weights, x_float):
        step_fn = jax.checkpoint(partial(block_step, weights))
        start_carry = (jnp.zeros((HEAD_TOTAL, DH, DH), jnp.float32), jnp.zeros((STATE - 1, D), jnp.float32))
        final_carry, outputs = lax.scan(step_fn, start_carry, (x_float.reshape(block_count, length, D),) + side_inputs)
        return outputs.reshape(TOKEN_TOTAL, D)
    output, pullback = jax.vjp(forward, params, block_input.astype(jnp.float32))
    weight_grads, input_grad = pullback(out_grad.astype(jnp.float32))
    return (output.astype(jnp.bfloat16), input_grad.astype(jnp.bfloat16), weight_grads[0], weight_grads[1], weight_grads[2], weight_grads[3], weight_grads[4], weight_grads[5], weight_grads[6], weight_grads[7], weight_grads[8], weight_grads[9], weight_grads[10])
```

```python
import jax
import jax.numpy as jnp
from jax import lax
from jax.sharding import PartitionSpec as P

NORM_EPS = 1e-05
RATE_CAP = 0.05
FAR_BACK = 1 << 20
HIGHEST = lax.Precision.HIGHEST


def passed_along(array, axis, by):
    count = lax.axis_size(axis)
    pairs = [(i, i + by) for i in range(count) if 0 <= i + by < count]
    return lax.ppermute(array, axis, pairs)


def digits_of(count):
    digits, stride = [], 1
    while count > 1:
        radix = 4 if count % 4 == 0 else (2 if count % 2 == 0 else count)
        digits.append((stride, radix))
        stride, count = stride * radix, count // radix
    return digits


def turned(array, stride, radix, by):
    count = lax.axis_size("seq")
    pairs = []
    for i in range(count):
        member = i // stride % radix
        pairs.append((i, i + ((member + by) % radix - member) * stride))
    return lax.ppermute(array, "seq", pairs)


def crossed(array, stride, radix, mask):
    count = lax.axis_size("seq")
    pairs = []
    for i in range(count):
        member = i // stride % radix
        pairs.append((i, i + ((member ^ mask) - member) * stride))
    return lax.ppermute(array, "seq", pairs)


def swapped(array):
    count = lax.axis_size("head")
    return lax.ppermute(array, "head", [(i, (i + 1) % count) for i in range(count)])


def pair_sum(array):
    low = array.astype(jnp.bfloat16)
    return low.astype(jnp.float32) + swapped(low).astype(jnp.float32)


def scattered_sum(parts):
    count = lax.axis_size("seq")
    mine = lax.axis_index("seq")
    rows = parts.shape[0] // count
    held = parts.reshape(count, rows, parts.shape[1])
    for stride, radix in digits_of(count):
        held = held.reshape(-1, radix, rows, held.shape[-1])
        member = mine // stride % radix
        total = lax.dynamic_index_in_dim(held, member, 1, keepdims=False).astype(jnp.float32)
        for by in range(1, radix):
            piece = lax.dynamic_index_in_dim(held, (member + by) % radix, 1, keepdims=False)
            got = turned(piece.astype(jnp.bfloat16), stride, radix, by)
            total = total + got.astype(jnp.float32)
        held = total
    return held.reshape(rows, -1)


def summed(arrays):
    count = lax.axis_size("seq")
    for stride, radix in digits_of(count):
        got = [
            [a] + [crossed(a, stride, radix, mask) for mask in range(1, radix)] for a in arrays
        ]
        arrays = [
            ((g[0] + g[1]) + (g[2] + g[3])) if radix == 4 else sum(g) for g in got
        ]
    return arrays


def entering(array, combine, identity, reverse):
    count = lax.axis_size("seq")
    mine = lax.axis_index("seq")
    sign = -1 if reverse else 1
    before, total = identity, array
    for stride, radix in digits_of(count):
        member = mine // stride % radix
        if reverse:
            member = radix - 1 - member
        sent = jax.tree.map(lambda a: a.astype(jnp.bfloat16), total)
        own = total
        got = [
            jax.tree.map(
                lambda s, a: turned(s, stride, radix, sign * by % radix).astype(a.dtype), sent, total
            )
            for by in range(1, radix)
        ]
        lower = identity
        for by in range(radix - 1, 0, -1):
            kept = jax.tree.map(
                lambda a, zero: jnp.where(by <= member, a, zero), got[by - 1], identity
            )
            lower = combine(lower, kept)
        upper = identity
        for by in range(radix - 1, 0, -1):
            kept = jax.tree.map(
                lambda a, zero: jnp.where(by > member, a, zero), got[by - 1], identity
            )
            upper = combine(upper, kept)
        before = combine(lower, before)
        total = combine(combine(lower, own), upper)
    return before


def as_sent(array):
    return jax.tree.map(lambda a: a.astype(jnp.bfloat16) if a.dtype == jnp.float32 else a, array)


def norm_forward(rows_in, gain_vec, bias_vec):
    center = rows_in - jnp.mean(rows_in, axis=-1, keepdims=True)
    inverse = lax.rsqrt(jnp.mean(center * center, axis=-1, keepdims=True) + NORM_EPS)
    unit_rows = center * inverse
    return (unit_rows * gain_vec + bias_vec, unit_rows, inverse)


def norm_backward(grad_rows, unit_rows, inverse, gain_vec):
    scaled = grad_rows * gain_vec
    return inverse * (
        scaled
        - jnp.mean(scaled, axis=-1, keepdims=True)
        - unit_rows * jnp.mean(scaled * unit_rows, axis=-1, keepdims=True)
    )


def gelu_tanh(pre_act):
    return jax.nn.gelu(pre_act, approximate=True)


def chain(earlier_part, later_part):
    return (
        earlier_part[0] * later_part[0],
        later_part[0][:, None, None] * earlier_part[1] + later_part[1],
    )


def local(
    block_input,
    starts,
    decay_rate,
    norm1_gain,
    norm1_bias,
    q_weight,
    k_weight,
    v_weight,
    shift_kernel,
    out_weight,
    norm2_gain,
    norm2_bias,
    up_weight,
    down_weight,
    out_grad,
):
    tok_rows, half_width = block_input.shape
    head_count = decay_rate.shape[0]
    head_width = half_width // head_count
    tap_count = shift_kernel.shape[0]
    edge_rows = tap_count - 1
    block_len = 512
    block_count = tok_rows // block_len
    head_size = lax.axis_size("head")
    head_index = lax.axis_index("head")
    full_width = half_width * head_size
    own_start = head_index * half_width
    row_count = tok_rows // head_size
    row_start = head_index * row_count
    position = jnp.arange(tok_rows, dtype=jnp.int32)
    last_start = lax.cummax(jnp.where(starts > 0, position, -FAR_BACK), axis=0)
    distance = position - last_start
    tail_mask = (position[tok_rows - edge_rows :] >= last_start[tok_rows - 1]).astype(jnp.float32)[
        :, None
    ]
    whole_input, whole_grad = (
        lax.all_gather(block_input, "head", axis=1, tiled=True),
        lax.all_gather(out_grad, "head", axis=1, tiled=True),
    )
    normed_one, unit_one, inverse_one = norm_forward(
        whole_input.astype(jnp.float32), norm1_gain, norm1_bias
    )
    normed_one = normed_one.astype(jnp.bfloat16)
    query_rows = jnp.dot(normed_one, q_weight, preferred_element_type=jnp.float32).astype(
        jnp.bfloat16
    )
    key_rows = jnp.dot(normed_one, k_weight, preferred_element_type=jnp.float32).astype(
        jnp.bfloat16
    )
    value_rows = jnp.dot(normed_one, v_weight, preferred_element_type=jnp.float32).astype(
        jnp.bfloat16
    )
    tail_send = (key_rows[tok_rows - edge_rows :] * tail_mask).astype(jnp.bfloat16)
    prev_tail = passed_along(tail_send, "seq", 1)
    padded = jnp.concatenate([prev_tail, key_rows], axis=0)
    kernel = shift_kernel.astype(jnp.float32)
    shifted = jnp.zeros((tok_rows, half_width), jnp.float32)
    for tap_index in range(tap_count):
        keep_mask = (distance >= tap_index).astype(jnp.float32)[:, None]
        shifted = shifted + keep_mask * kernel[tap_index][None, :] * padded[
            edge_rows - tap_index : edge_rows - tap_index + tok_rows
        ].astype(jnp.float32)
    gain_in = jnp.sqrt(-jnp.expm1(-2.0 * jnp.minimum(decay_rate, RATE_CAP)))
    scaled_key = (shifted.reshape(tok_rows, head_count, head_width) * gain_in.T[:, :, None]).astype(
        jnp.bfloat16
    )
    query_blocks = query_rows.reshape(block_count, block_len, head_count, head_width)
    key_blocks = scaled_key.reshape(block_count, block_len, head_count, head_width)
    value_blocks = value_rows.reshape(block_count, block_len, head_count, head_width)
    cumulative = jnp.cumsum(
        decay_rate.reshape(head_count, block_count, block_len).transpose(1, 0, 2), axis=-1
    )
    doc_index = jnp.cumsum(starts.reshape(block_count, block_len), axis=1, dtype=jnp.int32)
    place_rows = jnp.arange(block_len, dtype=jnp.int32)
    same_doc = (doc_index[:, :, None] == doc_index[:, None, :]) & (
        place_rows[:, None] >= place_rows[None, :]
    )[None]
    decay_mat = jnp.where(
        same_doc[:, None],
        jnp.exp(jnp.minimum(cumulative[:, :, None, :] - cumulative[:, :, :, None], 0.0)),
        0.0,
    )
    first_w = jnp.where(doc_index[:, None, :] == 0, jnp.exp(-cumulative), 0.0)
    last_w = jnp.where(
        doc_index[:, None, :] == doc_index[:, None, -1:],
        jnp.exp(cumulative - cumulative[:, :, -1:]),
        0.0,
    )
    block_gate = jnp.where(doc_index[:, -1:] == 0, jnp.exp(-cumulative[:, :, -1]), 0.0)
    first_rows = first_w.transpose(0, 2, 1)[..., None]
    last_rows = last_w.transpose(0, 2, 1)[..., None]
    scores = jnp.einsum(
        "bthd,bshd->bhts", query_blocks, key_blocks, preferred_element_type=jnp.float32
    )
    weights_low = (scores * decay_mat).astype(jnp.bfloat16)
    inside = jnp.einsum(
        "bhts,bshd->bthd", weights_low, value_blocks, preferred_element_type=jnp.float32
    )
    value_float = value_blocks.astype(jnp.float32)
    weighted_key = key_blocks.astype(jnp.float32) * last_rows
    block_state = jnp.einsum("bshd,bshe->bhde", weighted_key, value_float, precision=HIGHEST)
    carried = jnp.zeros((head_count, head_width, head_width), jnp.float32)
    through = jnp.ones((head_count,), jnp.float32)
    block_index = 0
    local_inits = [carried]
    pass_factors = [through]
    carried = block_gate[block_index][:, None, None] * carried + block_state[block_index]
    through = through * block_gate[block_index]
    identity = (
        jnp.ones((head_count,), jnp.float32),
        jnp.zeros((head_count, head_width, head_width), jnp.float32),
    )
    prefix_gate, incoming = entering((through, carried), chain, identity, False)
    pass_stack = jnp.stack(pass_factors)[:, :, None, None]
    block_init = jnp.stack(local_inits) + pass_stack * incoming[None]
    query_float = query_blocks.astype(jnp.float32)
    from_state = jnp.einsum("bthd,bhde->bthe", query_float, block_init, precision=HIGHEST)
    mixed_rows = (
        (0.125 * (inside + first_rows * from_state))
        .reshape(tok_rows, half_width)
        .astype(jnp.bfloat16)
    )
    attn_part = jnp.einsum("th,dh->td", mixed_rows, out_weight, preferred_element_type=jnp.float32)
    attn_own = lax.psum_scatter(
        attn_part.astype(jnp.bfloat16), "head", scatter_dimension=1, tiled=True
    ).astype(jnp.float32)
    residual = block_input.astype(jnp.float32) + attn_own
    whole_resid = lax.all_gather(residual.astype(jnp.bfloat16), "head", axis=1, tiled=True).astype(
        residual.dtype
    )
    normed_two, unit_two, inverse_two = norm_forward(whole_resid, norm2_gain, norm2_bias)
    normed_two = normed_two.astype(jnp.bfloat16)
    pre_act = jnp.dot(normed_two, up_weight, preferred_element_type=jnp.float32)
    hidden = gelu_tanh(pre_act).astype(jnp.bfloat16)
    ffn_part = jnp.einsum("tf,df->td", hidden, down_weight, preferred_element_type=jnp.float32)
    ffn_own = lax.psum_scatter(
        ffn_part.astype(jnp.bfloat16), "head", scatter_dimension=1, tiled=True
    ).astype(jnp.float32)
    block_output = (residual + ffn_own).astype(jnp.bfloat16)
    hidden_grad = jnp.dot(whole_grad, down_weight, preferred_element_type=jnp.float32)
    gelu_value, gelu_pull = jax.vjp(gelu_tanh, pre_act)
    pre_grad = gelu_pull(hidden_grad)[0].astype(jnp.bfloat16)
    down_grad = jnp.einsum("td,tf->df", whole_grad, hidden, preferred_element_type=jnp.float32)
    up_grad = jnp.einsum("td,tf->df", normed_two, pre_grad, preferred_element_type=jnp.float32)
    ffn_total = (
        scattered_sum(up_grad),
        scattered_sum(down_grad),
    )
    norm2_part = jnp.einsum("tf,df->td", pre_grad, up_weight, preferred_element_type=jnp.float32)
    norm2_full = pair_sum(norm2_part)
    norm2_half = lax.dynamic_slice_in_dim(norm2_full, row_start, row_count, axis=0)
    unit_half = lax.dynamic_slice_in_dim(unit_two, row_start, row_count, axis=0)
    gain2_grad = jnp.sum(norm2_half * unit_half, axis=0)
    bias2_grad = jnp.sum(norm2_half, axis=0)
    resid_back = norm_backward(norm2_full, unit_two, inverse_two, norm2_gain)
    resid_grad = out_grad.astype(jnp.float32) + lax.dynamic_slice_in_dim(
        resid_back, own_start, half_width, axis=1
    )
    branch_grad = resid_grad.astype(jnp.bfloat16)
    whole_branch = lax.all_gather(branch_grad, "head", axis=1, tiled=True)
    mixed_grad = jnp.dot(whole_branch, out_weight, preferred_element_type=jnp.float32).astype(
        jnp.bfloat16
    )
    out_w_grad = jnp.einsum(
        "td,th->dh", whole_branch, mixed_rows, preferred_element_type=jnp.float32
    )
    grad_low = (mixed_grad * 0.125).reshape(block_count, block_len, head_count, head_width)
    grad_float = grad_low.astype(jnp.float32)
    prob_grad = jnp.einsum(
        "bthd,bshd->bhts", grad_low, value_blocks, preferred_element_type=jnp.float32
    )
    score_grad = (prob_grad * decay_mat).astype(jnp.bfloat16)
    value_grad = jnp.einsum(
        "bhts,bthd->bshd", weights_low, grad_low, preferred_element_type=jnp.float32
    )
    query_grad = jnp.einsum(
        "bhts,bshd->bthd", score_grad, key_blocks, preferred_element_type=jnp.float32
    )
    key_scaled_grad = jnp.einsum(
        "bhts,bthd->bshd", score_grad, query_blocks, preferred_element_type=jnp.float32
    )
    query_grad = query_grad + first_rows * jnp.einsum(
        "bthe,bhde->bthd", grad_float, block_init, precision=HIGHEST
    )
    init_grad = jnp.einsum(
        "bthd,bthe->bhde", query_float * first_rows, grad_float, precision=HIGHEST
    )
    local_sum = jnp.sum(pass_stack * init_grad, axis=0)
    later_gate, later_grad = entering((through, local_sum), chain, identity, True)
    running = later_grad
    state_grad_list = [running] * block_count
    for block_index in reversed(range(block_count)):
        state_grad_list[block_index] = running
        running = block_gate[block_index][:, None, None] * running + init_grad[block_index]
    state_grad = jnp.stack(state_grad_list)
    key_scaled_grad = key_scaled_grad + last_rows * jnp.einsum(
        "bhde,bshe->bshd", state_grad, value_float, precision=HIGHEST
    )
    value_grad = value_grad + jnp.einsum(
        "bhde,bshd->bshe", state_grad, weighted_key, precision=HIGHEST
    )
    query_grad_low = query_grad.reshape(tok_rows, half_width).astype(jnp.bfloat16)
    value_grad_low = value_grad.reshape(tok_rows, half_width).astype(jnp.bfloat16)
    shifted_grad = (
        key_scaled_grad.reshape(tok_rows, head_count, head_width) * gain_in.T[:, :, None]
    ).reshape(tok_rows, half_width)
    grad_wide = jnp.pad(shifted_grad, ((edge_rows, edge_rows), (0, 0)))
    distance_wide = jnp.pad(distance, (edge_rows, edge_rows), constant_values=-1)
    span_rows = tok_rows + edge_rows
    padded_grad = jnp.zeros((span_rows, half_width), jnp.float32)
    for tap_index in range(tap_count):
        tap_mask = (distance_wide[tap_index : tap_index + span_rows] >= tap_index)[:, None]
        padded_grad = padded_grad + kernel[tap_index][None, :] * jnp.where(
            tap_mask, grad_wide[tap_index : tap_index + span_rows], 0.0
        )
    kernel_rows = []
    for tap_index in range(tap_count):
        keep_mask = (distance >= tap_index)[:, None]
        kernel_rows.append(
            jnp.sum(
                jnp.where(
                    keep_mask,
                    shifted_grad
                    * padded[edge_rows - tap_index : edge_rows - tap_index + tok_rows].astype(
                        jnp.float32
                    ),
                    0.0,
                ),
                axis=0,
            )
        )
    kernel_grad = jnp.stack(kernel_rows)
    back_edge = passed_along(as_sent(padded_grad[:edge_rows]), "seq", -1)
    key_grad = padded_grad[edge_rows:].at[tok_rows - edge_rows :].add(back_edge * tail_mask)
    key_grad_low = key_grad.astype(jnp.bfloat16)
    q_grad = jnp.einsum("td,th->dh", normed_one, query_grad_low, preferred_element_type=jnp.float32)
    k_grad = jnp.einsum("td,th->dh", normed_one, key_grad_low, preferred_element_type=jnp.float32)
    v_grad = jnp.einsum("td,th->dh", normed_one, value_grad_low, preferred_element_type=jnp.float32)
    norm1_part = jnp.einsum(
        "th,dh->td", query_grad_low, q_weight, preferred_element_type=jnp.float32
    )
    norm1_part = norm1_part + jnp.einsum(
        "th,dh->td", key_grad_low, k_weight, preferred_element_type=jnp.float32
    )
    norm1_part = norm1_part + jnp.einsum(
        "th,dh->td", value_grad_low, v_weight, preferred_element_type=jnp.float32
    )
    norm1_full = pair_sum(norm1_part)
    norm1_half = lax.dynamic_slice_in_dim(norm1_full, row_start, row_count, axis=0)
    unit_one_half = lax.dynamic_slice_in_dim(unit_one, row_start, row_count, axis=0)
    gain1_grad = jnp.sum(norm1_half * unit_one_half, axis=0)
    bias1_grad = jnp.sum(norm1_half, axis=0)
    input_back = norm_backward(norm1_full, unit_one, inverse_one, norm1_gain)
    input_grad = (
        resid_grad + lax.dynamic_slice_in_dim(input_back, own_start, half_width, axis=1)
    ).astype(jnp.bfloat16)
    gains = jnp.stack([gain1_grad, bias1_grad, gain2_grad, bias2_grad])
    gains = gains + swapped(gains)
    kernel_total, gains = summed([kernel_grad, gains])
    mixer_total = (
        scattered_sum(q_grad),
        scattered_sum(k_grad),
        scattered_sum(v_grad),
        scattered_sum(out_w_grad),
    )
    return (
        block_output,
        input_grad,
        gains[0],
        gains[1],
        mixer_total[0],
        mixer_total[1],
        mixer_total[2],
        kernel_total,
        mixer_total[3],
        gains[2],
        gains[3],
        ffn_total[0],
        ffn_total[1],
    )


def solution(mesh):
    in_specs = (
        P("seq", "head"),
        P("seq"),
        P("head", "seq"),
        P(),
        P(),
        P(None, "head"),
        P(None, "head"),
        P(None, "head"),
        P(None, "head"),
        P(None, "head"),
        P(),
        P(),
        P(None, "head"),
        P(None, "head"),
        P("seq", "head"),
    )
    out_specs = (
        P("seq", "head"),
        P("seq", "head"),
        P(),
        P(),
        P("seq", "head"),
        P("seq", "head"),
        P("seq", "head"),
        P(None, "head"),
        P("seq", "head"),
        P(),
        P(),
        P("seq", "head"),
        P("seq", "head"),
    )
    return jax.shard_map(local, mesh=mesh, in_specs=in_specs, out_specs=out_specs, check_vma=False)
```

```python
import functools

import jax
import jax.numpy as jnp
from jax import lax
from jax.experimental import pallas as pl
from jax.experimental.pallas import tpu as pltpu
from jax.sharding import PartitionSpec as P

NORM_EPS = 1e-05
RATE_CAP = 0.05
LANES = 128
STEP = 64
FAR = float(1 << 20)
GELU_SCALE = 0.7978845608028654
GELU_CUBE = 0.044715
F32 = jnp.float32
BF16 = jnp.bfloat16

NN = (((1,), (0,)), ((), ()))
NT = (((1,), (1,)), ((), ()))
TN = (((0,), (0,)), ((), ()))


def mm(a, b, dims=NN):
    return lax.dot_general(a, b, dims, preferred_element_type=F32)


def shape(dims, kind):
    return pltpu.HBM(dims, kind)


def shape(dims, kind):
    return jax.ShapeDtypeStruct(dims, kind)


FEW = pl.BlockSpec(memory_space=pltpu.SMEM)


def whole(array):
    dims = array.shape
    return pl.BlockSpec(dims, lambda *_: (0,) * len(dims), pipeline_mode=pl.Buffered(1))


def run(body, outs, *ins, scratch=(), scalars=0, grid=(1,), in_specs=None, out_specs=None, mib=16,
        us=1.0, far=()):
    many = isinstance(outs, (tuple, list))
    held = [pltpu.with_memory_space_constraint(x, pltpu.HBM) if i in far else x for i, x in enumerate(ins)]
    if in_specs is None:
        in_specs = [None] * (len(ins) - scalars)
    if out_specs is None:
        out_specs = (None,) * len(outs) if many else None
    in_specs = [spec or whole(x) for spec, x in zip(in_specs, ins[scalars:])]
    pick = lambda spec, x: spec or whole(x)
    out_specs = tuple(map(pick, out_specs, outs)) if many else pick(out_specs, outs)
    return pl.pallas_call(
        body, out_shape=outs, grid=grid, in_specs=[FEW] * scalars + list(in_specs), out_specs=out_specs,
        scratch_shapes=list(scratch), compiler_params=pltpu.CompilerParams(vmem_limit_bytes=mib << 20),
        cost_estimate=pl.CostEstimate(flops=int(us * 1e9), transcendentals=0, bytes_accessed=int(us * 3e6)))(*held)


def after(value, *first):
    return lax.optimization_barrier((value,) + first)[0]


def lanes(width):
    return range(0, width, LANES)


def half_of(ref, h, width):
    return ref.at[:, pl.ds(pl.multiple_of(h * width, LANES), width)]


def digits_of(count):
    digits, stride = [], 1
    while count > 1:
        radix = 4 if count % 4 == 0 else (2 if count % 2 == 0 else count)
        digits.append((stride, radix))
        stride, count = stride * radix, count // radix
    return digits


def turned(array, stride, radix, by):
    pairs = []
    for i in range(lax.axis_size("seq")):
        member = i // stride % radix
        pairs.append((i, i + ((member + by) % radix - member) * stride))
    return lax.ppermute(array, "seq", pairs)


def crossed(array, stride, radix, mask):
    pairs = []
    for i in range(lax.axis_size("seq")):
        member = i // stride % radix
        pairs.append((i, i + ((member ^ mask) - member) * stride))
    return lax.ppermute(array, "seq", pairs)


def swapped(array):
    count = lax.axis_size("head")
    return lax.ppermute(array, "head", [(i, (i + 1) % count) for i in range(count)])


def passed_along(array, by):
    count = lax.axis_size("seq")
    return lax.ppermute(array, "seq", [(i, i + by) for i in range(count) if 0 <= i + by < count])


def member_at(place_ref, stride, radix):
    return lax.rem(lax.div(place_ref[0], stride), radix)


def send_pieces(pieces, stride, radix):
    return [pieces[0]] + [turned(pieces[by], stride, radix, by) for by in range(1, radix)]


def bits_of(count):
    return [1 << k for k in range(count.bit_length() - 1)]


def mirrored(array, stride):
    pairs = [(i, i ^ stride) for i in range(lax.axis_size("seq"))]
    return lax.ppermute(array, "seq", pairs)


def halve(total, bit, keep, send, low):
    for g in range(keep.shape[0]):
        at = g // low * 2 * low + g % low
        keep[g] = total[at + bit * low].astype(BF16)
        send[g] = total[at + (1 - bit) * low].astype(BF16)


def split_shapes(count, rows, widths):
    return tuple(shape((count // 2, rows, w), BF16) for w in widths for _ in range(2))


def half_width(width):
    return -(-width // (2 * LANES)) * LANES


def put_rows(total, at, grad):
    rows = total.shape[1]
    for s in range(total.shape[0]):
        total[s, :, at : at + grad.shape[1]] = grad[s * rows : (s + 1) * rows]


def both_halves(total, place_ref, outs):
    middle = outs[0].shape[2]
    halve(total.at[:, :, :middle], member_at(place_ref, 1, 2), outs[0], outs[1], 1)
    halve(total.at[:, :, middle:], member_at(place_ref, 2, 2), outs[2], outs[3], 2)


def grads_kernel(spans, place_ref, *refs):
    lefts, rights, outs, total = refs[: len(spans)], refs[len(spans) : 2 * len(spans)], refs[-5:-1], refs[-1]
    for left, right, at in zip(lefts, rights, spans):
        put_rows(total, at, mm(left[...], right[...], TN))
    both_halves(total, place_ref, outs)


def grad_halves(place, pairs, us):
    count = lax.axis_size("seq")
    depth = pairs[0][0].shape[1]
    spans, width = [], 0
    for _, right in pairs:
        spans.append(width)
        width += right.shape[1]
    middle = half_width(width)
    rows = depth // count
    return run(
        functools.partial(grads_kernel, spans), split_shapes(count, rows, (middle, width - middle)),
        place, *[left for left, _ in pairs], *[right for _, right in pairs],
        scalars=1, scratch=[pltpu.VMEM((count, rows, width), F32)], mib=24, us=us)


def fold_rest(place, halves, got, at, widths):
    bits = bits_of(lax.axis_size("seq"))
    while True:
        halves = fold_bit(place, halves, got, at, widths)
        at += 1
        if at >= len(bits):
            return halves
        got = mirrored(halves[1], bits[at])


def down_kernel(place_ref, grad_ref, hidden_ref, down_ref, resid_ref, *refs):
    outs, own_ref, send_ref, total, part = refs[:4], refs[4], refs[5], refs[6], refs[7]
    part[...] = mm(hidden_ref[...], down_ref[...], NT)
    width = own_ref.shape[1]
    h = place_ref[1]
    own_ref[...] = half_of(part, h, width)[...] + half_of(resid_ref, h, width)[...]
    send_ref[...] = half_of(part, 1 - h, width)[...].astype(BF16)
    put_rows(total, 0, mm(grad_ref[...], hidden_ref[...], TN))
    both_halves(total, place_ref, outs)


def cross_kernel(place_ref, keep_a, got_a, keep_b, got_b, *refs):
    outs, sum_a, sum_b = refs[:4], refs[4], refs[5]
    for keep, got, total in ((keep_a, got_a, sum_a), (keep_b, got_b, sum_b)):
        for g in range(total.shape[0]):
            total[g] = keep[g].astype(F32) + got[g].astype(F32)
    halve(sum_a, member_at(place_ref, 2, 2), outs[0], outs[1], 1)
    halve(sum_b, member_at(place_ref, 1, 2), outs[2], outs[3], 1)


def cross(place, halves, got_a, got_b):
    keep_a, _, keep_b, _ = halves
    count, rows, _ = keep_a.shape
    return run(
        cross_kernel, split_shapes(count, rows, (keep_a.shape[2], keep_b.shape[2])),
        place, keep_a, got_a, keep_b, got_b, scalars=1,
        scratch=[pltpu.VMEM(keep_a.shape, F32), pltpu.VMEM(keep_b.shape, F32)], us=8)


def join_kernel(stride, place_ref, keep_a, got_a, keep_b, got_b, *refs):
    outs, total = refs[:-1], refs[-1]
    middle = keep_a.shape[2]
    for g in range(total.shape[0]):
        total[g, :, :middle] = keep_a[g].astype(F32) + got_a[g].astype(F32)
        total[g, :, middle:] = keep_b[g].astype(F32) + got_b[g].astype(F32)
    put_folded(stride, total, place_ref, outs)


def fold_kernel(stride, place_ref, keep, got, *refs):
    outs, total = refs[:-1], refs[-1]
    for g in range(total.shape[0]):
        total[g] = keep[g].astype(F32) + got[g].astype(F32)
    put_folded(stride, total, place_ref, outs)


def put_folded(stride, total, place_ref, outs):
    if stride:
        halve(total, member_at(place_ref, stride, 2), outs[0], outs[1], 1)
        return
    begin = 0
    for out in outs:
        out[...] = total[0, :, begin : begin + out.shape[1]]
        begin += out.shape[1]


def fold_outs(entries, rows, widths):
    if entries == 1:
        return tuple(shape((rows, w), F32) for w in widths)
    return split_shapes(entries, rows, (sum(widths),))


def join(place, halves, got_a, got_b, widths):
    keep_a, _, keep_b, _ = halves
    entries, rows, _ = keep_a.shape
    bits = bits_of(lax.axis_size("seq"))
    last = entries == 1
    return run(
        functools.partial(join_kernel, 0 if last else bits[2]), fold_outs(entries, rows, widths), place,
        keep_a, got_a, keep_b, got_b, scalars=1, scratch=[pltpu.VMEM((entries, rows, sum(widths)), F32)], us=8)


def fold_bit(place, halves, got, at, widths):
    keep = halves[0]
    entries, rows, _ = keep.shape
    bits = bits_of(lax.axis_size("seq"))
    last = entries == 1
    return run(
        functools.partial(fold_kernel, 0 if last else bits[at + 1]), fold_outs(entries, rows, widths), place,
        keep, got, scalars=1, scratch=[pltpu.VMEM((entries, rows, sum(widths)), F32)], us=8)


def add_kernel(stage, later, rows, place_ref, *refs):
    radix = stage[1]
    got, outs, total, sorted_parts = refs[:radix], refs[radix:-2], refs[-2], refs[-1]
    entries = total.shape[0]
    for g in range(entries):
        at = slice(g * rows, (g + 1) * rows)
        acc = got[0][at].astype(F32)
        for by in range(1, radix):
            acc = acc + got[by][at].astype(F32)
        total[g] = acc
    tail = [m.at[entries * rows :] for m in got]
    shared = in_order(member_at(place_ref, *stage), tail, sorted_parts)
    if later:
        put_messages(total, shared, later[1], member_at(place_ref, *later), outs)
    else:
        outs[0][...] = total[0]
        outs[1][...] = shared[:STEP]
        put_vectors(shared[STEP:], outs[2:4])
        put_vectors(shared[STEP + 8 :], outs[4:])


def put_messages(total, shared, radix, member, outs):
    rows = total.shape[1]
    for by in range(radix):
        to = lax.rem(member + by, radix)
        groups = total.shape[0] // radix
        for g in range(groups):
            outs[by][g * rows : (g + 1) * rows] = total[g * radix + to].astype(BF16)
        outs[by][groups * rows :] = shared.astype(BF16)


def add_messages(place, got, at, rows):
    stages = digits_of(lax.axis_size("seq"))
    radix = stages[at][1]
    depth, width = got[0].shape
    extra = STEP + 16
    entries = (depth - extra) // rows
    later = ()
    if at + 1 < len(stages):
        later = stages[at + 1]
        outs = (shape((entries // later[1] * rows + extra, width), BF16),) * later[1]
    else:
        outs = (shape((rows, width), F32), shape((STEP, width), F32)) + (shape((2 * width,), F32),) * 4
    return run(
        functools.partial(add_kernel, stages[at], later, rows), outs, place, *got, scalars=1,
        scratch=[pltpu.VMEM((entries, rows, width), F32), pltpu.VMEM((radix, extra, width), F32)], us=8)


def in_order(member, got, sorted_parts):
    radix = len(got)
    for by in range(radix):
        sorted_parts[lax.rem(member + radix - by, radix)] = got[by][...].astype(F32)
    acc = sorted_parts[0]
    for c in range(1, radix):
        acc = acc + sorted_parts[c]
    return acc


def put_vectors(rows_in, outs):
    width = rows_in.shape[1]
    for k, out in enumerate(outs):
        out[:width] = rows_in[k]
        out[width:] = rows_in[k + 2]


def flat_rows(sums, width):
    return jnp.concatenate([sums[:, :width], sums[:, width:]], axis=0)


def chained(first, second):
    return first[0] * second[0], second[0] * first[1] + second[1]


def link(stage, reverse, place_ref, messages, before, want_total):
    radix = stage[1]
    member = member_at(place_ref, *stage)
    if reverse:
        member = radix - 1 - member
    rows = messages[0].shape[0] - 16
    pairs = []
    for m in messages:
        whole = m[...].astype(F32)
        pairs.append((whole[rows : rows + 1], whole[:rows]))
    none = (jnp.ones_like(pairs[0][0]), jnp.zeros_like(pairs[0][1]))

    def side(use):
        acc = none
        for by in range(radix - 1, 0, -1):
            kept = use(by)
            part = (jnp.where(kept, pairs[by][0], none[0]), jnp.where(kept, pairs[by][1], none[1]))
            acc = chained(acc, part)
        return acc

    lower = side(lambda by: by <= member)
    before = chained(lower, tuple(b[...] for b in before)) if before else lower
    if not want_total:
        return before, None
    return before, chained(chained(lower, pairs[0]), side(lambda by: by > member))


def link_kernel(stage, reverse, place_ref, *refs):
    messages, held, outs = refs[: stage[1]], refs[stage[1] : -3], refs[-3:]
    before, total = link(stage, reverse, place_ref, messages, held, True)
    outs[0][...], outs[1][...] = before
    rows = outs[1].shape[0]
    outs[2][:rows] = total[1].astype(BF16)
    outs[2][rows:] = jnp.broadcast_to(total[0], (outs[2].shape[0] - rows, total[0].shape[1])).astype(BF16)


def scan_send(message, at, reverse):
    stride, radix = digits_of(lax.axis_size("seq"))[at]
    return [message] + [
        turned(message, stride, radix, (radix - by) if reverse else by) for by in range(1, radix)
    ]


def scan_link(place, got, before, at, reverse):
    stage = digits_of(lax.axis_size("seq"))[at]
    rows, width = got[0].shape
    outs = run(functools.partial(link_kernel, stage, reverse),
               (shape((1, width), F32), shape((rows - 16, width), F32), shape((rows, width), BF16)),
               place, *got, *before, scalars=1, us=8)
    return outs[:2], outs[2]


def split_parts(x, count):
    parts = []
    for _ in range(count):
        low = x.astype(BF16)
        parts.append(low)
        x = x - low.astype(F32)
    return parts


def side_kernel(starts_ref, decay_ref, beta_ref, lamr_ref, lamc_ref, docr_ref, docc_ref, dist_ref,
                beta_out, first_out, last_out, gate_out, tri, same, wide):
    tok = starts_ref.shape[0]
    heads = decay_ref.shape[0]
    head_pairs = lamc_ref.shape[0] // tok
    width = beta_out.shape[1]
    row = lax.broadcasted_iota(jnp.int32, (tok, tok), 0)
    col = lax.broadcasted_iota(jnp.int32, (tok, tok), 1)
    tri[...] = (col <= row).astype(F32).astype(BF16)
    begins = jnp.broadcast_to(row_of(starts_ref).astype(F32), (LANES, tok)).astype(BF16)
    doc_col = mm(tri[...], begins, NT)
    doc_row = mm(begins[:16], tri[...], NT)[:8]
    docr_ref[...] = doc_row
    docc_ref[...] = doc_col
    wide[...] = jnp.zeros_like(wide)
    wide[:heads] = decay_ref[...]
    lam_col = jnp.zeros((tok, LANES), F32)
    lam_row = jnp.zeros((16, tok), F32)
    for part in split_parts(wide[...], 3):
        lam_col = lam_col + mm(tri[...], part, NT)
        lam_row = lam_row + mm(part[:16], tri[...], NT)
    lamr_ref[...] = jnp.zeros_like(lamr_ref)
    for p in range(head_pairs):
        lamr_ref[8 * p : 8 * p + 2] = lam_row[2 * p : 2 * p + 2]
        lamc_ref[p * tok : (p + 1) * tok] = lam_col if p == 0 else pltpu.roll(lam_col, LANES - 2 * p, 1)
    ones = jnp.ones((tok, LANES), BF16)
    alike = doc_col[:, :1] == doc_row[:1]
    same[...] = jnp.where(alike & (col <= row), 1.0, 0.0).astype(BF16)
    behind = mm(same[...], ones)
    dist_ref[...] = jnp.where(doc_col == 0.0, FAR, behind - 1.0)
    lam_end = lam_col[tok - 1 :]
    doc_end = doc_col[tok - 1 :]
    first = jnp.where(doc_col == 0.0, jnp.exp(-lam_col), 0.0)
    last = jnp.where(doc_col == doc_end, jnp.exp(lam_col - lam_end), 0.0)
    spread = (lax.broadcasted_iota(jnp.int32, (LANES, width), 0)
              == lax.broadcasted_iota(jnp.int32, (LANES, width), 1) // (width // heads))
    spread = spread.astype(F32).astype(BF16)
    for ref, value in ((first_out, first), (last_out, last)):
        parts = split_parts(value, 2)
        ref[...] = mm(parts[0], spread) + mm(parts[1], spread)
    wide[:heads] = beta_ref[...]
    eye = (row == col).astype(F32).astype(BF16)
    beta_col = jnp.zeros((tok, LANES), F32)
    for part in split_parts(wide[...], 2):
        beta_col = beta_col + mm(eye, part, NT)
    parts = split_parts(beta_col, 2)
    beta_out[...] = mm(parts[0], spread) + mm(parts[1], spread)
    gate_out[...] = first_out[tok - 16 :].astype(BF16)


def row_of(ref):
    return ref[...].reshape(1, ref.shape[0])


def norm_rows(rows_in):
    count = rows_in.shape[1]
    center = rows_in - jnp.sum(rows_in, axis=1, keepdims=True) * (1.0 / count)
    spread = jnp.sum(center * center, axis=1, keepdims=True) * (1.0 / count)
    inverse = lax.rsqrt(spread + NORM_EPS)
    return center * inverse, inverse


def norm_back(grad_rows, unit_rows, inverse, gain_vec):
    scale = 1.0 / grad_rows.shape[1]
    scaled = grad_rows * gain_vec
    return inverse * (scaled - jnp.sum(scaled, axis=1, keepdims=True) * scale
                      - unit_rows * (jnp.sum(scaled * unit_rows, axis=1, keepdims=True) * scale))


def by_rows(tok, body, size=64):
    def step(i, carry):
        body(pl.ds(pl.multiple_of(i * size, size), size))
        return carry

    lax.fori_loop(0, tok // size, step, 0)


def in_kernel(place_ref, own_ref, other_ref, gain_ref, bias_ref, wq_ref, wk_ref, wv_ref, docc_ref,
              normed_ref, q_ref, k_ref, v_ref, tail_ref, rows):
    h = place_ref[1]
    tok, width = own_ref.shape
    half_of(rows, h, width)[...] = own_ref[...]
    half_of(rows, 1 - h, width)[...] = other_ref[...]

    def norm(at):
        unit, _ = norm_rows(rows[at].astype(F32))
        normed_ref[at] = (unit * row_of(gain_ref) + row_of(bias_ref)).astype(BF16)

    by_rows(tok, norm)
    normed = normed_ref[...]
    k_ref[...] = mm(normed, wk_ref[...]).astype(BF16)
    keep = docc_ref[tok - STEP :] == docc_ref[tok - 1 :]
    for l in lanes(width):
        tail_ref[:, l : l + LANES] = jnp.where(
            keep, k_ref[tok - STEP :, l : l + LANES].astype(F32), 0.0).astype(BF16)
    q_ref[...] = mm(normed, wq_ref[...]).astype(BF16)
    v_ref[...] = mm(normed, wv_ref[...]).astype(BF16)


def filter_chunk(keys, taps, dist, count, t0):
    def group(a, acc):
        acc = list(acc)
        for b in range(8):
            j = a * 8 + b
            keep = dist >= j.astype(F32)
            for l in range(count):
                x = keys[l, pl.ds(STEP + t0 - a * 8 - b, STEP), :]
                acc[l] = acc[l] + jnp.where(keep, x * taps[l, pl.ds(j, 1), :], 0.0)
        return tuple(acc)

    return lax.fori_loop(0, 8, group, tuple(jnp.zeros((STEP, LANES), F32) for _ in range(count)))


def filter_kernel(k_ref, taps_ref, dist_ref, beta_ref, out_ref, keys, taps):
    tok, width = k_ref.shape
    count = width // LANES
    for l in range(count):
        keys[l, STEP:] = k_ref[:, l * LANES : (l + 1) * LANES].astype(F32)
        taps[l] = taps_ref[:, l * LANES : (l + 1) * LANES].astype(F32)
    out_ref[:STEP] = jnp.zeros((STEP, width), BF16)

    def chunk(c, carry):
        t0 = pl.multiple_of(c * STEP, STEP)
        at = pl.ds(t0, STEP)
        acc = filter_chunk(keys, taps, dist_ref[at], count, t0)
        for l in range(count):
            span = slice(l * LANES, (l + 1) * LANES)
            out_ref[at, span] = (acc[l] * beta_ref[at, span]).astype(BF16)
        return carry

    lax.fori_loop(1, tok // STEP, chunk, 0)


def fold(square, low):
    return jnp.where(low, square[:STEP], square[STEP:])


def unfold(flat, low):
    return jnp.concatenate([jnp.where(low, flat, 0.0), jnp.where(low, 0.0, flat)], axis=0)


def low_lanes(rows):
    return lax.broadcasted_iota(jnp.int32, (rows, LANES), 1) < STEP


def state_kernel(part_ref, tail_ref, k_ref, taps_ref, dist_ref, beta_ref, last_ref, v_ref, gate_ref,
                 sk_ref, message_ref, keys, taps):
    tok, width = part_ref.shape
    count = width // LANES
    for l in range(count):
        span = slice(l * LANES, (l + 1) * LANES)
        keys[l, :STEP] = tail_ref[:, span].astype(F32)
        keys[l, STEP:] = k_ref[:STEP, span].astype(F32)
        taps[l] = taps_ref[:, span].astype(F32)
    sk_ref[...] = part_ref[...]
    acc = filter_chunk(keys, taps, dist_ref[:STEP], count, 0)
    low = low_lanes(STEP)
    for l in range(count):
        span = slice(l * LANES, (l + 1) * LANES)
        sk_ref[:STEP, span] = (acc[l] * beta_ref[:STEP, span]).astype(BF16)
        weighted = (sk_ref[:, span].astype(F32) * last_ref[:, span]).astype(BF16)
        message_ref[:STEP, span] = fold(mm(weighted, v_ref[:, span], TN), low).astype(BF16)
    message_ref[STEP:] = gate_ref[...]


def kept_pairs(docc_ref, docr_ref):
    tok = docc_ref.shape[0]
    order = lax.broadcasted_iota(jnp.int32, (tok, tok), 0) >= lax.broadcasted_iota(jnp.int32, (tok, tok), 1)
    return (docc_ref[:, :1] == docr_ref[:1]) & order


def own_lanes(x, low, e):
    return jnp.where(low if e == 0 else ~low, x.astype(F32), 0.0).astype(BF16)


def decay_of(lamr_ref, lamc_ref, keep, e):
    span = jnp.minimum(lamr_ref[e : e + 1] - lamc_ref[:, e : e + 1], 0.0)
    return jnp.where(keep, jnp.exp(span), 0.0)


def inside_kernel(q_ref, k_ref, v_ref, lamr_ref, lamc_ref, docr_ref, docc_ref, out_ref):
    low = low_lanes(q_ref.shape[0])
    keep = kept_pairs(docc_ref, docr_ref)
    outs = []
    for e in range(2):
        score = mm(own_lanes(q_ref[...], low, e), k_ref[...], NT)
        outs.append(mm((score * decay_of(lamr_ref, lamc_ref, keep, e)).astype(BF16), v_ref[...]))
    out_ref[...] = jnp.where(low, outs[0], outs[1])


def mixed_kernel(stage, place_ref, inside_ref, q_ref, first_ref, *refs):
    (state_ref, mixed_ref) = refs[-2:]
    before, _ = link(stage, False, place_ref, refs[: stage[1]], refs[stage[1] : -2], False)
    state_ref[...] = before[1]
    low = low_lanes(STEP)
    for l in lanes(q_ref.shape[1]):
        span = slice(l, l + LANES)
        square = unfold(state_ref[:, span], low).astype(BF16)
        mixed_ref[:, span] = (0.125 * (inside_ref[:, span] + first_ref[:, span] * mm(q_ref[:, span], square))
                              ).astype(BF16)


def hidden_grad_kernel(place_ref, own_ref, other_ref, down_ref, out_ref, full_ref):
    @pl.when(pl.program_id(0) == 0)
    def _():
        width = own_ref.shape[1]
        half_of(full_ref, place_ref[1], width)[...] = own_ref[...]
        half_of(full_ref, 1 - place_ref[1], width)[...] = other_ref[...]

    out_ref[...] = mm(full_ref[...], down_ref[...]).astype(BF16)


def ffn_kernel(place_ref, own_ref, other_ref, mix_own_ref, mix_other_ref, out_own_ref, out_other_ref, gain_ref,
               bias_ref, up_ref, hg_ref, resid_ref, normed_ref, hidden_ref, pre_ref, part_ref, rows, acc):
    h = place_ref[1]
    step = pl.program_id(0)
    tok, width = own_ref.shape

    @pl.when(step == 0)
    def _():
        half_of(rows, h, width)[...] = own_ref[...]
        half_of(rows, 1 - h, width)[...] = other_ref[...]
        resid_ref[...] = mm(mix_own_ref[...], out_own_ref[...], NT) + mm(mix_other_ref[...], out_other_ref[...], NT)

        def norm(at):
            resid = rows[at].astype(F32) + resid_ref[at]
            resid_ref[at] = resid
            unit, _ = norm_rows(resid)
            normed_ref[at] = (unit * row_of(gain_ref) + row_of(bias_ref)).astype(BF16)

        by_rows(tok, norm)
        acc[...] = jnp.zeros_like(acc)

    pre = mm(normed_ref[...], up_ref[...])
    square = pre * pre
    bent = jnp.tanh(GELU_SCALE * (pre + GELU_CUBE * (square * pre)))
    outer = 0.5 * (1.0 + bent)
    hidden_ref[...] = (pre * outer).astype(BF16)
    slope = outer + 0.5 * pre * (1.0 - bent * bent) * (GELU_SCALE * (1.0 + 3.0 * GELU_CUBE * square))
    pre_ref[...] = (hg_ref[...].astype(F32) * slope).astype(BF16)
    acc[...] += mm(pre_ref[...], up_ref[...], NT)

    @pl.when(step == pl.num_programs(0) - 1)
    def _():
        part_ref[...] = acc[...].astype(BF16)


def norm2_kernel(place_ref, part_ref, got_ref, resid_ref, grad_ref, gain_ref, out_w_ref, q_ref, first_ref,
                 gate_ref, resid_grad_ref, branch_ref, g_ref, sums_ref, message_ref, rows):
    h = place_ref[1]
    tok, width = q_ref.shape
    sums_ref[...] = jnp.zeros_like(sums_ref)

    def norm(at):
        back = part_ref[at].astype(F32) + got_ref[at].astype(F32)
        unit, inverse = norm_rows(resid_ref[at])
        grad = grad_ref[at].astype(F32) + norm_back(back, unit, inverse, row_of(gain_ref))
        rows[at] = grad
        branch_ref[at] = grad.astype(BF16)
        sums_ref[0:1] += jnp.sum(back * unit, axis=0, keepdims=True)
        sums_ref[1:2] += jnp.sum(back, axis=0, keepdims=True)

    by_rows(tok, norm)
    resid_grad_ref[...] = half_of(rows, h, width)[...]
    g_ref[...] = (0.125 * mm(branch_ref[...], out_w_ref[...]).astype(BF16).astype(F32)).astype(BF16)
    low = low_lanes(STEP)
    for l in lanes(width):
        span = slice(l, l + LANES)
        weighted = (q_ref[:, span].astype(F32) * first_ref[:, span]).astype(BF16)
        message_ref[:STEP, span] = fold(mm(weighted, g_ref[:, span], TN), low).astype(BF16)
    message_ref[STEP:] = gate_ref[...]


def back_kernel(q_ref, k_ref, v_ref, g_ref, lamr_ref, lamc_ref, docr_ref, docc_ref, first_ref, state_ref,
                dq_ref, dk_ref, dv_ref):
    low = low_lanes(q_ref.shape[0])
    keep = kept_pairs(docc_ref, docr_ref)
    square = unfold(state_ref[...], low_lanes(STEP)).astype(BF16)
    outs = []
    for e in range(2):
        decay = decay_of(lamr_ref, lamc_ref, keep, e)
        prob = (mm(own_lanes(q_ref[...], low, e), k_ref[...], NT) * decay).astype(BF16)
        score = (mm(own_lanes(g_ref[...], low, e), v_ref[...], NT) * decay).astype(BF16)
        outs.append((mm(score, k_ref[...]), mm(score, q_ref[...], TN), mm(prob, g_ref[...], TN)))
    from_state = first_ref[...] * mm(g_ref[...], square, NT)
    dq_ref[...] = (jnp.where(low, outs[0][0], outs[1][0]) + from_state).astype(BF16)
    dk_ref[...] = jnp.where(low, outs[0][1], outs[1][1])
    dv_ref[...] = jnp.where(low, outs[0][2], outs[1][2])


def filter_back_chunk(sg, keys, taps, ahead, sums, count, s0):
    held = [keys[l, pl.ds(s0, STEP), :] for l in range(count)]

    def group(a, acc):
        acc = list(acc)
        for b in range(8):
            j = a * 8 + b
            keep = ahead > j.astype(F32)
            for l in range(count):
                u = jnp.where(keep, sg[l, pl.ds(s0 + a * 8 + b, STEP), :], 0.0)
                acc[l] = acc[l] + u * taps[l, pl.ds(j, 1), :]
                sums[l, j] += jnp.sum((held[l] * u).reshape(STEP // 8, 8, LANES), axis=0)
        return tuple(acc)

    return lax.fori_loop(0, 8, group, tuple(jnp.zeros((STEP, LANES), F32) for _ in range(count)))


def reach(docr_ref, docc_ref, ahead_ref):
    tok = docc_ref.shape[0]
    order = lax.broadcasted_iota(jnp.int32, (tok, tok), 0) <= lax.broadcasted_iota(jnp.int32, (tok, tok), 1)
    same = jnp.where((docc_ref[:, :1] == docr_ref[:1]) & order, 1.0, 0.0).astype(BF16)
    ahead_ref[STEP:] = mm(same, jnp.ones((tok, LANES), BF16))
    unbroken = jnp.sum(jnp.where(docr_ref[:1] == 0.0, 1.0, 0.0), axis=1, keepdims=True)
    ahead_ref[:STEP] = unbroken + STEP - lax.broadcasted_iota(jnp.int32, (STEP, LANES), 0).astype(F32)


def carry_kernel(stage, place_ref, dk_ref, dv_ref, k_ref, v_ref, last_ref, beta_ref, docr_ref, docc_ref, taps_ref,
                 tail_ref, ffn_own_ref, ffn_other_ref, *refs):
    value_ref, sg_ref, edge_ref, sums, ahead_ref, block_ref, taps, keys = refs[-8:]
    block_ref[...] = (ffn_own_ref[...] + ffn_other_ref[...].astype(F32)).astype(BF16)
    reach(docr_ref, docc_ref, ahead_ref)
    before, _ = link(stage, True, place_ref, refs[: stage[1]], refs[stage[1] : -8], False)
    state = before[1]
    tok, width = dk_ref.shape
    count = width // LANES
    low = low_lanes(STEP)
    for l in range(count):
        span = slice(l * LANES, (l + 1) * LANES)
        square = unfold(state[:, span], low).astype(BF16)
        last = last_ref[:, span]
        value_ref[:, span] = (dv_ref[:, span] + last * mm(k_ref[:, span], square)).astype(BF16)
        sg_ref[l, :STEP] = jnp.zeros((STEP, LANES), F32)
        sg_ref[l, STEP : STEP + tok] = beta_ref[:, span] * (
            dk_ref[:, span] + last * mm(v_ref[:, span], square, NT))
        sg_ref[l, STEP + tok :] = jnp.zeros((STEP, LANES), F32)
        keys[l] = tail_ref[:, span].astype(F32)
        taps[l] = taps_ref[:, span].astype(F32)
    sums[...] = jnp.zeros_like(sums)
    acc = filter_back_chunk(sg_ref, keys, taps, ahead_ref[:STEP], sums, count, 0)
    for l in range(count):
        edge_ref[:, l * LANES : (l + 1) * LANES] = acc[l].astype(BF16)


def filter_back_kernel(sg_ref, k_ref, ahead_ref, taps_ref, sums_in, sums2_ref, grad_ref, small_ref, keys, taps, sums):
    tok, width = k_ref.shape
    count = width // LANES
    for l in range(count):
        span = slice(l * LANES, (l + 1) * LANES)
        keys[l, STEP:] = k_ref[:, span].astype(F32)
        taps[l] = taps_ref[:, span].astype(F32)
    sums[...] = sums_in[...]

    def chunk(c, carry):
        s0 = pl.multiple_of(c * STEP, STEP)
        acc = filter_back_chunk(sg_ref, keys, taps, ahead_ref[pl.ds(s0, STEP)], sums, count, s0)
        for l in range(count):
            grad_ref[pl.ds(s0 - STEP, STEP), l * LANES : (l + 1) * LANES] = acc[l]
        return carry

    lax.fori_loop(1, tok // STEP + 1, chunk, 0)
    for l in range(count):
        small_ref[:STEP, l * LANES : (l + 1) * LANES] = jnp.sum(sums[l], axis=1)
    small_ref[STEP:] = jnp.zeros_like(small_ref[STEP:])
    small_ref[STEP : STEP + 4] = flat_rows(sums2_ref[:2], width)


def out_kernel(place_ref, grad_ref, edge_ref, docc_ref, dq_ref, dv_ref, wq_ref, wk_ref, wv_ref, own_ref, other_ref,
               key_ref, part_ref, rows, total, sums_ref):
    h = place_ref[1]
    tok, width = own_ref.shape
    keep = docc_ref[tok - STEP :] == docc_ref[tok - 1 :]
    key_ref[: tok - STEP] = grad_ref[: tok - STEP].astype(BF16)
    for l in lanes(width):
        span = slice(l, l + LANES)
        edge = jnp.where(keep, edge_ref[:, span].astype(F32), 0.0)
        key_ref[tok - STEP :, span] = (grad_ref[tok - STEP :, span] + edge).astype(BF16)
    total[...] = (mm(dq_ref[...], wq_ref[...], NT) + mm(dv_ref[...], wv_ref[...], NT)
                  + mm(key_ref[...], wk_ref[...], NT))
    part_ref[:tok] = total[...].astype(BF16)
    half_of(rows, h, width)[...] = own_ref[...]
    half_of(rows, 1 - h, width)[...] = other_ref[...]
    sums_ref[...] = jnp.zeros_like(sums_ref)

    def norm(at):
        unit, _ = norm_rows(rows[at].astype(F32))
        sums_ref[0:1] += jnp.sum(total[at] * unit, axis=0, keepdims=True)
        sums_ref[1:2] += jnp.sum(total[at], axis=0, keepdims=True)

    by_rows(tok, norm)
    part_ref[tok:] = sums_ref[...].astype(BF16)


def key_grads_kernel(stage, place_ref, normed_ref, key_ref, small_ref, part_ref, got_ref, *refs):
    radix = stage[1]
    outs, total, shared = refs[:radix], refs[-2], refs[-1]
    put_rows(total, 0, mm(normed_ref[...], key_ref[...], TN))
    tok, width = key_ref.shape
    sums = part_ref[tok:].astype(F32) + got_ref[tok:].astype(F32)
    shared[...] = small_ref[...]
    shared[STEP + 8 : STEP + 12] = flat_rows(sums[:2], width)
    put_messages(total, shared[...], radix, member_at(place_ref, *stage), outs)


def input_kernel(place_ref, part_ref, got_ref, own_ref, other_ref, gain_ref, resid_grad_ref, out_ref, rows, back):
    h = place_ref[1]
    tok, width = own_ref.shape
    half_of(rows, h, width)[...] = own_ref[...]
    half_of(rows, 1 - h, width)[...] = other_ref[...]

    def norm(at):
        unit, inverse = norm_rows(rows[at].astype(F32))
        grad = part_ref[at].astype(F32) + got_ref[at].astype(F32)
        back[at] = norm_back(grad, unit, inverse, row_of(gain_ref))

    by_rows(tok, norm)
    out_ref[...] = (half_of(back, h, width)[...] + resid_grad_ref[...]).astype(BF16)


def local(block_input, starts, decay_rate, norm1_gain, norm1_bias, q_weight, k_weight, v_weight,
          shift_kernel, out_weight, norm2_gain, norm2_bias, up_weight, down_weight, out_grad):
    tok, width = block_input.shape
    heads = decay_rate.shape[0]
    full = 2 * width
    hidden_width = up_weight.shape[1]
    count = width // LANES
    seqs = lax.axis_size("seq")
    place = jnp.stack([lax.axis_index("seq"), lax.axis_index("head")]).astype(jnp.int32)
    gain1, bias1, gain2, bias2 = norm1_gain, norm1_bias, norm2_gain, norm2_bias
    vm = pltpu.VMEM

    stages = digits_of(seqs)
    other_input = swapped(block_input)
    other_grad = swapped(out_grad)
    other_out = swapped(out_weight)
    beta = jnp.sqrt(-jnp.expm1(-2.0 * jnp.minimum(decay_rate, RATE_CAP)))
    lamr, lamc, docr, docc, dist, beta_w, first_w, last_w, gate_w = run(
        side_kernel,
        (shape((8 * count, tok), F32), shape((count * tok, LANES), F32), shape((8, tok), F32),
         shape((tok, LANES), F32), shape((tok, LANES), F32),
         shape((tok, width), F32), shape((tok, width), F32), shape((tok, width), F32), shape((16, width), BF16)),
        starts, decay_rate, beta,
        scratch=[vm((tok, tok), BF16), vm((tok, tok), BF16), vm((LANES, tok), F32)], us=2.7)
    other_input = after(other_input, docc)
    normed1, query, key, value, tail = run(
        in_kernel,
        (shape((tok, full), BF16),) + (shape((tok, width), BF16),) * 3 + (shape((STEP, width), BF16),),
        place, block_input, other_input, gain1, bias1, q_weight, k_weight, v_weight, docc,
        scratch=[vm((tok, full), BF16)], scalars=1, us=3.0)
    prev_tail = passed_along(tail, 1)
    scaled_part = run(
        filter_kernel, shape((tok, width), BF16), key, shift_kernel, dist, beta_w,
        scratch=[vm((count, tok + STEP, LANES), F32), vm((count, STEP, LANES), F32)], us=5.4)
    prev_tail = after(prev_tail, scaled_part)
    scaled, message = run(
        state_kernel, (shape((tok, width), BF16), shape((STEP + 16, width), BF16)),
        scaled_part, prev_tail, key, shift_kernel, dist, beta_w, last_w, value, gate_w,
        scratch=[vm((count, 2 * STEP, LANES), F32), vm((count, STEP, LANES), F32)], us=1.7)
    pair_spec = pl.BlockSpec((tok, LANES), lambda p: (0, p))
    lamr_spec = pl.BlockSpec((8, tok), lambda p: (p, 0))
    lamc_spec = pl.BlockSpec((tok, LANES), lambda p: (p, 0))
    state_spec = pl.BlockSpec((STEP, LANES), lambda p: (0, p))
    tile = 512

    before = ()
    got = scan_send(message, 0, False)
    hidden_grad, grad_full = run(
        hidden_grad_kernel, (shape((tok, hidden_width), BF16), shape((tok, full), BF16)),
        place, out_grad, after(other_grad, message), down_weight, scalars=1,
        grid=(hidden_width // tile,), in_specs=[None, None, pl.BlockSpec((full, tile), lambda i: (0, i))],
        out_specs=(pl.BlockSpec((tok, tile), lambda i: (0, i)), None), us=2.5)
    last_got = [after(g, hidden_grad) for g in got]
    for at in range(len(stages) - 1):
        before, message = scan_link(place, last_got, before, at, False)
        last_got = scan_send(message, at + 1, False)
    query_late = after(query, message)
    inside = run(
        inside_kernel, shape((tok, width), F32), query_late, scaled, value, lamr, lamc, docr, docc,
        grid=(count,),
        in_specs=[pair_spec] * 3 + [lamr_spec, lamc_spec, None, None], out_specs=pair_spec, us=3.5)
    last_got = [after(g, inside) for g in last_got]
    state, mixed = run(
        functools.partial(mixed_kernel, stages[-1]), (shape((STEP, width), F32), shape((tok, width), BF16)),
        place, inside, query, first_w, *last_got, *before, scalars=1, us=1.2)
    mixed_other = swapped(mixed)

    wide_tile = pl.BlockSpec((full, tile), lambda i: (0, i))
    tok_tile = pl.BlockSpec((tok, tile), lambda i: (0, i))
    resid, normed2, hidden, pre_grad, part2 = run(
        ffn_kernel,
        (shape((tok, full), F32), shape((tok, full), BF16), shape((tok, hidden_width), BF16),
         shape((tok, hidden_width), BF16), shape((tok, full), BF16)),
        place, block_input, other_input, mixed, mixed_other, out_weight, other_out, gain2, bias2, up_weight, hidden_grad,
        scratch=[vm((tok, full), BF16), vm((tok, full), F32)], scalars=1, mib=24,
        grid=(hidden_width // tile,),
        in_specs=[None] * 8 + [wide_tile, tok_tile],
        out_specs=(None, None, tok_tile, tok_tile, None), us=10.8)
    got2 = swapped(part2)
    *down_halves, ffn_own, ffn_send = run(
        down_kernel,
        split_shapes(seqs, full // seqs, (half_width(hidden_width), hidden_width - half_width(hidden_width)))
        + (shape((tok, width), F32), shape((tok, width), BF16)),
        place, grad_full, hidden, down_weight, resid, scalars=1,
        scratch=[vm((seqs, full // seqs, hidden_width), F32), vm((tok, full), F32)], mib=24, us=4.0)
    got2 = after(got2, ffn_own)
    resid_grad, branch, g_low, sums2, message = run(
        norm2_kernel,
        (shape((tok, width), F32), shape((tok, full), BF16), shape((tok, width), BF16), shape((8, full), F32),
         shape((STEP + 16, width), BF16)),
        place, part2, got2, resid, grad_full, gain2, out_weight, query, first_w, gate_w,
        scratch=[vm((tok, full), F32)], scalars=1, us=3.2)
    before = ()
    got = scan_send(message, 0, True)
    ffn_other = swapped(after(ffn_send, message))
    up_halves = grad_halves(place, [(after(normed2, message), pre_grad)], 2.5)
    got = [after(g, up_halves[0]) for g in got]
    for at in range(len(stages) - 1):
        before, message = scan_link(place, got, before, at, True)
        got = scan_send(message, at + 1, True)
    down_got = mirrored(after(down_halves[1], message), 1), mirrored(after(down_halves[3], message), 2)
    query_late = after(query, message)
    query_grad, dk_part, dv_part = run(
        back_kernel, (shape((tok, width), BF16), shape((tok, width), F32), shape((tok, width), F32)),
        query_late, scaled, value, g_low, lamr, lamc, docr, docc, first_w, state,
        grid=(count,),
        in_specs=[pair_spec] * 4 + [lamr_spec, lamc_spec, None, None, pair_spec, state_spec],
        out_specs=(pair_spec,) * 3, us=5.6)
    got = [after(g, query_grad) for g in got]
    value_grad, shifted_grad, edge, sums, ahead, block_output = run(
        functools.partial(carry_kernel, stages[-1]),
        (shape((tok, width), BF16), shape((count, tok + 2 * STEP, LANES), F32), shape((STEP, width), BF16),
         shape((count, STEP, 8, LANES), F32), shape((tok + STEP, LANES), F32), shape((tok, width), BF16)),
        place, dk_part, dv_part, scaled, value, last_w, beta_w, docr, docc, shift_kernel, prev_tail, ffn_own, ffn_other,
        *got, *before, scalars=1,
        scratch=[vm((count, STEP, LANES), F32), vm((count, STEP, LANES), F32)], us=2.4)
    got_edge = passed_along(edge, -1)
    mix_halves = grad_halves(place, [(branch, mixed), (normed1, query_grad), (normed1, after(value_grad, edge))], 2.6)
    mix_widths, ffn_widths = (width,) * 3, (hidden_width,)
    down_got = [after(g, mix_halves[0]) for g in down_got]
    down_halves = cross(place, down_halves, *down_got)
    down_got = mirrored(down_halves[1], 2), mirrored(down_halves[3], 1)
    up_got = mirrored(after(up_halves[1], down_halves[0]), 1), mirrored(after(up_halves[3], down_halves[0]), 2)
    sums = after(sums, down_halves[0])
    key_rows, small_rows = run(
        filter_back_kernel, (shape((tok, width), F32), shape((STEP + 16, width), F32)),
        shifted_grad, key, ahead, shift_kernel, sums, sums2,
        scratch=[vm((count, tok + STEP, LANES), F32), vm((count, STEP, LANES), F32),
                 vm((count, STEP, 8, LANES), F32)], us=12.0)
    down_got = [after(g, key_rows) for g in down_got]
    down_halves = join(place, down_halves, *down_got, ffn_widths)
    down_got = mirrored(down_halves[1], 4)
    up_got = [after(g, down_halves[0]) for g in up_got]
    up_halves = cross(place, up_halves, *up_got)
    up_got = mirrored(up_halves[1], 2), mirrored(up_halves[3], 1)
    got_edge = after(got_edge, up_halves[0])
    key_grad, part1 = run(
        out_kernel, (shape((tok, width), BF16), shape((tok + 8, full), BF16)),
        place, key_rows, got_edge, docc, query_grad, value_grad, q_weight, k_weight, v_weight, block_input, other_input,
        scratch=[vm((tok, full), BF16), vm((tok, full), F32), vm((8, full), F32)], scalars=1, us=3.2)
    got1 = swapped(part1)
    up_got = [after(g, key_grad) for g in up_got]
    up_halves = join(place, up_halves, *up_got, ffn_widths)
    up_got = mirrored(up_halves[1], 4)
    mix_got = mirrored(after(mix_halves[1], up_halves[0]), 1), mirrored(after(mix_halves[3], up_halves[0]), 2)
    down_halves = fold_bit(place, down_halves, after(down_got, up_halves[0]), 2, ffn_widths)
    down_got = mirrored(down_halves[1], 8)
    rows = full // seqs
    radix = stages[0][1]
    key_messages = run(
        functools.partial(key_grads_kernel, stages[0]),
        (shape((seqs // radix * rows + STEP + 16, width), BF16),) * radix,
        place, normed1, key_grad, small_rows, part1, after(got1, down_halves[0]), scalars=1,
        scratch=[vm((seqs, rows, width), F32), vm((STEP + 16, width), F32)], us=1.4)
    key_got = send_pieces(key_messages, *stages[0])
    input_grad = run(
        input_kernel, shape((tok, width), BF16),
        place, part1, after(got1, key_messages[0]), block_input, other_input, gain1, resid_grad, scalars=1,
        scratch=[vm((tok, full), BF16), vm((tok, full), F32)], us=3.2)
    mix_got = [after(g, input_grad) for g in mix_got]
    mix_halves = cross(place, mix_halves, *mix_got)
    mix_got = mirrored(mix_halves[1], 2), mirrored(mix_halves[3], 1)
    up_halves = fold_bit(place, up_halves, after(up_got, mix_halves[0]), 2, ffn_widths)
    up_got = mirrored(up_halves[1], 8)
    (down_total,) = fold_rest(place, down_halves, after(down_got, up_halves[0]), 3, ffn_widths)
    key_got = [after(g, down_total) for g in key_got]
    key_messages = add_messages(place, key_got, 0, rows)
    key_got = send_pieces(key_messages, *stages[1])
    mix_got = [after(g, key_messages[0]) for g in mix_got]
    mix_halves = join(place, mix_halves, *mix_got, mix_widths)
    mix_got = mirrored(mix_halves[1], 4)
    (up_total,) = fold_rest(place, up_halves, after(up_got, mix_halves[0]), 3, ffn_widths)
    mix_halves = fold_bit(place, mix_halves, after(mix_got, up_total), 2, mix_widths)
    mix_got = mirrored(mix_halves[1], 8)
    key_got = [after(g, mix_halves[0]) for g in key_got]
    for at in range(1, len(stages) - 1):
        key_got = send_pieces(add_messages(place, key_got, at, rows), *stages[at + 1])
    k_total, taps_total, gain2_grad, bias2_grad, gain1_grad, bias1_grad = add_messages(
        place, key_got, len(stages) - 1, rows)
    out_total, q_total, v_total = fold_rest(place, mix_halves, after(mix_got, k_total), 3, mix_widths)
    return (block_output, input_grad, gain1_grad, bias1_grad, q_total, k_total, v_total, taps_total, out_total,
            gain2_grad, bias2_grad, up_total, down_total)


def solution(mesh):
    both, head = P("seq", "head"), P(None, "head")
    in_specs = (both, P("seq"), P("head", "seq"), P(), P(), head, head, head, head, head, P(), P(), head, head, both)
    out_specs = (both, both, P(), P(), both, both, both, head, both, P(), P(), both, both)
    return jax.shard_map(local, mesh=mesh, in_specs=in_specs, out_specs=out_specs, check_vma=False)
```

```python
import functools

import jax
import jax.numpy as jnp
from jax import lax
from jax.experimental import pallas as pl
from jax.experimental.pallas import tpu as pltpu
from jax.sharding import PartitionSpec as P

NORM_EPS = 1e-05
RATE_CAP = 0.05
LANES = 128
STEP = 64
FAR = float(1 << 20)
GELU_SCALE = 0.7978845608028654
GELU_CUBE = 0.044715
F32 = jnp.float32
BF16 = jnp.bfloat16

NN = (((1,), (0,)), ((), ()))
NT = (((1,), (1,)), ((), ()))
TN = (((0,), (0,)), ((), ()))


def mm(a, b, dims=NN):
    return lax.dot_general(a, b, dims, preferred_element_type=F32)


def shape(dims, kind):
    return pltpu.HBM(dims, kind)


def shape(dims, kind):
    return jax.ShapeDtypeStruct(dims, kind)


FEW = pl.BlockSpec(memory_space=pltpu.SMEM)


def whole(array):
    dims = array.shape
    return pl.BlockSpec(dims, lambda *_: (0,) * len(dims), pipeline_mode=pl.Buffered(1))


def run(body, outs, *ins, scratch=(), scalars=0, grid=(1,), in_specs=None, out_specs=None, mib=16,
        us=1.0, far=()):
    many = isinstance(outs, (tuple, list))
    held = [pltpu.with_memory_space_constraint(x, pltpu.HBM) if i in far else x for i, x in enumerate(ins)]
    if in_specs is None:
        in_specs = [None] * (len(ins) - scalars)
    if out_specs is None:
        out_specs = (None,) * len(outs) if many else None
    in_specs = [spec or whole(x) for spec, x in zip(in_specs, ins[scalars:])]
    pick = lambda spec, x: spec or whole(x)
    out_specs = tuple(map(pick, out_specs, outs)) if many else pick(out_specs, outs)
    return pl.pallas_call(
        body, out_shape=outs, grid=grid, in_specs=[FEW] * scalars + list(in_specs), out_specs=out_specs,
        scratch_shapes=list(scratch), compiler_params=pltpu.CompilerParams(vmem_limit_bytes=mib << 20),
        cost_estimate=pl.CostEstimate(flops=int(us * 1e9), transcendentals=0, bytes_accessed=int(us * 3e6)))(*held)


def after(value, *first):
    return lax.optimization_barrier((value,) + first)[0]


def lanes(width):
    return range(0, width, LANES)


def half_of(ref, h, width):
    return ref.at[:, pl.ds(pl.multiple_of(h * width, LANES), width)]


def digits_of(count):
    digits, stride = [], 1
    while count > 1:
        radix = 4 if count % 4 == 0 else (2 if count % 2 == 0 else count)
        digits.append((stride, radix))
        stride, count = stride * radix, count // radix
    return digits


def turned(array, stride, radix, by):
    pairs = []
    for i in range(lax.axis_size("seq")):
        member = i // stride % radix
        pairs.append((i, i + ((member + by) % radix - member) * stride))
    return lax.ppermute(array, "seq", pairs)


def crossed(array, stride, radix, mask):
    pairs = []
    for i in range(lax.axis_size("seq")):
        member = i // stride % radix
        pairs.append((i, i + ((member ^ mask) - member) * stride))
    return lax.ppermute(array, "seq", pairs)


def swapped(array):
    count = lax.axis_size("head")
    return lax.ppermute(array, "head", [(i, (i + 1) % count) for i in range(count)])


def passed_along(array, by):
    count = lax.axis_size("seq")
    return lax.ppermute(array, "seq", [(i, i + by) for i in range(count) if 0 <= i + by < count])


def member_at(place_ref, stride, radix):
    return lax.rem(lax.div(place_ref[0], stride), radix)


def strides_of(count):
    bits = [1 << k for k in range(count.bit_length() - 1)]
    order = []
    for k in range(0, len(bits) - 1, 2):
        order += [(bits[k], bits[k + 1]), (bits[k + 1], bits[k])]
    return order + [(b, b) for b in bits[len(order) :]]


def mirrored(array, at):
    count, cores = lax.axis_size("seq"), lax.axis_size("head")
    strides = strides_of(count)[at]
    pairs = [(i * cores + h, (i ^ strides[h % 2]) * cores + h) for i in range(count) for h in range(cores)]
    return lax.ppermute(array, ("seq", "head"), pairs)


def pick(place_ref, first, second):
    return jnp.where(place_ref[1] == 0, first, second)


def halved(place_ref, at, count):
    pairs = strides_of(count)
    left = count >> at
    bit = pick(place_ref, *(lax.rem(lax.div(place_ref[0], stride), 2) for stride in pairs[at]))
    split = at % 2 == 0 and pairs[at][0] != pairs[at][1]
    places = []
    for g in range(left // 2):
        if split:
            base, low = pick(place_ref, 2 * g, g // 2 * 4 + g % 2), pick(place_ref, 1, 2)
        else:
            base, low = 2 * g, 1
        places.append((base + bit * low, base + (1 - bit) * low))
    return places


def put_halves(place_ref, at, count, total, keep, send):
    for g, (mine, other) in enumerate(halved(place_ref, at, count)):
        keep[g] = total[mine].astype(BF16)
        send[g] = total[other].astype(BF16)


def put_rows(total, at, grad):
    rows = total.shape[1]
    for s in range(total.shape[0]):
        total[s, :, at : at + grad.shape[1]] = grad[s * rows : (s + 1) * rows]


def half_shapes(entries, rows, width):
    return (shape((entries // 2, rows, width), BF16),) * 2


def grads_kernel(spans, place_ref, *refs):
    lefts, rights, (keep, send), total = refs[: len(spans)], refs[len(spans) : 2 * len(spans)], refs[-3:-1], refs[-1]
    for left, right, at in zip(lefts, rights, spans):
        put_rows(total, at, mm(left[...], right[...], TN))
    put_halves(place_ref, 0, total.shape[0], total, keep, send)


def up_kernel(spans, place_ref, *refs):
    grads_kernel(spans, place_ref, *refs[:4], *refs[6:8], refs[-1])
    refs[8][...] = (refs[4][...] + refs[5][...].astype(F32)).astype(BF16)


def down_kernel(place_ref, grad_ref, hidden_ref, down_ref, resid_ref, keep, send, own_ref, send_ref, total, part):
    part[...] = mm(hidden_ref[...], down_ref[...], NT)
    width = own_ref.shape[1]
    h = place_ref[1]
    own_ref[...] = half_of(part, h, width)[...] + half_of(resid_ref, h, width)[...]
    send_ref[...] = half_of(part, 1 - h, width)[...].astype(BF16)
    put_rows(total, 0, mm(grad_ref[...], hidden_ref[...], TN))
    put_halves(place_ref, 0, total.shape[0], total, keep, send)


def fold_kernel(at, count, place_ref, keep_ref, got_ref, *refs):
    outs, total = refs[:-1], refs[-1]
    for g in range(total.shape[0]):
        total[g] = keep_ref[g].astype(F32) + got_ref[g].astype(F32)
    if total.shape[0] > 1:
        put_halves(place_ref, at + 1, count, total, *outs)
        return
    begin = 0
    for out in outs:
        out[...] = total[0, :, begin : begin + out.shape[1]]
        begin += out.shape[1]


def folded(place, keep, got, at, widths, us):
    entries, rows, width = keep.shape
    outs = half_shapes(entries, rows, width) if entries > 1 else tuple(shape((rows, w), F32) for w in widths)
    return run(functools.partial(fold_kernel, at, lax.axis_size("seq")), outs, place, keep, got, scalars=1,
               scratch=[pltpu.VMEM((entries, rows, width), F32)], us=us)


def folded_last(place, keep, got, at, widths, us):
    while True:
        res = folded(place, keep, got, at, widths, us)
        if keep.shape[0] == 1:
            return res
        keep, got, at = res[0], mirrored(res[1], at + 1), at + 1


def put_messages(place_ref, at, count, total, shared, keep, send):
    rows = total.shape[1]
    places = halved(place_ref, at, count)
    for g, (mine, other) in enumerate(places):
        keep[g * rows : (g + 1) * rows] = total[mine].astype(BF16)
        send[g * rows : (g + 1) * rows] = total[other].astype(BF16)
    end = len(places) * rows
    keep[end:] = shared.astype(BF16)
    send[end:] = shared.astype(BF16)


def message_kernel(at, count, place_ref, keep_ref, got_ref, *refs):
    outs, total = refs[:-1], refs[-1]
    entries, rows, _ = total.shape
    for g in range(entries):
        span = slice(g * rows, (g + 1) * rows)
        total[g] = keep_ref[span].astype(F32) + got_ref[span].astype(F32)
    shared = keep_ref[entries * rows :].astype(F32) + got_ref[entries * rows :].astype(F32)
    if entries > 1:
        put_messages(place_ref, at + 1, count, total, shared, *outs)
        return
    outs[0][...] = total[0]
    outs[1][...] = shared[:STEP]
    outs[2][...] = shared[STEP:]


def folded_message(place, keep, got, at, rows, us):
    depth, width = keep.shape
    extra = STEP + 8
    entries = (depth - extra) // rows
    if entries > 1:
        outs = (shape((entries // 2 * rows + extra, width), BF16),) * 2
    else:
        outs = (shape((rows, width), F32), shape((STEP, width), F32), shape((8, width), F32))
    return run(functools.partial(message_kernel, at, lax.axis_size("seq")), outs, place, keep, got, scalars=1,
               scratch=[pltpu.VMEM((entries, rows, width), F32)], us=us)


def vector_kernel(place_ref, own_ref, other_ref, *outs):
    h = place_ref[1]
    width = own_ref.shape[1]
    own, other = own_ref[...], other_ref[...]
    for k, out in enumerate(outs):
        out[:width] = jnp.where(h == 0, own[k], other[k])
        out[width:] = jnp.where(h == 0, other[k], own[k])


def chained(first, second):
    return first[0] * second[0], second[0] * first[1] + second[1]


def link(stage, reverse, place_ref, messages, before, want_total):
    radix = stage[1]
    member = member_at(place_ref, *stage)
    if reverse:
        member = radix - 1 - member
    rows = messages[0].shape[0] - 16
    pairs = []
    for m in messages:
        whole = m[...].astype(F32)
        pairs.append((whole[rows : rows + 1], whole[:rows]))
    none = (jnp.ones_like(pairs[0][0]), jnp.zeros_like(pairs[0][1]))

    def side(use):
        acc = none
        for by in range(radix - 1, 0, -1):
            kept = use(by)
            part = (jnp.where(kept, pairs[by][0], none[0]), jnp.where(kept, pairs[by][1], none[1]))
            acc = chained(acc, part)
        return acc

    lower = side(lambda by: by <= member)
    before = chained(lower, tuple(b[...] for b in before)) if before else lower
    if not want_total:
        return before, None
    return before, chained(chained(lower, pairs[0]), side(lambda by: by > member))


def link_kernel(stage, reverse, place_ref, *refs):
    messages, held, outs = refs[: stage[1]], refs[stage[1] : -3], refs[-3:]
    before, total = link(stage, reverse, place_ref, messages, held, True)
    outs[0][...], outs[1][...] = before
    rows = outs[1].shape[0]
    outs[2][:rows] = total[1].astype(BF16)
    outs[2][rows:] = jnp.broadcast_to(total[0], (outs[2].shape[0] - rows, total[0].shape[1])).astype(BF16)


def scan_send(message, at, reverse):
    stride, radix = digits_of(lax.axis_size("seq"))[at]
    return [message] + [
        turned(message, stride, radix, (radix - by) if reverse else by) for by in range(1, radix)
    ]


def scan_link(place, got, before, at, reverse):
    stage = digits_of(lax.axis_size("seq"))[at]
    rows, width = got[0].shape
    outs = run(functools.partial(link_kernel, stage, reverse),
               (shape((1, width), F32), shape((rows - 16, width), F32), shape((rows, width), BF16)),
               place, *got, *before, scalars=1, us=8)
    return outs[:2], outs[2]


def split_parts(x, count):
    parts = []
    for _ in range(count):
        low = x.astype(BF16)
        parts.append(low)
        x = x - low.astype(F32)
    return parts


def side_kernel(starts_ref, decay_ref, beta_ref, lamr_ref, lamc_ref, docr_ref, docc_ref, dist_ref,
                beta_out, first_out, last_out, gate_out, tri, same, wide):
    tok = starts_ref.shape[0]
    heads = decay_ref.shape[0]
    head_pairs = lamc_ref.shape[0] // tok
    width = beta_out.shape[1]
    row = lax.broadcasted_iota(jnp.int32, (tok, tok), 0)
    col = lax.broadcasted_iota(jnp.int32, (tok, tok), 1)
    tri[...] = (col <= row).astype(F32).astype(BF16)
    begins = jnp.broadcast_to(row_of(starts_ref).astype(F32), (LANES, tok)).astype(BF16)
    doc_col = mm(tri[...], begins, NT)
    doc_row = mm(begins[:16], tri[...], NT)[:8]
    docr_ref[...] = doc_row
    docc_ref[...] = doc_col
    wide[...] = jnp.zeros_like(wide)
    wide[:heads] = decay_ref[...]
    lam_col = jnp.zeros((tok, LANES), F32)
    lam_row = jnp.zeros((16, tok), F32)
    for part in split_parts(wide[...], 3):
        lam_col = lam_col + mm(tri[...], part, NT)
        lam_row = lam_row + mm(part[:16], tri[...], NT)
    lamr_ref[...] = jnp.zeros_like(lamr_ref)
    for p in range(head_pairs):
        lamr_ref[8 * p : 8 * p + 2] = lam_row[2 * p : 2 * p + 2]
        lamc_ref[p * tok : (p + 1) * tok] = lam_col if p == 0 else pltpu.roll(lam_col, LANES - 2 * p, 1)
    ones = jnp.ones((tok, LANES), BF16)
    alike = doc_col[:, :1] == doc_row[:1]
    same[...] = jnp.where(alike & (col <= row), 1.0, 0.0).astype(BF16)
    behind = mm(same[...], ones)
    dist_ref[...] = jnp.where(doc_col == 0.0, FAR, behind - 1.0)
    lam_end = lam_col[tok - 1 :]
    doc_end = doc_col[tok - 1 :]
    first = jnp.where(doc_col == 0.0, jnp.exp(-lam_col), 0.0)
    last = jnp.where(doc_col == doc_end, jnp.exp(lam_col - lam_end), 0.0)
    spread = (lax.broadcasted_iota(jnp.int32, (LANES, width), 0)
              == lax.broadcasted_iota(jnp.int32, (LANES, width), 1) // (width // heads))
    spread = spread.astype(F32).astype(BF16)
    for ref, value in ((first_out, first), (last_out, last)):
        parts = split_parts(value, 2)
        ref[...] = mm(parts[0], spread) + mm(parts[1], spread)
    wide[:heads] = beta_ref[...]
    eye = (row == col).astype(F32).astype(BF16)
    beta_col = jnp.zeros((tok, LANES), F32)
    for part in split_parts(wide[...], 2):
        beta_col = beta_col + mm(eye, part, NT)
    parts = split_parts(beta_col, 2)
    beta_out[...] = mm(parts[0], spread) + mm(parts[1], spread)
    gate_out[...] = jnp.broadcast_to(first_out[tok - 1 :], gate_out.shape).astype(BF16)


def row_of(ref):
    return ref[...].reshape(1, ref.shape[0])


def norm_rows(rows_in):
    count = rows_in.shape[1]
    center = rows_in - jnp.sum(rows_in, axis=1, keepdims=True) * (1.0 / count)
    spread = jnp.sum(center * center, axis=1, keepdims=True) * (1.0 / count)
    inverse = lax.rsqrt(spread + NORM_EPS)
    return center * inverse, inverse


def norm_back(grad_rows, unit_rows, inverse, gain_vec):
    scale = 1.0 / grad_rows.shape[1]
    scaled = grad_rows * gain_vec
    return inverse * (scaled - jnp.sum(scaled, axis=1, keepdims=True) * scale
                      - unit_rows * (jnp.sum(scaled * unit_rows, axis=1, keepdims=True) * scale))


def by_rows(tok, body, size=64):
    def step(i, carry):
        body(pl.ds(pl.multiple_of(i * size, size), size))
        return carry

    lax.fori_loop(0, tok // size, step, 0)


def in_kernel(place_ref, own_ref, other_ref, gain_ref, bias_ref, wq_ref, wk_ref, wv_ref, docc_ref,
              normed_ref, q_ref, k_ref, v_ref, tail_ref, rows):
    h = place_ref[1]
    tok, width = own_ref.shape
    half_of(rows, h, width)[...] = own_ref[...]
    half_of(rows, 1 - h, width)[...] = other_ref[...]

    def norm(at):
        unit, _ = norm_rows(rows[at].astype(F32))
        normed_ref[at] = (unit * row_of(gain_ref) + row_of(bias_ref)).astype(BF16)

    by_rows(tok, norm)
    normed = normed_ref[...]
    k_ref[...] = mm(normed, wk_ref[...]).astype(BF16)
    keep = docc_ref[tok - STEP :] == docc_ref[tok - 1 :]
    for l in lanes(width):
        tail_ref[:, l : l + LANES] = jnp.where(
            keep, k_ref[tok - STEP :, l : l + LANES].astype(F32), 0.0).astype(BF16)
    q_ref[...] = mm(normed, wq_ref[...]).astype(BF16)
    v_ref[...] = mm(normed, wv_ref[...]).astype(BF16)


def filter_chunk(keys, taps, dist, count, t0):
    def group(a, acc):
        acc = list(acc)
        for b in range(8):
            j = a * 8 + b
            keep = dist >= j.astype(F32)
            for l in range(count):
                x = keys[l, pl.ds(STEP + t0 - a * 8 - b, STEP), :]
                acc[l] = acc[l] + jnp.where(keep, x * taps[l, pl.ds(j, 1), :], 0.0)
        return tuple(acc)

    return lax.fori_loop(0, 8, group, tuple(jnp.zeros((STEP, LANES), F32) for _ in range(count)))


def filter_kernel(k_ref, taps_ref, dist_ref, beta_ref, out_ref, keys, taps):
    tok, width = k_ref.shape
    count = width // LANES
    for l in range(count):
        keys[l, STEP:] = k_ref[:, l * LANES : (l + 1) * LANES].astype(F32)
        taps[l] = taps_ref[:, l * LANES : (l + 1) * LANES].astype(F32)
    out_ref[:STEP] = jnp.zeros((STEP, width), BF16)

    def chunk(c, carry):
        t0 = pl.multiple_of(c * STEP, STEP)
        at = pl.ds(t0, STEP)
        acc = filter_chunk(keys, taps, dist_ref[at], count, t0)
        for l in range(count):
            span = slice(l * LANES, (l + 1) * LANES)
            out_ref[at, span] = (acc[l] * beta_ref[at, span]).astype(BF16)
        return carry

    lax.fori_loop(1, tok // STEP, chunk, 0)


def fold(square, low):
    return jnp.where(low, square[:STEP], square[STEP:])


def unfold(flat, low):
    return jnp.concatenate([jnp.where(low, flat, 0.0), jnp.where(low, 0.0, flat)], axis=0)


def low_lanes(rows):
    return lax.broadcasted_iota(jnp.int32, (rows, LANES), 1) < STEP


def state_kernel(part_ref, tail_ref, k_ref, taps_ref, dist_ref, beta_ref, last_ref, v_ref, gate_ref,
                 sk_ref, message_ref, keys, taps):
    tok, width = part_ref.shape
    count = width // LANES
    for l in range(count):
        span = slice(l * LANES, (l + 1) * LANES)
        keys[l, :STEP] = tail_ref[:, span].astype(F32)
        keys[l, STEP:] = k_ref[:STEP, span].astype(F32)
        taps[l] = taps_ref[:, span].astype(F32)
    sk_ref[...] = part_ref[...]
    acc = filter_chunk(keys, taps, dist_ref[:STEP], count, 0)
    low = low_lanes(STEP)
    for l in range(count):
        span = slice(l * LANES, (l + 1) * LANES)
        sk_ref[:STEP, span] = (acc[l] * beta_ref[:STEP, span]).astype(BF16)
        weighted = (sk_ref[:, span].astype(F32) * last_ref[:, span]).astype(BF16)
        message_ref[:STEP, span] = fold(mm(weighted, v_ref[:, span], TN), low).astype(BF16)
    message_ref[STEP:] = gate_ref[...]


def kept_pairs(docc_ref, docr_ref):
    tok = docc_ref.shape[0]
    order = lax.broadcasted_iota(jnp.int32, (tok, tok), 0) >= lax.broadcasted_iota(jnp.int32, (tok, tok), 1)
    return (docc_ref[:, :1] == docr_ref[:1]) & order


def own_lanes(x, low, e):
    return jnp.where(low if e == 0 else ~low, x.astype(F32), 0.0).astype(BF16)


def decay_of(lamr_ref, lamc_ref, keep, e):
    span = jnp.minimum(lamr_ref[e : e + 1] - lamc_ref[:, e : e + 1], 0.0)
    return jnp.where(keep, jnp.exp(span), 0.0)


def inside_kernel(q_ref, k_ref, v_ref, lamr_ref, lamc_ref, docr_ref, docc_ref, out_ref):
    low = low_lanes(q_ref.shape[0])
    keep = kept_pairs(docc_ref, docr_ref)
    outs = []
    for e in range(2):
        score = mm(own_lanes(q_ref[...], low, e), k_ref[...], NT)
        outs.append(mm((score * decay_of(lamr_ref, lamc_ref, keep, e)).astype(BF16), v_ref[...]))
    out_ref[...] = jnp.where(low, outs[0], outs[1])


def mixed_kernel(stage, place_ref, inside_ref, q_ref, first_ref, *refs):
    (state_ref, mixed_ref) = refs[-2:]
    before, _ = link(stage, False, place_ref, refs[: stage[1]], refs[stage[1] : -2], False)
    state_ref[...] = before[1]
    low = low_lanes(STEP)
    for l in lanes(q_ref.shape[1]):
        span = slice(l, l + LANES)
        square = unfold(state_ref[:, span], low).astype(BF16)
        mixed_ref[:, span] = (0.125 * (inside_ref[:, span] + first_ref[:, span] * mm(q_ref[:, span], square))
                              ).astype(BF16)


def hidden_grad_kernel(place_ref, own_ref, other_ref, down_ref, out_ref, full_ref):
    @pl.when(pl.program_id(0) == 0)
    def _():
        width = own_ref.shape[1]
        half_of(full_ref, place_ref[1], width)[...] = own_ref[...]
        half_of(full_ref, 1 - place_ref[1], width)[...] = other_ref[...]

    out_ref[...] = mm(full_ref[...], down_ref[...]).astype(BF16)


def ffn_kernel(place_ref, own_ref, other_ref, mix_own_ref, mix_other_ref, out_own_ref, out_other_ref, gain_ref,
               bias_ref, up_ref, hg_ref, resid_ref, normed_ref, hidden_ref, pre_ref, part_ref, rows, acc):
    h = place_ref[1]
    step = pl.program_id(0)
    tok, width = own_ref.shape

    @pl.when(step == 0)
    def _():
        half_of(rows, h, width)[...] = own_ref[...]
        half_of(rows, 1 - h, width)[...] = other_ref[...]
        resid_ref[...] = mm(mix_own_ref[...], out_own_ref[...], NT) + mm(mix_other_ref[...], out_other_ref[...], NT)

        def norm(at):
            resid = rows[at].astype(F32) + resid_ref[at]
            resid_ref[at] = resid
            unit, _ = norm_rows(resid)
            normed_ref[at] = (unit * row_of(gain_ref) + row_of(bias_ref)).astype(BF16)

        by_rows(tok, norm)
        acc[...] = jnp.zeros_like(acc)

    pre = mm(normed_ref[...], up_ref[...])
    square = pre * pre
    bent = jnp.tanh(GELU_SCALE * (pre + GELU_CUBE * (square * pre)))
    outer = 0.5 * (1.0 + bent)
    hidden_ref[...] = (pre * outer).astype(BF16)
    slope = outer + 0.5 * pre * (1.0 - bent * bent) * (GELU_SCALE * (1.0 + 3.0 * GELU_CUBE * square))
    pre_ref[...] = (hg_ref[...].astype(F32) * slope).astype(BF16)
    acc[...] += mm(pre_ref[...], up_ref[...], NT)

    @pl.when(step == pl.num_programs(0) - 1)
    def _():
        part_ref[...] = acc[...].astype(BF16)


def norm2_kernel(place_ref, part_ref, got_ref, resid_ref, grad_ref, gain_ref, out_w_ref, q_ref, first_ref,
                 gate_ref, resid_grad_ref, branch_ref, g_ref, sums_ref, message_ref, rows):
    h = place_ref[1]
    tok, width = q_ref.shape
    sums_ref[...] = jnp.zeros_like(sums_ref)

    def norm(at):
        back = part_ref[at].astype(F32) + got_ref[at].astype(F32)
        unit, inverse = norm_rows(resid_ref[at])
        grad = grad_ref[at].astype(F32) + norm_back(back, unit, inverse, row_of(gain_ref))
        rows[at] = grad
        branch_ref[at] = grad.astype(BF16)
        sums_ref[0:1] += jnp.sum(back * unit, axis=0, keepdims=True)
        sums_ref[1:2] += jnp.sum(back, axis=0, keepdims=True)

    by_rows(tok, norm)
    resid_grad_ref[...] = half_of(rows, h, width)[...]
    g_ref[...] = (0.125 * mm(branch_ref[...], out_w_ref[...]).astype(BF16).astype(F32)).astype(BF16)
    low = low_lanes(STEP)
    for l in lanes(width):
        span = slice(l, l + LANES)
        weighted = (q_ref[:, span].astype(F32) * first_ref[:, span]).astype(BF16)
        message_ref[:STEP, span] = fold(mm(weighted, g_ref[:, span], TN), low).astype(BF16)
    message_ref[STEP:] = gate_ref[...]


def back_kernel(q_ref, k_ref, v_ref, g_ref, lamr_ref, lamc_ref, docr_ref, docc_ref, first_ref, state_ref,
                dq_ref, dk_ref, dv_ref):
    low = low_lanes(q_ref.shape[0])
    keep = kept_pairs(docc_ref, docr_ref)
    square = unfold(state_ref[...], low_lanes(STEP)).astype(BF16)
    outs = []
    for e in range(2):
        decay = decay_of(lamr_ref, lamc_ref, keep, e)
        prob = (mm(own_lanes(q_ref[...], low, e), k_ref[...], NT) * decay).astype(BF16)
        score = (mm(own_lanes(g_ref[...], low, e), v_ref[...], NT) * decay).astype(BF16)
        outs.append((mm(score, k_ref[...]), mm(score, q_ref[...], TN), mm(prob, g_ref[...], TN)))
    from_state = first_ref[...] * mm(g_ref[...], square, NT)
    dq_ref[...] = (jnp.where(low, outs[0][0], outs[1][0]) + from_state).astype(BF16)
    dk_ref[...] = jnp.where(low, outs[0][1], outs[1][1])
    dv_ref[...] = jnp.where(low, outs[0][2], outs[1][2])


def filter_back_chunk(sg, keys, taps, ahead, sums, count, s0):
    held = [keys[l, pl.ds(s0, STEP), :] for l in range(count)]

    def group(a, acc):
        acc = list(acc)
        for b in range(8):
            j = a * 8 + b
            keep = ahead > j.astype(F32)
            for l in range(count):
                u = jnp.where(keep, sg[l, pl.ds(s0 + a * 8 + b, STEP), :], 0.0)
                acc[l] = acc[l] + u * taps[l, pl.ds(j, 1), :]
                sums[l, j] += jnp.sum((held[l] * u).reshape(STEP // 8, 8, LANES), axis=0)
        return tuple(acc)

    return lax.fori_loop(0, 8, group, tuple(jnp.zeros((STEP, LANES), F32) for _ in range(count)))


def reach(docr_ref, docc_ref, ahead_ref):
    tok = docc_ref.shape[0]
    order = lax.broadcasted_iota(jnp.int32, (tok, tok), 0) <= lax.broadcasted_iota(jnp.int32, (tok, tok), 1)
    same = jnp.where((docc_ref[:, :1] == docr_ref[:1]) & order, 1.0, 0.0).astype(BF16)
    ahead_ref[STEP:] = mm(same, jnp.ones((tok, LANES), BF16))
    unbroken = jnp.sum(jnp.where(docr_ref[:1] == 0.0, 1.0, 0.0), axis=1, keepdims=True)
    ahead_ref[:STEP] = unbroken + STEP - lax.broadcasted_iota(jnp.int32, (STEP, LANES), 0).astype(F32)


def carry_kernel(stage, place_ref, dk_ref, dv_ref, k_ref, v_ref, last_ref, beta_ref, docr_ref, docc_ref, taps_ref,
                 tail_ref, *refs):
    value_ref, sg_ref, edge_ref, sums, ahead_ref, taps, keys = refs[-7:]
    reach(docr_ref, docc_ref, ahead_ref)
    before, _ = link(stage, True, place_ref, refs[: stage[1]], refs[stage[1] : -7], False)
    state = before[1]
    tok, width = dk_ref.shape
    count = width // LANES
    low = low_lanes(STEP)
    for l in range(count):
        span = slice(l * LANES, (l + 1) * LANES)
        square = unfold(state[:, span], low).astype(BF16)
        last = last_ref[:, span]
        value_ref[:, span] = (dv_ref[:, span] + last * mm(k_ref[:, span], square)).astype(BF16)
        sg_ref[l, :STEP] = jnp.zeros((STEP, LANES), F32)
        sg_ref[l, STEP : STEP + tok] = beta_ref[:, span] * (
            dk_ref[:, span] + last * mm(v_ref[:, span], square, NT))
        sg_ref[l, STEP + tok :] = jnp.zeros((STEP, LANES), F32)
        keys[l] = tail_ref[:, span].astype(F32)
        taps[l] = taps_ref[:, span].astype(F32)
    sums[...] = jnp.zeros_like(sums)
    acc = filter_back_chunk(sg_ref, keys, taps, ahead_ref[:STEP], sums, count, 0)
    for l in range(count):
        edge_ref[:, l * LANES : (l + 1) * LANES] = acc[l].astype(BF16)


def filter_back_kernel(sg_ref, k_ref, ahead_ref, taps_ref, sums_in, grad_ref, taps_grad_ref, keys, taps, sums):
    tok, width = k_ref.shape
    count = width // LANES
    for l in range(count):
        span = slice(l * LANES, (l + 1) * LANES)
        keys[l, STEP:] = k_ref[:, span].astype(F32)
        taps[l] = taps_ref[:, span].astype(F32)
    sums[...] = sums_in[...]

    def chunk(c, carry):
        s0 = pl.multiple_of(c * STEP, STEP)
        acc = filter_back_chunk(sg_ref, keys, taps, ahead_ref[pl.ds(s0, STEP)], sums, count, s0)
        for l in range(count):
            grad_ref[pl.ds(s0 - STEP, STEP), l * LANES : (l + 1) * LANES] = acc[l]
        return carry

    lax.fori_loop(1, tok // STEP + 1, chunk, 0)
    for l in range(count):
        taps_grad_ref[:, l * LANES : (l + 1) * LANES] = jnp.sum(sums[l], axis=1)


def out_kernel(place_ref, grad_ref, edge_ref, docc_ref, dq_ref, dv_ref, wq_ref, wk_ref, wv_ref, own_ref, other_ref,
               key_ref, part_ref, rows, total, sums_ref):
    h = place_ref[1]
    tok, width = own_ref.shape
    keep = docc_ref[tok - STEP :] == docc_ref[tok - 1 :]
    key_ref[: tok - STEP] = grad_ref[: tok - STEP].astype(BF16)
    for l in lanes(width):
        span = slice(l, l + LANES)
        edge = jnp.where(keep, edge_ref[:, span].astype(F32), 0.0)
        key_ref[tok - STEP :, span] = (grad_ref[tok - STEP :, span] + edge).astype(BF16)
    total[...] = (mm(dq_ref[...], wq_ref[...], NT) + mm(dv_ref[...], wv_ref[...], NT)
                  + mm(key_ref[...], wk_ref[...], NT))
    part_ref[:tok] = total[...].astype(BF16)
    half_of(rows, h, width)[...] = own_ref[...]
    half_of(rows, 1 - h, width)[...] = other_ref[...]
    sums_ref[...] = jnp.zeros_like(sums_ref)

    def norm(at):
        unit, _ = norm_rows(rows[at].astype(F32))
        sums_ref[0:1] += jnp.sum(total[at] * unit, axis=0, keepdims=True)
        sums_ref[1:2] += jnp.sum(total[at], axis=0, keepdims=True)

    by_rows(tok, norm)
    part_ref[tok:] = sums_ref[...].astype(BF16)


def key_grads_kernel(place_ref, normed_ref, key_ref, taps_ref, sums2_ref, part_ref, got_ref, keep, send, total, shared):
    put_rows(total, 0, mm(normed_ref[...], key_ref[...], TN))
    tok, width = key_ref.shape
    shared[STEP:] = jnp.zeros_like(shared[STEP:])
    shared[:STEP] = taps_ref[...]
    sums1 = part_ref[tok:].astype(F32) + got_ref[tok:].astype(F32)
    for at, sums in ((STEP, sums1), (STEP + 2, sums2_ref[...])):
        shared[at : at + 2] = jnp.where(place_ref[1] == 0, sums[:2, :width], sums[:2, width:])
    put_messages(place_ref, 0, total.shape[0], total, shared[...], keep, send)


def input_kernel(place_ref, part_ref, got_ref, own_ref, other_ref, gain_ref, resid_grad_ref, out_ref, rows, back):
    h = place_ref[1]
    tok, width = own_ref.shape
    half_of(rows, h, width)[...] = own_ref[...]
    half_of(rows, 1 - h, width)[...] = other_ref[...]

    def norm(at):
        unit, inverse = norm_rows(rows[at].astype(F32))
        grad = part_ref[at].astype(F32) + got_ref[at].astype(F32)
        back[at] = norm_back(grad, unit, inverse, row_of(gain_ref))

    by_rows(tok, norm)
    out_ref[...] = (half_of(back, h, width)[...] + resid_grad_ref[...]).astype(BF16)


def local(block_input, starts, decay_rate, norm1_gain, norm1_bias, q_weight, k_weight, v_weight,
          shift_kernel, out_weight, norm2_gain, norm2_bias, up_weight, down_weight, out_grad):
    tok, width = block_input.shape
    heads = decay_rate.shape[0]
    full = 2 * width
    hidden_width = up_weight.shape[1]
    count = width // LANES
    seqs = lax.axis_size("seq")
    place = jnp.stack([lax.axis_index("seq"), lax.axis_index("head")]).astype(jnp.int32)
    gain1, bias1, gain2, bias2 = norm1_gain, norm1_bias, norm2_gain, norm2_bias
    vm = pltpu.VMEM

    stages = digits_of(seqs)
    other_input = swapped(block_input)
    other_grad = swapped(out_grad)
    other_out = swapped(out_weight)
    beta = jnp.sqrt(-jnp.expm1(-2.0 * jnp.minimum(decay_rate, RATE_CAP)))
    lamr, lamc, docr, docc, dist, beta_w, first_w, last_w, gate_w = run(
        side_kernel,
        (shape((8 * count, tok), F32), shape((count * tok, LANES), F32), shape((8, tok), F32),
         shape((tok, LANES), F32), shape((tok, LANES), F32),
         shape((tok, width), F32), shape((tok, width), F32), shape((tok, width), F32), shape((16, width), BF16)),
        starts, decay_rate, beta,
        scratch=[vm((tok, tok), BF16), vm((tok, tok), BF16), vm((LANES, tok), F32)], us=2.7)
    other_input = after(other_input, docc)
    normed1, query, key, value, tail = run(
        in_kernel,
        (shape((tok, full), BF16),) + (shape((tok, width), BF16),) * 3 + (shape((STEP, width), BF16),),
        place, block_input, other_input, gain1, bias1, q_weight, k_weight, v_weight, docc,
        scratch=[vm((tok, full), BF16)], scalars=1, us=3.0)
    prev_tail = passed_along(tail, 1)
    scaled_part = run(
        filter_kernel, shape((tok, width), BF16), key, shift_kernel, dist, beta_w,
        scratch=[vm((count, tok + STEP, LANES), F32), vm((count, STEP, LANES), F32)], us=5.4)
    prev_tail = after(prev_tail, scaled_part)
    scaled, message = run(
        state_kernel, (shape((tok, width), BF16), shape((STEP + 16, width), BF16)),
        scaled_part, prev_tail, key, shift_kernel, dist, beta_w, last_w, value, gate_w,
        scratch=[vm((count, 2 * STEP, LANES), F32), vm((count, STEP, LANES), F32)], us=1.7)
    pair_spec = pl.BlockSpec((tok, LANES), lambda p: (0, p))
    lamr_spec = pl.BlockSpec((8, tok), lambda p: (p, 0))
    lamc_spec = pl.BlockSpec((tok, LANES), lambda p: (p, 0))
    state_spec = pl.BlockSpec((STEP, LANES), lambda p: (0, p))
    tile = 512

    before = ()
    got = scan_send(message, 0, False)
    hidden_grad, grad_full = run(
        hidden_grad_kernel, (shape((tok, hidden_width), BF16), shape((tok, full), BF16)),
        place, out_grad, after(other_grad, message), down_weight, scalars=1,
        grid=(hidden_width // tile,), in_specs=[None, None, pl.BlockSpec((full, tile), lambda i: (0, i))],
        out_specs=(pl.BlockSpec((tok, tile), lambda i: (0, i)), None), us=2.5)
    last_got = [after(g, hidden_grad) for g in got]
    for at in range(len(stages) - 1):
        before, message = scan_link(place, last_got, before, at, False)
        last_got = scan_send(message, at + 1, False)
    query_late = after(query, message)
    inside = run(
        inside_kernel, shape((tok, width), F32), query_late, scaled, value, lamr, lamc, docr, docc,
        grid=(count,),
        in_specs=[pair_spec] * 3 + [lamr_spec, lamc_spec, None, None], out_specs=pair_spec, us=3.5)
    last_got = [after(g, inside) for g in last_got]
    state, mixed = run(
        functools.partial(mixed_kernel, stages[-1]), (shape((STEP, width), F32), shape((tok, width), BF16)),
        place, inside, query, first_w, *last_got, *before, scalars=1, us=1.2)
    mixed_other = swapped(mixed)

    wide_tile = pl.BlockSpec((full, tile), lambda i: (0, i))
    tok_tile = pl.BlockSpec((tok, tile), lambda i: (0, i))
    resid, normed2, hidden, pre_grad, part2 = run(
        ffn_kernel,
        (shape((tok, full), F32), shape((tok, full), BF16), shape((tok, hidden_width), BF16),
         shape((tok, hidden_width), BF16), shape((tok, full), BF16)),
        place, block_input, other_input, mixed, mixed_other, out_weight, other_out, gain2, bias2, up_weight, hidden_grad,
        scratch=[vm((tok, full), BF16), vm((tok, full), F32)], scalars=1, mib=24,
        grid=(hidden_width // tile,),
        in_specs=[None] * 8 + [wide_tile, tok_tile],
        out_specs=(None, None, tok_tile, tok_tile, None), us=10.8)
    got2 = swapped(part2)
    rows = full // seqs
    up_width = hidden_width + width
    down_keep, down_send, ffn_own, ffn_send = run(
        down_kernel,
        half_shapes(seqs, rows, hidden_width) + (shape((tok, width), F32), shape((tok, width), BF16)),
        place, grad_full, hidden, down_weight, resid, scalars=1,
        scratch=[vm((seqs, rows, hidden_width), F32), vm((tok, full), F32)], mib=24, us=4.1)
    down_got = mirrored(down_send, 0)
    ffn_other = swapped(ffn_send)
    got2 = after(got2, ffn_own)
    resid_grad, branch, g_low, sums2, message = run(
        norm2_kernel,
        (shape((tok, width), F32), shape((tok, full), BF16), shape((tok, width), BF16), shape((8, full), F32),
         shape((STEP + 16, width), BF16)),
        place, part2, got2, resid, grad_full, gain2, out_weight, query, first_w, gate_w,
        scratch=[vm((tok, full), F32)], scalars=1, us=3.9)
    before = ()
    got = scan_send(message, 0, True)
    up_keep, up_send, block_output = run(
        functools.partial(up_kernel, (0, hidden_width)),
        half_shapes(seqs, rows, up_width) + (shape((tok, width), BF16),),
        place, after(normed2, message), branch, pre_grad, mixed, ffn_own, ffn_other, scalars=1,
        scratch=[vm((seqs, rows, up_width), F32)], mib=24, us=3.2)
    down_keep, down_send = folded(place, down_keep, after(down_got, block_output), 0, (), 4)
    down_got = mirrored(down_send, 1)
    got = [after(g, down_keep) for g in got]
    for at in range(len(stages) - 1):
        before, message = scan_link(place, got, before, at, True)
        got = scan_send(message, at + 1, True)
    up_got = mirrored(after(up_send, message), 0)
    query_late = after(query, message)
    query_grad, dk_part, dv_part = run(
        back_kernel, (shape((tok, width), BF16), shape((tok, width), F32), shape((tok, width), F32)),
        query_late, scaled, value, g_low, lamr, lamc, docr, docc, first_w, state,
        grid=(count,),
        in_specs=[pair_spec] * 4 + [lamr_spec, lamc_spec, None, None, pair_spec, state_spec],
        out_specs=(pair_spec,) * 3, us=2.14)
    got = [after(g, query_grad) for g in got]
    value_grad, shifted_grad, edge, sums, ahead = run(
        functools.partial(carry_kernel, stages[-1]),
        (shape((tok, width), BF16), shape((count, tok + 2 * STEP, LANES), F32), shape((STEP, width), BF16),
         shape((count, STEP, 8, LANES), F32), shape((tok + STEP, LANES), F32)),
        place, dk_part, dv_part, scaled, value, last_w, beta_w, docr, docc, shift_kernel, prev_tail,
        *got, *before, scalars=1,
        scratch=[vm((count, STEP, LANES), F32), vm((count, STEP, LANES), F32)], us=1.0)
    got_edge = passed_along(edge, -1)
    down_keep, down_send = folded(place, down_keep, after(down_got, edge), 1, (), 8)
    down_got = mirrored(down_send, 2)
    mix_keep, mix_send = run(
        functools.partial(grads_kernel, (0, width)), half_shapes(seqs, rows, 2 * width),
        place, normed1, normed1, query_grad, after(value_grad, down_keep), scalars=1,
        scratch=[vm((seqs, rows, 2 * width), F32)], us=1.9)
    mix_got = mirrored(mix_send, 0)
    key_rows, taps_grad = run(
        filter_back_kernel, (shape((tok, width), F32), shape((STEP, width), F32)),
        shifted_grad, key, ahead, shift_kernel, after(sums, mix_keep),
        scratch=[vm((count, tok + STEP, LANES), F32), vm((count, STEP, LANES), F32),
                 vm((count, STEP, 8, LANES), F32)], us=4.7)
    up_keep, up_send = folded(place, up_keep, after(up_got, key_rows), 0, (), 0.2)
    up_got = mirrored(up_send, 1)
    down_keep, down_send = folded(place, down_keep, after(down_got, up_keep), 2, (), 2)
    down_got = mirrored(down_send, 3)
    mix_keep, mix_send = folded(place, mix_keep, after(mix_got, down_keep), 0, (), 2)
    mix_got = mirrored(mix_send, 1)
    key_grad, part1 = run(
        out_kernel, (shape((tok, width), BF16), shape((tok + 8, full), BF16)),
        place, key_rows, after(got_edge, mix_keep), docc, query_grad, value_grad, q_weight, k_weight, v_weight,
        block_input, other_input,
        scratch=[vm((tok, full), BF16), vm((tok, full), F32), vm((8, full), F32)], scalars=1, us=3.6)
    got1 = swapped(part1)
    up_keep, up_send = folded(place, up_keep, after(up_got, key_grad), 1, (), 8)
    up_got = mirrored(up_send, 2)
    key_keep, key_send = run(
        key_grads_kernel, (shape((seqs // 2 * rows + STEP + 8, width), BF16),) * 2,
        place, normed1, key_grad, taps_grad, sums2, part1, after(got1, up_keep), scalars=1,
        scratch=[vm((seqs, rows, width), F32), vm((STEP + 8, width), F32)], us=1.3)
    key_got = mirrored(key_send, 0)
    input_grad = run(
        input_kernel, shape((tok, width), BF16),
        place, part1, after(got1, key_keep), block_input, other_input, gain1, resid_grad, scalars=1,
        scratch=[vm((tok, full), BF16), vm((tok, full), F32)], us=3.7)
    mix_keep, mix_send = folded(place, mix_keep, after(mix_got, input_grad), 1, (), 1)
    mix_got = mirrored(mix_send, 2)
    key_keep, key_send = folded_message(place, key_keep, after(key_got, mix_keep), 0, rows, 8)
    key_got = mirrored(key_send, 1)
    (down_total,) = folded_last(place, down_keep, after(down_got, key_keep), 3, (hidden_width,), 0.5)
    up_keep, up_send = folded(place, up_keep, after(up_got, down_total), 2, (), 0.5)
    up_got = mirrored(up_send, 3)
    key_keep, key_send = folded_message(place, key_keep, after(key_got, up_keep), 1, rows, 2)
    key_got = mirrored(key_send, 2)
    mix_keep, mix_send = folded(place, mix_keep, after(mix_got, key_keep), 2, (), 1)
    mix_got = mirrored(mix_send, 3)
    key_keep, key_send = folded_message(place, key_keep, after(key_got, mix_keep), 2, rows, 0.2)
    key_got = mirrored(key_send, 3)
    up_total, out_total = folded_last(place, up_keep, after(up_got, key_keep), 3, (hidden_width, width), 8)
    key_got = after(key_got, up_total)
    for at in range(3, len(strides_of(seqs)) - 1):
        key_keep, key_send = folded_message(place, key_keep, key_got, at, rows, 0.2)
        key_got = mirrored(key_send, at + 1)
    k_total, taps_total, vectors = folded_message(
        place, key_keep, key_got, len(strides_of(seqs)) - 1, rows, 8)
    other_vectors = swapped(vectors)
    q_total, v_total = folded_last(place, mix_keep, after(mix_got, vectors), 3, (width, width), 4)
    gain1_grad, bias1_grad, gain2_grad, bias2_grad = run(
        vector_kernel, (shape((full,), F32),) * 4, place, vectors, after(other_vectors, q_total), scalars=1, us=0.7)
    return (block_output, input_grad, gain1_grad, bias1_grad, q_total, k_total, v_total, taps_total, out_total,
            gain2_grad, bias2_grad, up_total, down_total)


def solution(mesh):
    both, head = P("seq", "head"), P(None, "head")
    in_specs = (both, P("seq"), P("head", "seq"), P(), P(), head, head, head, head, head, P(), P(), head, head, both)
    out_specs = (both, both, P(), P(), both, both, both, head, both, P(), P(), both, both)
    return jax.shard_map(local, mesh=mesh, in_specs=in_specs, out_specs=out_specs, check_vma=False)
```

```python
import functools

import jax
import jax.numpy as jnp
from jax import lax
from jax.experimental import pallas as pl
from jax.experimental.pallas import tpu as pltpu
from jax.sharding import PartitionSpec as P

NORM_EPS = 1e-05
RATE_CAP = 0.05
LANES = 128
STEP = 64
FAR = float(1 << 20)
GELU_SCALE = 0.7978845608028654
GELU_CUBE = 0.044715
F32 = jnp.float32
BF16 = jnp.bfloat16

NN = (((1,), (0,)), ((), ()))
NT = (((1,), (1,)), ((), ()))
TN = (((0,), (0,)), ((), ()))


def mm(a, b, dims=NN):
    return lax.dot_general(a, b, dims, preferred_element_type=F32)


def shape(dims, kind):
    return pltpu.HBM(dims, kind)


def shape(dims, kind):
    return jax.ShapeDtypeStruct(dims, kind)


FEW = pl.BlockSpec(memory_space=pltpu.SMEM)


def whole(array):
    dims = array.shape
    return pl.BlockSpec(dims, lambda *_: (0,) * len(dims), pipeline_mode=pl.Buffered(1))


def run(body, outs, *ins, scratch=(), scalars=0, grid=(1,), in_specs=None, out_specs=None, mib=16,
        us=1.0, far=()):
    many = isinstance(outs, (tuple, list))
    held = [pltpu.with_memory_space_constraint(x, pltpu.HBM) if i in far else x for i, x in enumerate(ins)]
    if in_specs is None:
        in_specs = [None] * (len(ins) - scalars)
    if out_specs is None:
        out_specs = (None,) * len(outs) if many else None
    in_specs = [spec or whole(x) for spec, x in zip(in_specs, ins[scalars:])]
    pick = lambda spec, x: spec or whole(x)
    out_specs = tuple(map(pick, out_specs, outs)) if many else pick(out_specs, outs)
    return pl.pallas_call(
        body, out_shape=outs, grid=grid, in_specs=[FEW] * scalars + list(in_specs), out_specs=out_specs,
        scratch_shapes=list(scratch), compiler_params=pltpu.CompilerParams(vmem_limit_bytes=mib << 20),
        cost_estimate=pl.CostEstimate(flops=int(us * 1e9), transcendentals=0, bytes_accessed=int(us * 3e6)))(*held)


def after(value, *first):
    return lax.optimization_barrier((value,) + first)[0]


def lanes(width):
    return range(0, width, LANES)


def half_of(ref, h, width):
    return ref.at[:, pl.ds(pl.multiple_of(h * width, LANES), width)]


def digits_of(count):
    digits, stride = [], 1
    while count > 1:
        radix = 4 if count % 4 == 0 else (2 if count % 2 == 0 else count)
        digits.append((stride, radix))
        stride, count = stride * radix, count // radix
    return digits


def turned(array, stride, radix, by):
    pairs = []
    for i in range(lax.axis_size("seq")):
        member = i // stride % radix
        pairs.append((i, i + ((member + by) % radix - member) * stride))
    return lax.ppermute(array, "seq", pairs)


def crossed(array, stride, radix, mask):
    pairs = []
    for i in range(lax.axis_size("seq")):
        member = i // stride % radix
        pairs.append((i, i + ((member ^ mask) - member) * stride))
    return lax.ppermute(array, "seq", pairs)


def swapped(array):
    count = lax.axis_size("head")
    return lax.ppermute(array, "head", [(i, (i + 1) % count) for i in range(count)])


def passed_along(array, by):
    count = lax.axis_size("seq")
    return lax.ppermute(array, "seq", [(i, i + by) for i in range(count) if 0 <= i + by < count])


def member_at(place_ref, stride, radix):
    return lax.rem(lax.div(place_ref[0], stride), radix)


def strides_of(count, z_first=False):
    bits = [1 << k for k in range(count.bit_length() - 1)]
    if z_first and len(bits) > 3:
        x, y, low, high = bits[:4]
        return [(low, high), (x, y), (y, x), (high, low)] + [(b, b) for b in bits[4:]]
    order = []
    for k in range(0, len(bits) - 1, 2):
        order += [(bits[k], bits[k + 1]), (bits[k + 1], bits[k])]
    return order + [(b, b) for b in bits[len(order) :]]


def mirrored(array, at, z_first=False):
    count, cores = lax.axis_size("seq"), lax.axis_size("head")
    strides = strides_of(count, z_first)[at]
    pairs = [(i * cores + h, (i ^ strides[h % 2]) * cores + h) for i in range(count) for h in range(cores)]
    return lax.ppermute(array, ("seq", "head"), pairs)


def pick(place_ref, first, second):
    return jnp.where(place_ref[1] == 0, first, second)


def halved(place_ref, at, count, z_first=False):
    pairs = strides_of(count, z_first)
    lows = []
    for h in range(2):
        left = sorted(set(p[h] for p in pairs) - set(p[h] for p in pairs[:at]))
        lows.append(1 << left.index(pairs[at][h]))
    bit = pick(place_ref, *(lax.rem(lax.div(place_ref[0], stride), 2) for stride in pairs[at]))
    places = []
    for g in range((count >> at) // 2):
        bases = [g // low * 2 * low + g % low for low in lows]
        base, low = pick(place_ref, *bases), pick(place_ref, *lows)
        places.append((base + bit * low, base + (1 - bit) * low))
    return places


def put_halves(place_ref, at, count, total, keep, send, z_first=False):
    for g, (mine, other) in enumerate(halved(place_ref, at, count, z_first)):
        keep[g] = total[mine].astype(BF16)
        send[g] = total[other].astype(BF16)


def put_rows(total, at, grad):
    rows = total.shape[1]
    for s in range(total.shape[0]):
        total[s, :, at : at + grad.shape[1]] = grad[s * rows : (s + 1) * rows].astype(total.dtype)


def half_shapes(entries, rows, width):
    return (shape((entries // 2, rows, width), BF16),) * 2


def grads_kernel(spans, place_ref, *refs):
    lefts, rights, (keep, send), total = refs[: len(spans)], refs[len(spans) : 2 * len(spans)], refs[-3:-1], refs[-1]
    for left, right, at in zip(lefts, rights, spans):
        put_rows(total, at, mm(left[...], right[...], TN))
    put_halves(place_ref, 0, total.shape[0], total, keep, send)


def up_kernel(spans, place_ref, *refs):
    grads_kernel(spans, place_ref, *refs[:4], *refs[6:8], refs[-1])
    refs[8][...] = (refs[4][...] + refs[5][...].astype(F32)).astype(BF16)


def down_kernel(place_ref, grad_ref, hidden_ref, down_ref, resid_ref, keep, send, own_ref, send_ref, total, part):
    part[...] = mm(hidden_ref[...], down_ref[...], NT)
    width = own_ref.shape[1]
    h = place_ref[1]
    own_ref[...] = half_of(part, h, width)[...] + half_of(resid_ref, h, width)[...]
    send_ref[...] = half_of(part, 1 - h, width)[...].astype(BF16)
    put_rows(total, 0, mm(grad_ref[...], hidden_ref[...], TN))
    put_halves(place_ref, 0, total.shape[0], total, keep, send, True)


def fold_kernel(at, count, z_first, place_ref, keep_ref, got_ref, *refs):
    outs, total = refs[:-1], refs[-1]
    for g in range(total.shape[0]):
        total[g] = (keep_ref[g].astype(F32) + got_ref[g].astype(F32)).astype(total.dtype)
    if total.shape[0] > 1:
        put_halves(place_ref, at + 1, count, total, *outs, z_first)
        return
    begin = 0
    for out in outs:
        out[...] = total[0, :, begin : begin + out.shape[1]]
        begin += out.shape[1]


def folded(place, keep, got, at, widths, us, z_first=False):
    entries, rows, width = keep.shape
    outs = half_shapes(entries, rows, width) if entries > 1 else tuple(shape((rows, w), F32) for w in widths)
    return run(functools.partial(fold_kernel, at, lax.axis_size("seq"), z_first), outs, place, keep, got, scalars=1,
               scratch=[pltpu.VMEM((entries, rows, width), BF16 if entries > 1 else F32)], us=us)


def folded_last(place, keep, got, at, widths, us, z_first=False):
    while True:
        res = folded(place, keep, got, at, widths, us, z_first)
        if keep.shape[0] == 1:
            return res
        keep, got, at = res[0], mirrored(res[1], at + 1, z_first), at + 1


def put_messages(place_ref, at, count, total, shared, keep, send):
    rows = total.shape[1]
    places = halved(place_ref, at, count)
    for g, (mine, other) in enumerate(places):
        keep[g * rows : (g + 1) * rows] = total[mine].astype(BF16)
        send[g * rows : (g + 1) * rows] = total[other].astype(BF16)
    end = len(places) * rows
    keep[end:] = shared.astype(BF16)
    send[end:] = shared.astype(BF16)


def message_kernel(at, count, place_ref, keep_ref, got_ref, *refs):
    outs, total = refs[:-1], refs[-1]
    entries, rows, _ = total.shape
    for g in range(entries):
        span = slice(g * rows, (g + 1) * rows)
        total[g] = keep_ref[span].astype(F32) + got_ref[span].astype(F32)
    shared = keep_ref[entries * rows :].astype(F32) + got_ref[entries * rows :].astype(F32)
    if entries > 1:
        put_messages(place_ref, at + 1, count, total, shared, *outs)
        return
    outs[0][...] = total[0]
    outs[1][...] = shared[:STEP]
    outs[2][...] = shared[STEP:]


def folded_message(place, keep, got, at, rows, us):
    depth, width = keep.shape
    extra = STEP + 8
    entries = (depth - extra) // rows
    if entries > 1:
        outs = (shape((entries // 2 * rows + extra, width), BF16),) * 2
    else:
        outs = (shape((rows, width), F32), shape((STEP, width), F32), shape((8, width), F32))
    return run(functools.partial(message_kernel, at, lax.axis_size("seq")), outs, place, keep, got, scalars=1,
               scratch=[pltpu.VMEM((entries, rows, width), F32)], us=us)


def vector_kernel(place_ref, own_ref, other_ref, *outs):
    h = place_ref[1]
    width = own_ref.shape[1]
    own, other = own_ref[...], other_ref[...]
    for k, out in enumerate(outs):
        out[:width] = jnp.where(h == 0, own[k], other[k])
        out[width:] = jnp.where(h == 0, other[k], own[k])


def chained(first, second):
    return first[0] * second[0], second[0] * first[1] + second[1]


def link(stage, reverse, place_ref, messages, before, want_total):
    radix = stage[1]
    member = member_at(place_ref, *stage)
    if reverse:
        member = radix - 1 - member
    rows = messages[0].shape[0] - 16
    pairs = []
    for m in messages:
        whole = m[...].astype(F32)
        pairs.append((whole[rows : rows + 1], whole[:rows]))
    none = (jnp.ones_like(pairs[0][0]), jnp.zeros_like(pairs[0][1]))

    def side(use):
        acc = none
        for by in range(radix - 1, 0, -1):
            kept = use(by)
            part = (jnp.where(kept, pairs[by][0], none[0]), jnp.where(kept, pairs[by][1], none[1]))
            acc = chained(acc, part)
        return acc

    lower = side(lambda by: by <= member)
    before = chained(lower, tuple(b[...] for b in before)) if before else lower
    if not want_total:
        return before, None
    return before, chained(chained(lower, pairs[0]), side(lambda by: by > member))


def link_kernel(stage, reverse, place_ref, *refs):
    messages, held, outs = refs[: stage[1]], refs[stage[1] : -3], refs[-3:]
    before, total = link(stage, reverse, place_ref, messages, held, True)
    outs[0][...], outs[1][...] = before
    rows = outs[1].shape[0]
    outs[2][:rows] = total[1].astype(BF16)
    outs[2][rows:] = jnp.broadcast_to(total[0], (outs[2].shape[0] - rows, total[0].shape[1])).astype(BF16)


def scan_send(message, at, reverse):
    stride, radix = digits_of(lax.axis_size("seq"))[at]
    return [message] + [
        turned(message, stride, radix, (radix - by) if reverse else by) for by in range(1, radix)
    ]


def scan_link(place, got, before, at, reverse):
    stage = digits_of(lax.axis_size("seq"))[at]
    rows, width = got[0].shape
    outs = run(functools.partial(link_kernel, stage, reverse),
               (shape((1, width), F32), shape((rows - 16, width), F32), shape((rows, width), BF16)),
               place, *got, *before, scalars=1, us=8)
    return outs[:2], outs[2]


def split_parts(x, count):
    parts = []
    for _ in range(count):
        low = x.astype(BF16)
        parts.append(low)
        x = x - low.astype(F32)
    return parts


def one_less_exp(x):
    acc = jnp.ones_like(x)
    for k in range(7, 1, -1):
        acc = 1.0 - x * (1.0 / k) * acc
    return x * acc


def side_kernel(starts_ref, decay_ref, lamr_ref, lamc_ref, docr_ref, docc_ref, dist_ref,
                beta_out, first_out, last_out, gate_out, tri, same, wide):
    tok = starts_ref.shape[0]
    heads = decay_ref.shape[0]
    head_pairs = lamc_ref.shape[0] // tok
    width = beta_out.shape[1]
    row = lax.broadcasted_iota(jnp.int32, (tok, tok), 0)
    col = lax.broadcasted_iota(jnp.int32, (tok, tok), 1)
    tri[...] = (col <= row).astype(F32).astype(BF16)
    begins = jnp.broadcast_to(row_of(starts_ref).astype(F32), (LANES, tok)).astype(BF16)
    doc_col = mm(tri[...], begins, NT)
    doc_row = mm(begins[:16], tri[...], NT)[:8]
    docr_ref[...] = doc_row
    docc_ref[...] = doc_col
    wide[...] = jnp.zeros_like(wide)
    wide[:heads] = decay_ref[...]
    lam_col = jnp.zeros((tok, LANES), F32)
    lam_row = jnp.zeros((16, tok), F32)
    for part in split_parts(wide[...], 3):
        lam_col = lam_col + mm(tri[...], part, NT)
        lam_row = lam_row + mm(part[:16], tri[...], NT)
    lamr_ref[...] = jnp.zeros_like(lamr_ref)
    for p in range(head_pairs):
        lamr_ref[8 * p : 8 * p + 2] = lam_row[2 * p : 2 * p + 2]
        lamc_ref[p * tok : (p + 1) * tok] = lam_col if p == 0 else pltpu.roll(lam_col, LANES - 2 * p, 1)
    ones = jnp.ones((tok, LANES), BF16)
    alike = doc_col[:, :1] == doc_row[:1]
    same[...] = jnp.where(alike & (col <= row), 1.0, 0.0).astype(BF16)
    behind = mm(same[...], ones)
    dist_ref[...] = jnp.where(doc_col == 0.0, FAR, behind - 1.0)
    lam_end = lam_col[tok - 1 :]
    doc_end = doc_col[tok - 1 :]
    first = jnp.where(doc_col == 0.0, jnp.exp(-lam_col), 0.0)
    last = jnp.where(doc_col == doc_end, jnp.exp(lam_col - lam_end), 0.0)
    spread = (lax.broadcasted_iota(jnp.int32, (LANES, width), 0)
              == lax.broadcasted_iota(jnp.int32, (LANES, width), 1) // (width // heads))
    spread = spread.astype(F32).astype(BF16)
    for ref, value in ((first_out, first), (last_out, last)):
        parts = split_parts(value, 2)
        ref[...] = mm(parts[0], spread) + mm(parts[1], spread)
    wide[:heads] = jnp.sqrt(one_less_exp(2.0 * jnp.minimum(decay_ref[...], RATE_CAP)))
    eye = (row == col).astype(F32).astype(BF16)
    beta_col = jnp.zeros((tok, LANES), F32)
    for part in split_parts(wide[...], 2):
        beta_col = beta_col + mm(eye, part, NT)
    parts = split_parts(beta_col, 2)
    beta_out[...] = mm(parts[0], spread) + mm(parts[1], spread)
    gate_out[...] = jnp.broadcast_to(first_out[tok - 1 :], gate_out.shape).astype(BF16)


def row_of(ref):
    return ref[...].reshape(1, ref.shape[0])


def norm_rows(rows_in):
    count = rows_in.shape[1]
    center = rows_in - jnp.sum(rows_in, axis=1, keepdims=True) * (1.0 / count)
    spread = jnp.sum(center * center, axis=1, keepdims=True) * (1.0 / count)
    inverse = lax.rsqrt(spread + NORM_EPS)
    return center * inverse, inverse


def norm_back(grad_rows, unit_rows, inverse, gain_vec):
    scale = 1.0 / grad_rows.shape[1]
    scaled = grad_rows * gain_vec
    return inverse * (scaled - jnp.sum(scaled, axis=1, keepdims=True) * scale
                      - unit_rows * (jnp.sum(scaled * unit_rows, axis=1, keepdims=True) * scale))


def by_rows(tok, body, size=256):
    def step(i, carry):
        body(pl.ds(pl.multiple_of(i * size, size), size))
        return carry

    lax.fori_loop(0, tok // size, step, 0)


def in_kernel(place_ref, own_ref, other_ref, gain_ref, bias_ref, wq_ref, wk_ref, wv_ref, docc_ref,
              normed_ref, q_ref, k_ref, v_ref, tail_ref, rows):
    h = place_ref[1]
    tok, width = own_ref.shape
    half_of(rows, h, width)[...] = own_ref[...]
    half_of(rows, 1 - h, width)[...] = other_ref[...]

    def norm(at):
        unit, _ = norm_rows(rows[at].astype(F32))
        normed_ref[at] = (unit * row_of(gain_ref) + row_of(bias_ref)).astype(BF16)

    by_rows(tok, norm)
    normed = normed_ref[...]
    k_ref[...] = mm(normed, wk_ref[...]).astype(BF16)
    keep = docc_ref[tok - STEP :] == docc_ref[tok - 1 :]
    for l in lanes(width):
        tail_ref[:, l : l + LANES] = jnp.where(
            keep, k_ref[tok - STEP :, l : l + LANES].astype(F32), 0.0).astype(BF16)
    q_ref[...] = mm(normed, wq_ref[...]).astype(BF16)
    v_ref[...] = mm(normed, wv_ref[...]).astype(BF16)


def filter_chunk(keys, taps, dist, count, t0):
    def group(a, acc):
        acc = list(acc)
        for b in range(8):
            j = a * 8 + b
            keep = dist >= j.astype(F32)
            for l in range(count):
                x = keys[l, pl.ds(STEP + t0 - a * 8 - b, STEP), :]
                acc[l] = acc[l] + jnp.where(keep, x * taps[l, pl.ds(j, 1), :], 0.0)
        return tuple(acc)

    return lax.fori_loop(0, 8, group, tuple(jnp.zeros((STEP, LANES), F32) for _ in range(count)))


def filter_kernel(k_ref, taps_ref, dist_ref, beta_ref, out_ref, keys, taps):
    tok, width = k_ref.shape
    count = width // LANES
    for l in range(count):
        keys[l, STEP:] = k_ref[:, l * LANES : (l + 1) * LANES].astype(F32)
        taps[l] = taps_ref[:, l * LANES : (l + 1) * LANES].astype(F32)
    out_ref[:STEP] = jnp.zeros((STEP, width), BF16)

    def chunk(c, carry):
        t0 = pl.multiple_of(c * STEP, STEP)
        at = pl.ds(t0, STEP)
        acc = filter_chunk(keys, taps, dist_ref[at], count, t0)
        for l in range(count):
            span = slice(l * LANES, (l + 1) * LANES)
            out_ref[at, span] = (acc[l] * beta_ref[at, span]).astype(BF16)
        return carry

    lax.fori_loop(1, tok // STEP, chunk, 0)


def fold(square, low):
    return jnp.where(low, square[:STEP], square[STEP:])


def unfold(flat, low):
    return jnp.concatenate([jnp.where(low, flat, 0.0), jnp.where(low, 0.0, flat)], axis=0)


def low_lanes(rows):
    return lax.broadcasted_iota(jnp.int32, (rows, LANES), 1) < STEP


def state_kernel(part_ref, tail_ref, k_ref, taps_ref, dist_ref, beta_ref, last_ref, v_ref, gate_ref,
                 sk_ref, message_ref, keys, taps):
    tok, width = part_ref.shape
    count = width // LANES
    for l in range(count):
        span = slice(l * LANES, (l + 1) * LANES)
        keys[l, :STEP] = tail_ref[:, span].astype(F32)
        keys[l, STEP:] = k_ref[:STEP, span].astype(F32)
        taps[l] = taps_ref[:, span].astype(F32)
    sk_ref[...] = part_ref[...]
    acc = filter_chunk(keys, taps, dist_ref[:STEP], count, 0)
    low = low_lanes(STEP)
    for l in range(count):
        span = slice(l * LANES, (l + 1) * LANES)
        sk_ref[:STEP, span] = (acc[l] * beta_ref[:STEP, span]).astype(BF16)
        weighted = (sk_ref[:, span].astype(F32) * last_ref[:, span]).astype(BF16)
        message_ref[:STEP, span] = fold(mm(weighted, v_ref[:, span], TN), low).astype(BF16)
    message_ref[STEP:] = gate_ref[...]


def kept_pairs(docc_ref, docr_ref):
    tok = docc_ref.shape[0]
    order = lax.broadcasted_iota(jnp.int32, (tok, tok), 0) >= lax.broadcasted_iota(jnp.int32, (tok, tok), 1)
    return (docc_ref[:, :1] == docr_ref[:1]) & order


def own_lanes(x, low, e):
    return jnp.where(low if e == 0 else ~low, x.astype(F32), 0.0).astype(BF16)


def decay_of(lamr_ref, lamc_ref, keep, e):
    span = jnp.minimum(lamr_ref[e : e + 1] - lamc_ref[:, e : e + 1], 0.0)
    return jnp.where(keep, jnp.exp(span), 0.0)


def inside_kernel(q_ref, k_ref, v_ref, lamr_ref, lamc_ref, docr_ref, docc_ref, out_ref):
    low = low_lanes(q_ref.shape[0])
    keep = kept_pairs(docc_ref, docr_ref)
    outs = []
    for e in range(2):
        score = mm(own_lanes(q_ref[...], low, e), k_ref[...], NT)
        outs.append(mm((score * decay_of(lamr_ref, lamc_ref, keep, e)).astype(BF16), v_ref[...]))
    out_ref[...] = jnp.where(low, outs[0], outs[1])


def mixed_kernel(stage, place_ref, inside_ref, q_ref, first_ref, *refs):
    (state_ref, mixed_ref) = refs[-2:]
    before, _ = link(stage, False, place_ref, refs[: stage[1]], refs[stage[1] : -2], False)
    state_ref[...] = before[1]
    low = low_lanes(STEP)
    for l in lanes(q_ref.shape[1]):
        span = slice(l, l + LANES)
        square = unfold(state_ref[:, span], low).astype(BF16)
        mixed_ref[:, span] = (0.125 * (inside_ref[:, span] + first_ref[:, span] * mm(q_ref[:, span], square))
                              ).astype(BF16)


def hidden_grad_kernel(place_ref, own_ref, other_ref, down_ref, out_ref, full_ref):
    @pl.when(pl.program_id(0) == 0)
    def _():
        width = own_ref.shape[1]
        half_of(full_ref, place_ref[1], width)[...] = own_ref[...]
        half_of(full_ref, 1 - place_ref[1], width)[...] = other_ref[...]

    out_ref[...] = mm(full_ref[...], down_ref[...]).astype(BF16)


def ffn_kernel(place_ref, own_ref, other_ref, mix_own_ref, mix_other_ref, out_own_ref, out_other_ref, gain_ref,
               bias_ref, up_ref, hg_ref, resid_ref, normed_ref, hidden_ref, pre_ref, part_ref, rows, acc):
    h = place_ref[1]
    step = pl.program_id(0)
    tok, width = own_ref.shape

    @pl.when(step == 0)
    def _():
        half_of(rows, h, width)[...] = own_ref[...]
        half_of(rows, 1 - h, width)[...] = other_ref[...]
        resid_ref[...] = mm(mix_own_ref[...], out_own_ref[...], NT) + mm(mix_other_ref[...], out_other_ref[...], NT)

        def norm(at):
            resid = rows[at].astype(F32) + resid_ref[at]
            resid_ref[at] = resid
            unit, _ = norm_rows(resid)
            normed_ref[at] = (unit * row_of(gain_ref) + row_of(bias_ref)).astype(BF16)

        by_rows(tok, norm)
        acc[...] = jnp.zeros_like(acc)

    pre = mm(normed_ref[...], up_ref[...])
    square = pre * pre
    bent = jnp.tanh(GELU_SCALE * (pre + GELU_CUBE * (square * pre)))
    outer = 0.5 * (1.0 + bent)
    hidden_ref[...] = (pre * outer).astype(BF16)
    slope = outer + 0.5 * pre * (1.0 - bent * bent) * (GELU_SCALE * (1.0 + 3.0 * GELU_CUBE * square))
    pre_ref[...] = (hg_ref[...].astype(F32) * slope).astype(BF16)
    acc[...] += mm(pre_ref[...], up_ref[...], NT)

    @pl.when(step == pl.num_programs(0) - 1)
    def _():
        part_ref[...] = acc[...].astype(BF16)


def norm2_kernel(place_ref, part_ref, got_ref, resid_ref, grad_ref, gain_ref, out_w_ref, q_ref, first_ref,
                 gate_ref, resid_grad_ref, branch_ref, g_ref, sums_ref, message_ref, rows):
    h = place_ref[1]
    tok, width = q_ref.shape
    sums_ref[...] = jnp.zeros_like(sums_ref)

    def norm(at):
        back = part_ref[at].astype(F32) + got_ref[at].astype(F32)
        unit, inverse = norm_rows(resid_ref[at])
        grad = grad_ref[at].astype(F32) + norm_back(back, unit, inverse, row_of(gain_ref))
        rows[at] = grad
        branch_ref[at] = grad.astype(BF16)
        sums_ref[0:1] += jnp.sum(back * unit, axis=0, keepdims=True)
        sums_ref[1:2] += jnp.sum(back, axis=0, keepdims=True)

    by_rows(tok, norm)
    resid_grad_ref[...] = half_of(rows, h, width)[...]
    g_ref[...] = (0.125 * mm(branch_ref[...], out_w_ref[...]).astype(BF16).astype(F32)).astype(BF16)
    low = low_lanes(STEP)
    for l in lanes(width):
        span = slice(l, l + LANES)
        weighted = (q_ref[:, span].astype(F32) * first_ref[:, span]).astype(BF16)
        message_ref[:STEP, span] = fold(mm(weighted, g_ref[:, span], TN), low).astype(BF16)
    message_ref[STEP:] = gate_ref[...]


def back_kernel(q_ref, k_ref, v_ref, g_ref, lamr_ref, lamc_ref, docr_ref, docc_ref, first_ref, state_ref,
                dq_ref, dk_ref, dv_ref):
    low = low_lanes(q_ref.shape[0])
    keep = kept_pairs(docc_ref, docr_ref)
    square = unfold(state_ref[...], low_lanes(STEP)).astype(BF16)
    outs = []
    for e in range(2):
        decay = decay_of(lamr_ref, lamc_ref, keep, e)
        prob = (mm(own_lanes(q_ref[...], low, e), k_ref[...], NT) * decay).astype(BF16)
        score = (mm(own_lanes(g_ref[...], low, e), v_ref[...], NT) * decay).astype(BF16)
        outs.append((mm(score, k_ref[...]), mm(score, q_ref[...], TN), mm(prob, g_ref[...], TN)))
    from_state = first_ref[...] * mm(g_ref[...], square, NT)
    dq_ref[...] = (jnp.where(low, outs[0][0], outs[1][0]) + from_state).astype(BF16)
    dk_ref[...] = jnp.where(low, outs[0][1], outs[1][1])
    dv_ref[...] = jnp.where(low, outs[0][2], outs[1][2])


def filter_back_chunk(sg, keys, taps, ahead, sums, count, s0):
    held = [keys[l, pl.ds(s0, STEP), :] for l in range(count)]

    def group(a, acc):
        acc = list(acc)
        for b in range(8):
            j = a * 8 + b
            keep = ahead > j.astype(F32)
            for l in range(count):
                u = jnp.where(keep, sg[l, pl.ds(s0 + a * 8 + b, STEP), :], 0.0)
                acc[l] = acc[l] + u * taps[l, pl.ds(j, 1), :]
                sums[l, j] += jnp.sum((held[l] * u).reshape(STEP // 8, 8, LANES), axis=0)
        return tuple(acc)

    return lax.fori_loop(0, 8, group, tuple(jnp.zeros((STEP, LANES), F32) for _ in range(count)))


def reach(docr_ref, docc_ref, ahead_ref):
    tok = docc_ref.shape[0]
    order = lax.broadcasted_iota(jnp.int32, (tok, tok), 0) <= lax.broadcasted_iota(jnp.int32, (tok, tok), 1)
    same = jnp.where((docc_ref[:, :1] == docr_ref[:1]) & order, 1.0, 0.0).astype(BF16)
    ahead_ref[STEP:] = mm(same, jnp.ones((tok, LANES), BF16))
    unbroken = jnp.sum(jnp.where(docr_ref[:1] == 0.0, 1.0, 0.0), axis=1, keepdims=True)
    ahead_ref[:STEP] = unbroken + STEP - lax.broadcasted_iota(jnp.int32, (STEP, LANES), 0).astype(F32)


def carry_kernel(stage, place_ref, dk_ref, dv_ref, k_ref, v_ref, last_ref, beta_ref, docr_ref, docc_ref, taps_ref,
                 tail_ref, *refs):
    value_ref, sg_ref, edge_ref, sums, ahead_ref, taps, keys = refs[-7:]
    reach(docr_ref, docc_ref, ahead_ref)
    before, _ = link(stage, True, place_ref, refs[: stage[1]], refs[stage[1] : -7], False)
    state = before[1]
    tok, width = dk_ref.shape
    count = width // LANES
    low = low_lanes(STEP)
    for l in range(count):
        span = slice(l * LANES, (l + 1) * LANES)
        square = unfold(state[:, span], low).astype(BF16)
        last = last_ref[:, span]
        value_ref[:, span] = (dv_ref[:, span] + last * mm(k_ref[:, span], square)).astype(BF16)
        sg_ref[l, :STEP] = jnp.zeros((STEP, LANES), F32)
        sg_ref[l, STEP : STEP + tok] = beta_ref[:, span] * (
            dk_ref[:, span] + last * mm(v_ref[:, span], square, NT))
        sg_ref[l, STEP + tok :] = jnp.zeros((STEP, LANES), F32)
        keys[l] = tail_ref[:, span].astype(F32)
        taps[l] = taps_ref[:, span].astype(F32)
    sums[...] = jnp.zeros_like(sums)
    acc = filter_back_chunk(sg_ref, keys, taps, ahead_ref[:STEP], sums, count, 0)
    for l in range(count):
        edge_ref[:, l * LANES : (l + 1) * LANES] = acc[l].astype(BF16)


def filter_back_kernel(sg_ref, k_ref, ahead_ref, taps_ref, sums_in, grad_ref, taps_grad_ref, keys, taps, sums):
    tok, width = k_ref.shape
    count = width // LANES
    for l in range(count):
        span = slice(l * LANES, (l + 1) * LANES)
        keys[l, STEP:] = k_ref[:, span].astype(F32)
        taps[l] = taps_ref[:, span].astype(F32)
    sums[...] = sums_in[...]

    def chunk(c, carry):
        s0 = pl.multiple_of(c * STEP, STEP)
        acc = filter_back_chunk(sg_ref, keys, taps, ahead_ref[pl.ds(s0, STEP)], sums, count, s0)
        for l in range(count):
            grad_ref[pl.ds(s0 - STEP, STEP), l * LANES : (l + 1) * LANES] = acc[l]
        return carry

    lax.fori_loop(1, tok // STEP + 1, chunk, 0)
    for l in range(count):
        taps_grad_ref[:, l * LANES : (l + 1) * LANES] = jnp.sum(sums[l], axis=1)


def out_kernel(place_ref, grad_ref, edge_ref, docc_ref, dq_ref, dv_ref, wq_ref, wk_ref, wv_ref, own_ref, other_ref,
               key_ref, part_ref, rows, total, sums_ref):
    h = place_ref[1]
    tok, width = own_ref.shape
    keep = docc_ref[tok - STEP :] == docc_ref[tok - 1 :]
    key_ref[: tok - STEP] = grad_ref[: tok - STEP].astype(BF16)
    for l in lanes(width):
        span = slice(l, l + LANES)
        edge = jnp.where(keep, edge_ref[:, span].astype(F32), 0.0)
        key_ref[tok - STEP :, span] = (grad_ref[tok - STEP :, span] + edge).astype(BF16)
    total[...] = (mm(dq_ref[...], wq_ref[...], NT) + mm(dv_ref[...], wv_ref[...], NT)
                  + mm(key_ref[...], wk_ref[...], NT))
    part_ref[:tok] = total[...].astype(BF16)
    half_of(rows, h, width)[...] = own_ref[...]
    half_of(rows, 1 - h, width)[...] = other_ref[...]
    sums_ref[...] = jnp.zeros_like(sums_ref)

    def norm(at):
        unit, _ = norm_rows(rows[at].astype(F32))
        sums_ref[0:1] += jnp.sum(total[at] * unit, axis=0, keepdims=True)
        sums_ref[1:2] += jnp.sum(total[at], axis=0, keepdims=True)

    by_rows(tok, norm)
    part_ref[tok:] = sums_ref[...].astype(BF16)


def key_grads_kernel(place_ref, normed_ref, key_ref, taps_ref, sums2_ref, part_ref, got_ref, keep, send, total, shared):
    put_rows(total, 0, mm(normed_ref[...], key_ref[...], TN))
    tok, width = key_ref.shape
    shared[STEP:] = jnp.zeros_like(shared[STEP:])
    shared[:STEP] = taps_ref[...]
    sums1 = part_ref[tok:].astype(F32) + got_ref[tok:].astype(F32)
    for at, sums in ((STEP, sums1), (STEP + 2, sums2_ref[...])):
        shared[at : at + 2] = jnp.where(place_ref[1] == 0, sums[:2, :width], sums[:2, width:])
    put_messages(place_ref, 0, total.shape[0], total, shared[...], keep, send)


def input_kernel(place_ref, part_ref, got_ref, own_ref, other_ref, gain_ref, resid_grad_ref, out_ref, rows, back):
    h = place_ref[1]
    tok, width = own_ref.shape
    half_of(rows, h, width)[...] = own_ref[...]
    half_of(rows, 1 - h, width)[...] = other_ref[...]

    def norm(at):
        unit, inverse = norm_rows(rows[at].astype(F32))
        grad = part_ref[at].astype(F32) + got_ref[at].astype(F32)
        back[at] = norm_back(grad, unit, inverse, row_of(gain_ref))

    by_rows(tok, norm)
    out_ref[...] = (half_of(back, h, width)[...] + resid_grad_ref[...]).astype(BF16)


def local(block_input, starts, decay_rate, norm1_gain, norm1_bias, q_weight, k_weight, v_weight,
          shift_kernel, out_weight, norm2_gain, norm2_bias, up_weight, down_weight, out_grad):
    tok, width = block_input.shape
    heads = decay_rate.shape[0]
    full = 2 * width
    hidden_width = up_weight.shape[1]
    count = width // LANES
    seqs = lax.axis_size("seq")
    place = jnp.stack([lax.axis_index("seq"), lax.axis_index("head")]).astype(jnp.int32)
    gain1, bias1, gain2, bias2 = norm1_gain, norm1_bias, norm2_gain, norm2_bias
    vm = pltpu.VMEM

    stages = digits_of(seqs)
    other_input = swapped(block_input)
    other_grad = swapped(out_grad)
    other_out = swapped(out_weight)
    lamr, lamc, docr, docc, dist, beta_w, first_w, last_w, gate_w = run(
        side_kernel,
        (shape((8 * count, tok), F32), shape((count * tok, LANES), F32), shape((8, tok), F32),
         shape((tok, LANES), F32), shape((tok, LANES), F32),
         shape((tok, width), F32), shape((tok, width), F32), shape((tok, width), F32), shape((16, width), BF16)),
        starts, decay_rate, far=(0, 1),
        scratch=[vm((tok, tok), BF16), vm((tok, tok), BF16), vm((LANES, tok), F32)], us=2.7)
    other_input = after(other_input, docc)
    normed1, query, key, value, tail = run(
        in_kernel,
        (shape((tok, full), BF16),) + (shape((tok, width), BF16),) * 3 + (shape((STEP, width), BF16),),
        place, block_input, other_input, gain1, bias1, q_weight, k_weight, v_weight, docc,
        scratch=[vm((tok, full), BF16)], scalars=1, us=3.0)
    prev_tail = passed_along(tail, 1)
    scaled_part = run(
        filter_kernel, shape((tok, width), BF16), key, shift_kernel, dist, beta_w,
        scratch=[vm((count, tok + STEP, LANES), F32), vm((count, STEP, LANES), F32)], us=5.4)
    prev_tail = after(prev_tail, scaled_part)
    scaled, message = run(
        state_kernel, (shape((tok, width), BF16), shape((STEP + 16, width), BF16)),
        scaled_part, prev_tail, key, shift_kernel, dist, beta_w, last_w, value, gate_w,
        scratch=[vm((count, 2 * STEP, LANES), F32), vm((count, STEP, LANES), F32)], us=1.7)
    pair_spec = pl.BlockSpec((tok, LANES), lambda p: (0, p))
    lamr_spec = pl.BlockSpec((8, tok), lambda p: (p, 0))
    lamc_spec = pl.BlockSpec((tok, LANES), lambda p: (p, 0))
    state_spec = pl.BlockSpec((STEP, LANES), lambda p: (0, p))
    tile = 512

    before = ()
    got = scan_send(message, 0, False)
    hidden_grad, grad_full = run(
        hidden_grad_kernel, (shape((tok, hidden_width), BF16), shape((tok, full), BF16)),
        place, out_grad, after(other_grad, message), down_weight, scalars=1,
        grid=(hidden_width // tile,), in_specs=[None, None, pl.BlockSpec((full, tile), lambda i: (0, i))],
        out_specs=(pl.BlockSpec((tok, tile), lambda i: (0, i)), None), us=2.5)
    last_got = [after(g, hidden_grad) for g in got]
    for at in range(len(stages) - 1):
        before, message = scan_link(place, last_got, before, at, False)
        last_got = scan_send(message, at + 1, False)
    query_late = after(query, message)
    inside = run(
        inside_kernel, shape((tok, width), F32), query_late, scaled, value, lamr, lamc, docr, docc,
        grid=(count,),
        in_specs=[pair_spec] * 3 + [lamr_spec, lamc_spec, None, None], out_specs=pair_spec, us=3.5)
    last_got = [after(g, inside) for g in last_got]
    state, mixed = run(
        functools.partial(mixed_kernel, stages[-1]), (shape((STEP, width), F32), shape((tok, width), BF16)),
        place, inside, query, first_w, *last_got, *before, scalars=1, us=1.2)
    mixed_other = swapped(mixed)

    wide_tile = pl.BlockSpec((full, tile), lambda i: (0, i))
    tok_tile = pl.BlockSpec((tok, tile), lambda i: (0, i))
    resid, normed2, hidden, pre_grad, part2 = run(
        ffn_kernel,
        (shape((tok, full), F32), shape((tok, full), BF16), shape((tok, hidden_width), BF16),
         shape((tok, hidden_width), BF16), shape((tok, full), BF16)),
        place, block_input, other_input, mixed, mixed_other, out_weight, other_out, gain2, bias2, up_weight, hidden_grad,
        scratch=[vm((tok, full), BF16), vm((tok, full), F32)], scalars=1, mib=24,
        grid=(hidden_width // tile,),
        in_specs=[None] * 8 + [wide_tile, tok_tile],
        out_specs=(None, None, tok_tile, tok_tile, None), us=10.8)
    got2 = swapped(part2)
    rows = full // seqs
    up_width = hidden_width + width
    down_keep, down_send, ffn_own, ffn_send = run(
        down_kernel,
        half_shapes(seqs, rows, hidden_width) + (shape((tok, width), F32), shape((tok, width), BF16)),
        place, grad_full, hidden, down_weight, resid, scalars=1,
        scratch=[vm((seqs, rows, hidden_width), BF16), vm((tok, full), F32)], mib=24, us=2.46)
    ffn_other = swapped(ffn_send)
    got2 = after(got2, ffn_own)
    resid_grad, branch, g_low, sums2, message = run(
        norm2_kernel,
        (shape((tok, width), F32), shape((tok, full), BF16), shape((tok, width), BF16), shape((8, full), F32),
         shape((STEP + 16, width), BF16)),
        place, part2, got2, resid, grad_full, gain2, out_weight, query, first_w, gate_w,
        scratch=[vm((tok, full), F32)], scalars=1, us=2.34)
    before = ()
    got = scan_send(message, 0, True)
    up_keep, up_send, block_output = run(
        functools.partial(up_kernel, (0, hidden_width)),
        half_shapes(seqs, rows, up_width) + (shape((tok, width), BF16),),
        place, after(normed2, message), branch, pre_grad, mixed, ffn_own, ffn_other, scalars=1,
        scratch=[vm((seqs, rows, up_width), BF16)], mib=24, us=1.92)
    got = [after(g, block_output) for g in got]
    for at in range(len(stages) - 1):
        before, message = scan_link(place, got, before, at, True)
        got = scan_send(message, at + 1, True)
    up_got = mirrored(after(up_send, message), 0)
    down_got = mirrored(after(down_send, message), 0, True)
    query_late = after(query, message)
    query_grad, dk_part, dv_part = run(
        back_kernel, (shape((tok, width), BF16), shape((tok, width), F32), shape((tok, width), F32)),
        query_late, scaled, value, g_low, lamr, lamc, docr, docc, first_w, state,
        grid=(count,),
        in_specs=[pair_spec] * 4 + [lamr_spec, lamc_spec, None, None, pair_spec, state_spec],
        out_specs=(pair_spec,) * 3, us=1.28)
    got = [after(g, query_grad) for g in got]
    value_grad, shifted_grad, edge, sums, ahead = run(
        functools.partial(carry_kernel, stages[-1]),
        (shape((tok, width), BF16), shape((count, tok + 2 * STEP, LANES), F32), shape((STEP, width), BF16),
         shape((count, STEP, 8, LANES), F32), shape((tok + STEP, LANES), F32)),
        place, dk_part, dv_part, scaled, value, last_w, beta_w, docr, docc, shift_kernel, prev_tail,
        *got, *before, scalars=1,
        scratch=[vm((count, STEP, LANES), F32), vm((count, STEP, LANES), F32)], us=1.5)
    got_edge = passed_along(edge, -1)
    mix_keep, mix_send = run(
        functools.partial(grads_kernel, (0, width)), half_shapes(seqs, rows, 2 * width),
        place, normed1, normed1, query_grad, after(value_grad, edge), scalars=1,
        scratch=[vm((seqs, rows, 2 * width), BF16)], us=1.14)
    mix_got = mirrored(mix_send, 0)
    up_keep, up_send = folded(place, up_keep, after(up_got, mix_keep), 0, (), 8)
    up_got = mirrored(up_send, 1)
    key_rows, taps_grad = run(
        filter_back_kernel, (shape((tok, width), F32), shape((STEP, width), F32)),
        shifted_grad, key, ahead, shift_kernel, after(sums, up_keep),
        scratch=[vm((count, tok + STEP, LANES), F32), vm((count, STEP, LANES), F32),
                 vm((count, STEP, 8, LANES), F32)], us=7.05)
    key_grad, part1 = run(
        out_kernel, (shape((tok, width), BF16), shape((tok + 8, full), BF16)),
        place, key_rows, after(got_edge, key_rows), docc, query_grad, value_grad, q_weight, k_weight, v_weight,
        block_input, other_input,
        scratch=[vm((tok, full), BF16), vm((tok, full), F32), vm((8, full), F32)], scalars=1, us=2.16)
    got1 = swapped(part1)
    up_keep, up_send = folded(place, up_keep, after(up_got, key_grad), 1, (), 0.5)
    up_got = mirrored(up_send, 2)
    mix_keep, mix_send = folded(place, mix_keep, after(mix_got, up_keep), 0, (), 1)
    mix_got = mirrored(mix_send, 1)
    down_keep, down_send = folded(place, down_keep, after(down_got, mix_keep), 0, (), 1, True)
    down_got = mirrored(down_send, 1, True)
    key_keep, key_send = run(
        key_grads_kernel, (shape((seqs // 2 * rows + STEP + 8, width), BF16),) * 2,
        place, normed1, key_grad, taps_grad, sums2, part1, after(got1, down_keep), scalars=1,
        scratch=[vm((seqs, rows, width), BF16), vm((STEP + 8, width), F32)], us=0.78)
    key_got = mirrored(key_send, 0)
    input_grad = run(
        input_kernel, shape((tok, width), BF16),
        place, part1, after(got1, key_keep), block_input, other_input, gain1, resid_grad, scalars=1,
        scratch=[vm((tok, full), BF16), vm((tok, full), F32)], us=0.89)
    mix_keep, mix_send = folded(place, mix_keep, after(mix_got, input_grad), 1, (), 8)
    mix_got = mirrored(mix_send, 2)
    down_keep, down_send = folded(place, down_keep, after(down_got, mix_keep), 1, (), 1, True)
    down_got = mirrored(down_send, 2, True)
    up_keep, up_send = folded(place, up_keep, after(up_got, down_keep), 2, (), 0.2)
    up_got = mirrored(up_send, 3)
    key_keep, key_send = folded_message(place, key_keep, after(key_got, up_keep), 0, rows, 4)
    key_got = mirrored(key_send, 1)
    down_keep, down_send = folded(place, down_keep, after(down_got, key_keep), 2, (), 4, True)
    down_got = mirrored(down_send, 3, True)
    mix_keep, mix_send = folded(place, mix_keep, after(mix_got, down_keep), 2, (), 4)
    mix_got = mirrored(mix_send, 3)
    key_keep, key_send = folded_message(place, key_keep, after(key_got, mix_keep), 1, rows, 2)
    key_got = mirrored(key_send, 2)
    up_total, out_total = folded_last(place, up_keep, after(up_got, key_keep), 3, (hidden_width, width), 1)
    key_keep, key_send = folded_message(place, key_keep, after(key_got, up_total), 2, rows, 8)
    key_got = mirrored(key_send, 3)
    (down_total,) = folded_last(place, down_keep, after(down_got, key_keep), 3, (hidden_width,), 0.2, True)
    key_got = after(key_got, down_total)
    for at in range(3, len(strides_of(seqs)) - 1):
        key_keep, key_send = folded_message(place, key_keep, key_got, at, rows, 8)
        key_got = mirrored(key_send, at + 1)
    k_total, taps_total, vectors = folded_message(
        place, key_keep, key_got, len(strides_of(seqs)) - 1, rows, 0.5)
    other_vectors = swapped(vectors)
    q_total, v_total = folded_last(place, mix_keep, after(mix_got, vectors), 3, (width, width), 0.5)
    gain1_grad, bias1_grad, gain2_grad, bias2_grad = run(
        vector_kernel, (shape((full,), F32),) * 4, place, vectors, after(other_vectors, q_total), scalars=1, us=0.7)
    return (block_output, input_grad, gain1_grad, bias1_grad, q_total, k_total, v_total, taps_total, out_total,
            gain2_grad, bias2_grad, up_total, down_total)


def solution(mesh):
    both, head = P("seq", "head"), P(None, "head")
    in_specs = (both, P("seq"), P("head", "seq"), P(), P(), head, head, head, head, head, P(), P(), head, head, both)
    out_specs = (both, both, P(), P(), both, both, both, head, both, P(), P(), both, both)
    return jax.shard_map(local, mesh=mesh, in_specs=in_specs, out_specs=out_specs, check_vma=False)
```

```python
import functools

import jax
import jax.numpy as jnp
from jax import lax
from jax.experimental import pallas as pl
from jax.experimental.pallas import tpu as pltpu
from jax.sharding import PartitionSpec as P

NORM_EPS = 1e-05
RATE_CAP = 0.05
LANES = 128
STEP = 64
SPAN = 32
FAR = float(1 << 20)
GELU_SCALE = 0.7978845608028654
GELU_CUBE = 0.044715
F32 = jnp.float32
BF16 = jnp.bfloat16

NN = (((1,), (0,)), ((), ()))
NT = (((1,), (1,)), ((), ()))
TN = (((0,), (0,)), ((), ()))


def mm(a, b, dims=NN):
    return lax.dot_general(a, b, dims, preferred_element_type=F32)


def shape(dims, kind):
    return pltpu.HBM(dims, kind)


def shape(dims, kind):
    return jax.ShapeDtypeStruct(dims, kind)


FEW = pl.BlockSpec(memory_space=pltpu.SMEM)


def whole(array):
    dims = array.shape
    return pl.BlockSpec(dims, lambda *_: (0,) * len(dims), pipeline_mode=pl.Buffered(1))


def run(body, outs, *ins, scratch=(), scalars=0, grid=(1,), in_specs=None, out_specs=None, mib=16,
        us=1.0, far=()):
    many = isinstance(outs, (tuple, list))
    held = [pltpu.with_memory_space_constraint(x, pltpu.HBM) if i in far else x for i, x in enumerate(ins)]
    if in_specs is None:
        in_specs = [None] * (len(ins) - scalars)
    if out_specs is None:
        out_specs = (None,) * len(outs) if many else None
    in_specs = [spec or whole(x) for spec, x in zip(in_specs, ins[scalars:])]
    pick = lambda spec, x: spec or whole(x)
    out_specs = tuple(map(pick, out_specs, outs)) if many else pick(out_specs, outs)
    return pl.pallas_call(
        body, out_shape=outs, grid=grid, in_specs=[FEW] * scalars + list(in_specs), out_specs=out_specs,
        scratch_shapes=list(scratch), compiler_params=pltpu.CompilerParams(vmem_limit_bytes=mib << 20),
        cost_estimate=pl.CostEstimate(flops=int(us * 1e9), transcendentals=0, bytes_accessed=int(us * 3e6)))(*held)


def after(value, *first):
    return lax.optimization_barrier((value,) + first)[0]


def lanes(width):
    return range(0, width, LANES)


def half_of(ref, h, width):
    return ref.at[:, pl.ds(pl.multiple_of(h * width, LANES), width)]


def digits_of(count):
    digits, stride = [], 1
    while count > 1:
        radix = 4 if count % 4 == 0 else (2 if count % 2 == 0 else count)
        digits.append((stride, radix))
        stride, count = stride * radix, count // radix
    return digits


def turned(array, stride, radix, by):
    pairs = []
    for i in range(lax.axis_size("seq")):
        member = i // stride % radix
        pairs.append((i, i + ((member + by) % radix - member) * stride))
    return lax.ppermute(array, "seq", pairs)


def crossed(array, stride, radix, mask):
    pairs = []
    for i in range(lax.axis_size("seq")):
        member = i // stride % radix
        pairs.append((i, i + ((member ^ mask) - member) * stride))
    return lax.ppermute(array, "seq", pairs)


def swapped(array):
    count = lax.axis_size("head")
    return lax.ppermute(array, "head", [(i, (i + 1) % count) for i in range(count)])


def passed_along(array, by):
    count = lax.axis_size("seq")
    return lax.ppermute(array, "seq", [(i, i + by) for i in range(count) if 0 <= i + by < count])


def member_at(place_ref, stride, radix):
    return lax.rem(lax.div(place_ref[0], stride), radix)


def strides_of(count, z_first=False):
    bits = [1 << k for k in range(count.bit_length() - 1)]
    if z_first and len(bits) > 3:
        x, y, low, high = bits[:4]
        return [(low, high), (x, y), (y, x), (high, low)] + [(b, b) for b in bits[4:]]
    order = []
    for k in range(0, len(bits) - 1, 2):
        order += [(bits[k], bits[k + 1]), (bits[k + 1], bits[k])]
    return order + [(b, b) for b in bits[len(order) :]]


def mirrored(array, at, z_first=False):
    count, cores = lax.axis_size("seq"), lax.axis_size("head")
    strides = strides_of(count, z_first)[at]
    pairs = [(i * cores + h, (i ^ strides[h % 2]) * cores + h) for i in range(count) for h in range(cores)]
    return lax.ppermute(array, ("seq", "head"), pairs)


def pick(place_ref, first, second):
    return jnp.where(place_ref[1] == 0, first, second)


def halved(place_ref, at, count, z_first=False):
    pairs = strides_of(count, z_first)
    lows = []
    for h in range(2):
        left = sorted(set(p[h] for p in pairs) - set(p[h] for p in pairs[:at]))
        lows.append(1 << left.index(pairs[at][h]))
    bit = pick(place_ref, *(lax.rem(lax.div(place_ref[0], stride), 2) for stride in pairs[at]))
    places = []
    for g in range((count >> at) // 2):
        bases = [g // low * 2 * low + g % low for low in lows]
        base, low = pick(place_ref, *bases), pick(place_ref, *lows)
        places.append((base + bit * low, base + (1 - bit) * low))
    return places


def put_halves(place_ref, at, count, total, keep, send, z_first=False):
    for g, (mine, other) in enumerate(halved(place_ref, at, count, z_first)):
        keep[g] = total[mine].astype(BF16)
        send[g] = total[other].astype(BF16)


def put_rows(total, at, grad):
    rows = total.shape[1]
    for s in range(total.shape[0]):
        total[s, :, at : at + grad.shape[1]] = grad[s * rows : (s + 1) * rows].astype(total.dtype)


def half_shapes(entries, rows, width):
    return (shape((entries // 2, rows, width), BF16),) * 2


def grads_kernel(spans, place_ref, *refs):
    lefts, rights, (keep, send), total = refs[: len(spans)], refs[len(spans) : 2 * len(spans)], refs[-3:-1], refs[-1]
    for left, right, at in zip(lefts, rights, spans):
        put_rows(total, at, mm(left[...], right[...], TN))
    put_halves(place_ref, 0, total.shape[0], total, keep, send)


def up_kernel(spans, place_ref, *refs):
    grads_kernel(spans, place_ref, *refs[:4], *refs[6:8], refs[-1])
    refs[8][...] = (refs[4][...] + refs[5][...].astype(F32)).astype(BF16)


def down_kernel(place_ref, grad_ref, hidden_ref, down_ref, resid_ref, keep, send, own_ref, send_ref, total, part):
    part[...] = mm(hidden_ref[...], down_ref[...], NT)
    width = own_ref.shape[1]
    h = place_ref[1]
    own_ref[...] = half_of(part, h, width)[...] + half_of(resid_ref, h, width)[...]
    send_ref[...] = half_of(part, 1 - h, width)[...].astype(BF16)
    put_rows(total, 0, mm(grad_ref[...], hidden_ref[...], TN))
    put_halves(place_ref, 0, total.shape[0], total, keep, send, True)


def fold_kernel(at, count, z_first, place_ref, keep_ref, got_ref, *refs):
    outs, total = refs[:-1], refs[-1]
    for g in range(total.shape[0]):
        total[g] = (keep_ref[g].astype(F32) + got_ref[g].astype(F32)).astype(total.dtype)
    if total.shape[0] > 1:
        put_halves(place_ref, at + 1, count, total, *outs, z_first)
        return
    begin = 0
    for out in outs:
        out[...] = total[0, :, begin : begin + out.shape[1]]
        begin += out.shape[1]


def folded(place, keep, got, at, widths, us, z_first=False):
    entries, rows, width = keep.shape
    outs = half_shapes(entries, rows, width) if entries > 1 else tuple(shape((rows, w), F32) for w in widths)
    return run(functools.partial(fold_kernel, at, lax.axis_size("seq"), z_first), outs, place, keep, got, scalars=1,
               scratch=[pltpu.VMEM((entries, rows, width), BF16 if entries > 1 else F32)], us=us)


def folded_last(place, keep, got, at, widths, us, z_first=False):
    while True:
        res = folded(place, keep, got, at, widths, us, z_first)
        if keep.shape[0] == 1:
            return res
        keep, got, at = res[0], mirrored(res[1], at + 1, z_first), at + 1


def put_messages(place_ref, at, count, total, shared, keep, send):
    rows = total.shape[1]
    places = halved(place_ref, at, count)
    for g, (mine, other) in enumerate(places):
        keep[g * rows : (g + 1) * rows] = total[mine].astype(BF16)
        send[g * rows : (g + 1) * rows] = total[other].astype(BF16)
    end = len(places) * rows
    keep[end:] = shared.astype(BF16)
    send[end:] = shared.astype(BF16)


def message_kernel(at, count, place_ref, keep_ref, got_ref, *refs):
    outs, total = refs[:-1], refs[-1]
    entries, rows, _ = total.shape
    for g in range(entries):
        span = slice(g * rows, (g + 1) * rows)
        total[g] = keep_ref[span].astype(F32) + got_ref[span].astype(F32)
    shared = keep_ref[entries * rows :].astype(F32) + got_ref[entries * rows :].astype(F32)
    if entries > 1:
        put_messages(place_ref, at + 1, count, total, shared, *outs)
        return
    outs[0][...] = total[0]
    outs[1][...] = shared[:STEP]
    outs[2][...] = shared[STEP:]


def folded_message(place, keep, got, at, rows, us):
    depth, width = keep.shape
    extra = STEP + 8
    entries = (depth - extra) // rows
    if entries > 1:
        outs = (shape((entries // 2 * rows + extra, width), BF16),) * 2
    else:
        outs = (shape((rows, width), F32), shape((STEP, width), F32), shape((8, width), F32))
    return run(functools.partial(message_kernel, at, lax.axis_size("seq")), outs, place, keep, got, scalars=1,
               scratch=[pltpu.VMEM((entries, rows, width), F32)], us=us)


def vector_kernel(place_ref, own_ref, other_ref, *outs):
    h = place_ref[1]
    width = own_ref.shape[1]
    own, other = own_ref[...], other_ref[...]
    for k, out in enumerate(outs):
        out[:width] = jnp.where(h == 0, own[k], other[k])
        out[width:] = jnp.where(h == 0, other[k], own[k])


def chained(first, second):
    return first[0] * second[0], second[0] * first[1] + second[1]


def link(stage, reverse, place_ref, messages, before, want_total):
    radix = stage[1]
    member = member_at(place_ref, *stage)
    if reverse:
        member = radix - 1 - member
    rows = messages[0].shape[0] - 16
    pairs = []
    for m in messages:
        whole = m[...].astype(F32)
        pairs.append((whole[rows : rows + 1], whole[:rows]))
    none = (jnp.ones_like(pairs[0][0]), jnp.zeros_like(pairs[0][1]))

    def side(use):
        acc = none
        for by in range(radix - 1, 0, -1):
            kept = use(by)
            part = (jnp.where(kept, pairs[by][0], none[0]), jnp.where(kept, pairs[by][1], none[1]))
            acc = chained(acc, part)
        return acc

    lower = side(lambda by: by <= member)
    before = chained(lower, tuple(b[...] for b in before)) if before else lower
    if not want_total:
        return before, None
    return before, chained(chained(lower, pairs[0]), side(lambda by: by > member))


def link_kernel(stage, reverse, place_ref, *refs):
    messages, held, outs = refs[: stage[1]], refs[stage[1] : -3], refs[-3:]
    before, total = link(stage, reverse, place_ref, messages, held, True)
    outs[0][...], outs[1][...] = before
    rows = outs[1].shape[0]
    outs[2][:rows] = total[1].astype(BF16)
    outs[2][rows:] = jnp.broadcast_to(total[0], (outs[2].shape[0] - rows, total[0].shape[1])).astype(BF16)


def scan_send(message, at, reverse):
    stride, radix = digits_of(lax.axis_size("seq"))[at]
    return [message] + [
        turned(message, stride, radix, (radix - by) if reverse else by) for by in range(1, radix)
    ]


def scan_link(place, got, before, at, reverse):
    stage = digits_of(lax.axis_size("seq"))[at]
    rows, width = got[0].shape
    outs = run(functools.partial(link_kernel, stage, reverse),
               (shape((1, width), F32), shape((rows - 16, width), F32), shape((rows, width), BF16)),
               place, *got, *before, scalars=1, us=8)
    return outs[:2], outs[2]


def split_parts(x, count):
    parts = []
    for _ in range(count):
        low = x.astype(BF16)
        parts.append(low)
        x = x - low.astype(F32)
    return parts


def one_less_exp(x):
    acc = jnp.ones_like(x)
    for k in range(7, 1, -1):
        acc = 1.0 - x * (1.0 / k) * acc
    return x * acc


def side_kernel(starts_ref, decay_ref, lamr_ref, lamc_ref, docr_ref, docc_ref, dist_ref,
                beta_out, first_out, last_out, gate_out, tri, same, wide):
    tok = starts_ref.shape[0]
    heads = decay_ref.shape[0]
    head_pairs = lamc_ref.shape[0] // tok
    width = beta_out.shape[1]
    row = lax.broadcasted_iota(jnp.int32, (tok, tok), 0)
    col = lax.broadcasted_iota(jnp.int32, (tok, tok), 1)
    tri[...] = (col <= row).astype(F32).astype(BF16)
    begins = jnp.broadcast_to(row_of(starts_ref).astype(F32), (LANES, tok)).astype(BF16)
    doc_col = mm(tri[...], begins, NT)
    doc_row = mm(begins[:16], tri[...], NT)[:8]
    docr_ref[...] = doc_row
    docc_ref[...] = doc_col
    wide[...] = jnp.zeros_like(wide)
    wide[:heads] = decay_ref[...]
    lam_col = jnp.zeros((tok, LANES), F32)
    lam_row = jnp.zeros((16, tok), F32)
    for part in split_parts(wide[...], 3):
        lam_col = lam_col + mm(tri[...], part, NT)
        lam_row = lam_row + mm(part[:16], tri[...], NT)
    lamr_ref[...] = jnp.zeros_like(lamr_ref)
    for p in range(head_pairs):
        lamr_ref[8 * p : 8 * p + 2] = lam_row[2 * p : 2 * p + 2]
        lamc_ref[p * tok : (p + 1) * tok] = lam_col if p == 0 else pltpu.roll(lam_col, LANES - 2 * p, 1)
    ones = jnp.ones((tok, LANES), BF16)
    alike = doc_col[:, :1] == doc_row[:1]
    same[...] = jnp.where(alike & (col <= row), 1.0, 0.0).astype(BF16)
    behind = mm(same[...], ones)
    dist_ref[...] = jnp.where(doc_col == 0.0, FAR, behind - 1.0)
    lam_end = lam_col[tok - 1 :]
    doc_end = doc_col[tok - 1 :]
    first = jnp.where(doc_col == 0.0, jnp.exp(-lam_col), 0.0)
    last = jnp.where(doc_col == doc_end, jnp.exp(lam_col - lam_end), 0.0)
    spread = (lax.broadcasted_iota(jnp.int32, (LANES, width), 0)
              == lax.broadcasted_iota(jnp.int32, (LANES, width), 1) // (width // heads))
    spread = spread.astype(F32).astype(BF16)
    for ref, value in ((first_out, first), (last_out, last)):
        parts = split_parts(value, 2)
        ref[...] = mm(parts[0], spread) + mm(parts[1], spread)
    wide[:heads] = jnp.sqrt(one_less_exp(2.0 * jnp.minimum(decay_ref[...], RATE_CAP)))
    eye = (row == col).astype(F32).astype(BF16)
    beta_col = jnp.zeros((tok, LANES), F32)
    for part in split_parts(wide[...], 2):
        beta_col = beta_col + mm(eye, part, NT)
    parts = split_parts(beta_col, 2)
    beta_out[...] = mm(parts[0], spread) + mm(parts[1], spread)
    gate_out[...] = jnp.broadcast_to(first_out[tok - 1 :], gate_out.shape).astype(BF16)


def row_of(ref):
    return ref[...].reshape(1, ref.shape[0])


def norm_rows(rows_in):
    count = rows_in.shape[1]
    center = rows_in - jnp.sum(rows_in, axis=1, keepdims=True) * (1.0 / count)
    spread = jnp.sum(center * center, axis=1, keepdims=True) * (1.0 / count)
    inverse = lax.rsqrt(spread + NORM_EPS)
    return center * inverse, inverse


def norm_back(grad_rows, unit_rows, inverse, gain_vec):
    scale = 1.0 / grad_rows.shape[1]
    scaled = grad_rows * gain_vec
    return inverse * (scaled - jnp.sum(scaled, axis=1, keepdims=True) * scale
                      - unit_rows * (jnp.sum(scaled * unit_rows, axis=1, keepdims=True) * scale))


def by_rows(tok, body, size=512):
    def step(i, carry):
        body(pl.ds(pl.multiple_of(i * size, size), size))
        return carry

    lax.fori_loop(0, tok // size, step, 0)


def in_kernel(place_ref, own_ref, other_ref, gain_ref, bias_ref, wq_ref, wk_ref, wv_ref, docc_ref,
              normed_ref, q_ref, k_ref, v_ref, tail_ref, rows):
    h = place_ref[1]
    tok, width = own_ref.shape
    half_of(rows, h, width)[...] = own_ref[...]
    half_of(rows, 1 - h, width)[...] = other_ref[...]

    def norm(at):
        unit, _ = norm_rows(rows[at].astype(F32))
        normed_ref[at] = (unit * row_of(gain_ref) + row_of(bias_ref)).astype(BF16)

    by_rows(tok, norm)
    normed = normed_ref[...]
    k_ref[...] = mm(normed, wk_ref[...]).astype(BF16)
    keep = docc_ref[tok - STEP :] == docc_ref[tok - 1 :]
    for l in lanes(width):
        tail_ref[:, l : l + LANES] = jnp.where(
            keep, k_ref[tok - STEP :, l : l + LANES].astype(F32), 0.0).astype(BF16)
    q_ref[...] = mm(normed, wq_ref[...]).astype(BF16)
    v_ref[...] = mm(normed, wv_ref[...]).astype(BF16)


def filter_chunk(keys, taps, dist, count, t0):
    def group(a, acc):
        acc = list(acc)
        for b in range(32):
            j = a * 32 + b
            keep = dist >= j.astype(F32)
            for l in range(count):
                x = keys[l, pl.ds(STEP + t0 - a * 32 - b, STEP), :]
                acc[l] = acc[l] + jnp.where(keep, x * taps[l, pl.ds(j, 1), :], 0.0)
        return tuple(acc)

    return lax.fori_loop(0, STEP // 32, group, tuple(jnp.zeros((STEP, LANES), F32) for _ in range(count)))


def filter_kernel(k_ref, taps_ref, dist_ref, beta_ref, out_ref, keys, taps):
    tok, width = k_ref.shape
    count = width // LANES
    for l in range(count):
        keys[l, STEP:] = k_ref[:, l * LANES : (l + 1) * LANES].astype(F32)
        taps[l] = taps_ref[:, l * LANES : (l + 1) * LANES].astype(F32)
    out_ref[:STEP] = jnp.zeros((STEP, width), BF16)

    def chunk(c, carry):
        t0 = pl.multiple_of(c * STEP, STEP)
        at = pl.ds(t0, STEP)
        acc = filter_chunk(keys, taps, dist_ref[at], count, t0)
        for l in range(count):
            span = slice(l * LANES, (l + 1) * LANES)
            out_ref[at, span] = (acc[l] * beta_ref[at, span]).astype(BF16)
        return carry

    lax.fori_loop(1, tok // STEP, chunk, 0)


def fold(square, low):
    return jnp.where(low, square[:STEP], square[STEP:])


def unfold(flat, low):
    return jnp.concatenate([jnp.where(low, flat, 0.0), jnp.where(low, 0.0, flat)], axis=0)


def low_lanes(rows):
    return lax.broadcasted_iota(jnp.int32, (rows, LANES), 1) < STEP


def state_kernel(part_ref, tail_ref, k_ref, taps_ref, dist_ref, beta_ref, last_ref, v_ref, gate_ref,
                 sk_ref, message_ref, keys, taps):
    tok, width = part_ref.shape
    count = width // LANES
    for l in range(count):
        span = slice(l * LANES, (l + 1) * LANES)
        keys[l, :STEP] = tail_ref[:, span].astype(F32)
        keys[l, STEP:] = k_ref[:STEP, span].astype(F32)
        taps[l] = taps_ref[:, span].astype(F32)
    sk_ref[...] = part_ref[...]
    acc = filter_chunk(keys, taps, dist_ref[:STEP], count, 0)
    low = low_lanes(STEP)
    for l in range(count):
        span = slice(l * LANES, (l + 1) * LANES)
        sk_ref[:STEP, span] = (acc[l] * beta_ref[:STEP, span]).astype(BF16)
        weighted = (sk_ref[:, span].astype(F32) * last_ref[:, span]).astype(BF16)
        message_ref[:STEP, span] = fold(mm(weighted, v_ref[:, span], TN), low).astype(BF16)
    message_ref[STEP:] = gate_ref[...]


def kept_pairs(docc_ref, docr_ref):
    tok = docc_ref.shape[0]
    order = lax.broadcasted_iota(jnp.int32, (tok, tok), 0) >= lax.broadcasted_iota(jnp.int32, (tok, tok), 1)
    return (docc_ref[:, :1] == docr_ref[:1]) & order


def own_lanes(x, low, e):
    return jnp.where(low if e == 0 else ~low, x.astype(F32), 0.0).astype(BF16)


def decay_of(lamr_ref, lamc_ref, keep, e):
    span = jnp.minimum(lamr_ref[e : e + 1] - lamc_ref[:, e : e + 1], 0.0)
    return jnp.where(keep, jnp.exp(span), 0.0)


def inside_kernel(q_ref, k_ref, v_ref, lamr_ref, lamc_ref, docr_ref, docc_ref, out_ref):
    low = low_lanes(q_ref.shape[0])
    keep = kept_pairs(docc_ref, docr_ref)
    outs = []
    for e in range(2):
        score = mm(own_lanes(q_ref[...], low, e), k_ref[...], NT)
        outs.append(mm((score * decay_of(lamr_ref, lamc_ref, keep, e)).astype(BF16), v_ref[...]))
    out_ref[...] = jnp.where(low, outs[0], outs[1])


def mixed_kernel(stage, place_ref, inside_ref, q_ref, first_ref, *refs):
    (state_ref, mixed_ref) = refs[-2:]
    before, _ = link(stage, False, place_ref, refs[: stage[1]], refs[stage[1] : -2], False)
    state_ref[...] = before[1]
    low = low_lanes(STEP)
    for l in lanes(q_ref.shape[1]):
        span = slice(l, l + LANES)
        square = unfold(state_ref[:, span], low).astype(BF16)
        mixed_ref[:, span] = (0.125 * (inside_ref[:, span] + first_ref[:, span] * mm(q_ref[:, span], square))
                              ).astype(BF16)


def hidden_grad_kernel(place_ref, own_ref, other_ref, down_ref, out_ref, full_ref):
    @pl.when(pl.program_id(0) == 0)
    def _():
        width = own_ref.shape[1]
        half_of(full_ref, place_ref[1], width)[...] = own_ref[...]
        half_of(full_ref, 1 - place_ref[1], width)[...] = other_ref[...]

    out_ref[...] = mm(full_ref[...], down_ref[...]).astype(BF16)


def ffn_kernel(place_ref, own_ref, other_ref, mix_own_ref, mix_other_ref, out_own_ref, out_other_ref, gain_ref,
               bias_ref, up_ref, hg_ref, resid_ref, normed_ref, hidden_ref, pre_ref, part_ref, rows, acc):
    h = place_ref[1]
    step = pl.program_id(0)
    tok, width = own_ref.shape

    @pl.when(step == 0)
    def _():
        half_of(rows, h, width)[...] = own_ref[...]
        half_of(rows, 1 - h, width)[...] = other_ref[...]
        resid_ref[...] = mm(mix_own_ref[...], out_own_ref[...], NT) + mm(mix_other_ref[...], out_other_ref[...], NT)

        def norm(at):
            resid = rows[at].astype(F32) + resid_ref[at]
            resid_ref[at] = resid
            unit, _ = norm_rows(resid)
            normed_ref[at] = (unit * row_of(gain_ref) + row_of(bias_ref)).astype(BF16)

        by_rows(tok, norm)
        acc[...] = jnp.zeros_like(acc)

    pre = mm(normed_ref[...], up_ref[...])
    square = pre * pre
    bent = jnp.tanh(GELU_SCALE * (pre + GELU_CUBE * (square * pre)))
    outer = 0.5 * (1.0 + bent)
    hidden_ref[...] = (pre * outer).astype(BF16)
    slope = outer + 0.5 * pre * (1.0 - bent * bent) * (GELU_SCALE * (1.0 + 3.0 * GELU_CUBE * square))
    pre_ref[...] = (hg_ref[...].astype(F32) * slope).astype(BF16)
    acc[...] += mm(pre_ref[...], up_ref[...], NT)

    @pl.when(step == pl.num_programs(0) - 1)
    def _():
        part_ref[...] = acc[...].astype(BF16)


def norm2_kernel(place_ref, part_ref, got_ref, resid_ref, grad_ref, gain_ref, out_w_ref, q_ref, first_ref,
                 gate_ref, resid_grad_ref, branch_ref, g_ref, sums_ref, message_ref, rows):
    h = place_ref[1]
    tok, width = q_ref.shape
    sums_ref[...] = jnp.zeros_like(sums_ref)

    def norm(at):
        back = part_ref[at].astype(F32) + got_ref[at].astype(F32)
        unit, inverse = norm_rows(resid_ref[at])
        grad = grad_ref[at].astype(F32) + norm_back(back, unit, inverse, row_of(gain_ref))
        rows[at] = grad
        branch_ref[at] = grad.astype(BF16)
        sums_ref[0:1] += jnp.sum(back * unit, axis=0, keepdims=True)
        sums_ref[1:2] += jnp.sum(back, axis=0, keepdims=True)

    by_rows(tok, norm)
    resid_grad_ref[...] = half_of(rows, h, width)[...]
    g_ref[...] = (0.125 * mm(branch_ref[...], out_w_ref[...]).astype(BF16).astype(F32)).astype(BF16)
    low = low_lanes(STEP)
    for l in lanes(width):
        span = slice(l, l + LANES)
        weighted = (q_ref[:, span].astype(F32) * first_ref[:, span]).astype(BF16)
        message_ref[:STEP, span] = fold(mm(weighted, g_ref[:, span], TN), low).astype(BF16)
    message_ref[STEP:] = gate_ref[...]


def back_kernel(q_ref, k_ref, v_ref, g_ref, lamr_ref, lamc_ref, docr_ref, docc_ref, first_ref, state_ref,
                dq_ref, dk_ref, dv_ref):
    low = low_lanes(q_ref.shape[0])
    keep = kept_pairs(docc_ref, docr_ref)
    square = unfold(state_ref[...], low_lanes(STEP)).astype(BF16)
    outs = []
    for e in range(2):
        decay = decay_of(lamr_ref, lamc_ref, keep, e)
        prob = (mm(own_lanes(q_ref[...], low, e), k_ref[...], NT) * decay).astype(BF16)
        score = (mm(own_lanes(g_ref[...], low, e), v_ref[...], NT) * decay).astype(BF16)
        outs.append((mm(score, k_ref[...]), mm(score, q_ref[...], TN), mm(prob, g_ref[...], TN)))
    from_state = first_ref[...] * mm(g_ref[...], square, NT)
    dq_ref[...] = (jnp.where(low, outs[0][0], outs[1][0]) + from_state).astype(BF16)
    dk_ref[...] = jnp.where(low, outs[0][1], outs[1][1])
    dv_ref[...] = jnp.where(low, outs[0][2], outs[1][2])


def filter_back_chunk(sg, keys, taps, ahead, sums, count, s0):
    held = [keys[l, pl.ds(s0, SPAN), :] for l in range(count)]

    def group(a, acc):
        acc = list(acc)
        for b in range(16):
            j = a * 16 + b
            keep = ahead > j.astype(F32)
            for l in range(count):
                u = jnp.where(keep, sg[l, pl.ds(s0 + a * 16 + b, SPAN), :], 0.0)
                acc[l] = acc[l] + u * taps[l, pl.ds(j, 1), :]
                sums[l, j] += jnp.sum((held[l] * u).reshape(SPAN // 8, 8, LANES), axis=0)
        return tuple(acc)

    return lax.fori_loop(0, STEP // 16, group, tuple(jnp.zeros((SPAN, LANES), F32) for _ in range(count)))


def reach(docr_ref, docc_ref, ahead_ref):
    tok = docc_ref.shape[0]
    order = lax.broadcasted_iota(jnp.int32, (tok, tok), 0) <= lax.broadcasted_iota(jnp.int32, (tok, tok), 1)
    same = jnp.where((docc_ref[:, :1] == docr_ref[:1]) & order, 1.0, 0.0).astype(BF16)
    ahead_ref[STEP:] = mm(same, jnp.ones((tok, LANES), BF16))
    unbroken = jnp.sum(jnp.where(docr_ref[:1] == 0.0, 1.0, 0.0), axis=1, keepdims=True)
    ahead_ref[:STEP] = unbroken + STEP - lax.broadcasted_iota(jnp.int32, (STEP, LANES), 0).astype(F32)


def carry_kernel(stage, place_ref, dk_ref, dv_ref, k_ref, v_ref, last_ref, beta_ref, docr_ref, docc_ref, taps_ref,
                 tail_ref, *refs):
    value_ref, sg_ref, edge_ref, sums, ahead_ref, taps, keys = refs[-7:]
    reach(docr_ref, docc_ref, ahead_ref)
    before, _ = link(stage, True, place_ref, refs[: stage[1]], refs[stage[1] : -7], False)
    state = before[1]
    tok, width = dk_ref.shape
    count = width // LANES
    low = low_lanes(STEP)
    for l in range(count):
        span = slice(l * LANES, (l + 1) * LANES)
        square = unfold(state[:, span], low).astype(BF16)
        last = last_ref[:, span]
        value_ref[:, span] = (dv_ref[:, span] + last * mm(k_ref[:, span], square)).astype(BF16)
        sg_ref[l, :STEP] = jnp.zeros((STEP, LANES), F32)
        sg_ref[l, STEP : STEP + tok] = beta_ref[:, span] * (
            dk_ref[:, span] + last * mm(v_ref[:, span], square, NT))
        sg_ref[l, STEP + tok :] = jnp.zeros((STEP, LANES), F32)
        keys[l] = tail_ref[:, span].astype(F32)
        taps[l] = taps_ref[:, span].astype(F32)
    sums[...] = jnp.zeros_like(sums)
    for s0 in range(0, STEP, SPAN):
        at = slice(s0, s0 + SPAN)
        acc = filter_back_chunk(sg_ref, keys, taps, ahead_ref[at], sums, count, s0)
        for l in range(count):
            edge_ref[at, l * LANES : (l + 1) * LANES] = acc[l].astype(BF16)


def filter_back_kernel(sg_ref, k_ref, ahead_ref, taps_ref, sums_in, grad_ref, taps_grad_ref, keys, taps, sums):
    tok, width = k_ref.shape
    count = width // LANES
    for l in range(count):
        span = slice(l * LANES, (l + 1) * LANES)
        keys[l, STEP:] = k_ref[:, span].astype(F32)
        taps[l] = taps_ref[:, span].astype(F32)
    sums[...] = sums_in[...]

    def chunk(c, carry):
        s0 = pl.multiple_of(c * SPAN, SPAN)
        acc = filter_back_chunk(sg_ref, keys, taps, ahead_ref[pl.ds(s0, SPAN)], sums, count, s0)
        for l in range(count):
            grad_ref[pl.ds(s0 - STEP, SPAN), l * LANES : (l + 1) * LANES] = acc[l]
        return carry

    lax.fori_loop(STEP // SPAN, (tok + STEP) // SPAN, chunk, 0)
    for l in range(count):
        taps_grad_ref[:, l * LANES : (l + 1) * LANES] = jnp.sum(sums[l], axis=1)


def out_kernel(place_ref, grad_ref, edge_ref, docc_ref, dq_ref, dv_ref, wq_ref, wk_ref, wv_ref, own_ref, other_ref,
               key_ref, part_ref, rows, total, sums_ref):
    h = place_ref[1]
    tok, width = own_ref.shape
    keep = docc_ref[tok - STEP :] == docc_ref[tok - 1 :]
    key_ref[: tok - STEP] = grad_ref[: tok - STEP].astype(BF16)
    for l in lanes(width):
        span = slice(l, l + LANES)
        edge = jnp.where(keep, edge_ref[:, span].astype(F32), 0.0)
        key_ref[tok - STEP :, span] = (grad_ref[tok - STEP :, span] + edge).astype(BF16)
    total[...] = (mm(dq_ref[...], wq_ref[...], NT) + mm(dv_ref[...], wv_ref[...], NT)
                  + mm(key_ref[...], wk_ref[...], NT))
    part_ref[:tok] = total[...].astype(BF16)
    half_of(rows, h, width)[...] = own_ref[...]
    half_of(rows, 1 - h, width)[...] = other_ref[...]
    sums_ref[...] = jnp.zeros_like(sums_ref)

    def norm(at):
        unit, _ = norm_rows(rows[at].astype(F32))
        sums_ref[0:1] += jnp.sum(total[at] * unit, axis=0, keepdims=True)
        sums_ref[1:2] += jnp.sum(total[at], axis=0, keepdims=True)

    by_rows(tok, norm)
    part_ref[tok:] = sums_ref[...].astype(BF16)


def key_grads_kernel(place_ref, normed_ref, key_ref, taps_ref, sums2_ref, part_ref, got_ref, keep, send, total, shared):
    put_rows(total, 0, mm(normed_ref[...], key_ref[...], TN))
    tok, width = key_ref.shape
    shared[STEP:] = jnp.zeros_like(shared[STEP:])
    shared[:STEP] = taps_ref[...]
    sums1 = part_ref[tok:].astype(F32) + got_ref[tok:].astype(F32)
    for at, sums in ((STEP, sums1), (STEP + 2, sums2_ref[...])):
        shared[at : at + 2] = jnp.where(place_ref[1] == 0, sums[:2, :width], sums[:2, width:])
    put_messages(place_ref, 0, total.shape[0], total, shared[...], keep, send)


def input_kernel(place_ref, part_ref, got_ref, own_ref, other_ref, gain_ref, resid_grad_ref, out_ref, rows, back):
    h = place_ref[1]
    tok, width = own_ref.shape
    half_of(rows, h, width)[...] = own_ref[...]
    half_of(rows, 1 - h, width)[...] = other_ref[...]

    def norm(at):
        unit, inverse = norm_rows(rows[at].astype(F32))
        grad = part_ref[at].astype(F32) + got_ref[at].astype(F32)
        back[at] = norm_back(grad, unit, inverse, row_of(gain_ref))

    by_rows(tok, norm)
    out_ref[...] = (half_of(back, h, width)[...] + resid_grad_ref[...]).astype(BF16)


def local(block_input, starts, decay_rate, norm1_gain, norm1_bias, q_weight, k_weight, v_weight,
          shift_kernel, out_weight, norm2_gain, norm2_bias, up_weight, down_weight, out_grad):
    tok, width = block_input.shape
    heads = decay_rate.shape[0]
    full = 2 * width
    hidden_width = up_weight.shape[1]
    count = width // LANES
    seqs = lax.axis_size("seq")
    place = jnp.stack([lax.axis_index("seq"), lax.axis_index("head")]).astype(jnp.int32)
    gain1, bias1, gain2, bias2 = norm1_gain, norm1_bias, norm2_gain, norm2_bias
    vm = pltpu.VMEM

    stages = digits_of(seqs)
    other_input = swapped(block_input)
    other_grad = swapped(out_grad)
    other_out = swapped(out_weight)
    lamr, lamc, docr, docc, dist, beta_w, first_w, last_w, gate_w = run(
        side_kernel,
        (shape((8 * count, tok), F32), shape((count * tok, LANES), F32), shape((8, tok), F32),
         shape((tok, LANES), F32), shape((tok, LANES), F32),
         shape((tok, width), F32), shape((tok, width), F32), shape((tok, width), F32), shape((16, width), BF16)),
        starts, decay_rate, far=(0, 1),
        scratch=[vm((tok, tok), BF16), vm((tok, tok), BF16), vm((LANES, tok), F32)], us=2.7)
    other_input = after(other_input, docc)
    normed1, query, key, value, tail = run(
        in_kernel,
        (shape((tok, full), BF16),) + (shape((tok, width), BF16),) * 3 + (shape((STEP, width), BF16),),
        place, block_input, other_input, gain1, bias1, q_weight, k_weight, v_weight, docc,
        scratch=[vm((tok, full), BF16)], scalars=1, us=3.0)
    prev_tail = passed_along(tail, 1)
    scaled_part = run(
        filter_kernel, shape((tok, width), BF16), key, shift_kernel, dist, beta_w,
        scratch=[vm((count, tok + STEP, LANES), F32), vm((count, STEP, LANES), F32)], us=5.4)
    prev_tail = after(prev_tail, scaled_part)
    scaled, message = run(
        state_kernel, (shape((tok, width), BF16), shape((STEP + 16, width), BF16)),
        scaled_part, prev_tail, key, shift_kernel, dist, beta_w, last_w, value, gate_w,
        scratch=[vm((count, 2 * STEP, LANES), F32), vm((count, STEP, LANES), F32)], us=1.7)
    pair_spec = pl.BlockSpec((tok, LANES), lambda p: (0, p))
    lamr_spec = pl.BlockSpec((8, tok), lambda p: (p, 0))
    lamc_spec = pl.BlockSpec((tok, LANES), lambda p: (p, 0))
    state_spec = pl.BlockSpec((STEP, LANES), lambda p: (0, p))
    tile = 512

    before = ()
    got = scan_send(message, 0, False)
    hidden_grad, grad_full = run(
        hidden_grad_kernel, (shape((tok, hidden_width), BF16), shape((tok, full), BF16)),
        place, out_grad, after(other_grad, message), down_weight, scalars=1,
        grid=(hidden_width // tile,), in_specs=[None, None, pl.BlockSpec((full, tile), lambda i: (0, i))],
        out_specs=(pl.BlockSpec((tok, tile), lambda i: (0, i)), None), us=2.5)
    last_got = [after(g, hidden_grad) for g in got]
    for at in range(len(stages) - 1):
        before, message = scan_link(place, last_got, before, at, False)
        last_got = scan_send(message, at + 1, False)
    query_late = after(query, message)
    inside = run(
        inside_kernel, shape((tok, width), F32), query_late, scaled, value, lamr, lamc, docr, docc,
        grid=(count,),
        in_specs=[pair_spec] * 3 + [lamr_spec, lamc_spec, None, None], out_specs=pair_spec, us=3.5)
    last_got = [after(g, inside) for g in last_got]
    state, mixed = run(
        functools.partial(mixed_kernel, stages[-1]), (shape((STEP, width), F32), shape((tok, width), BF16)),
        place, inside, query, first_w, *last_got, *before, scalars=1, us=1.2)
    mixed_other = swapped(mixed)

    wide_tile = pl.BlockSpec((full, tile), lambda i: (0, i))
    tok_tile = pl.BlockSpec((tok, tile), lambda i: (0, i))
    resid, normed2, hidden, pre_grad, part2 = run(
        ffn_kernel,
        (shape((tok, full), F32), shape((tok, full), BF16), shape((tok, hidden_width), BF16),
         shape((tok, hidden_width), BF16), shape((tok, full), BF16)),
        place, block_input, other_input, mixed, mixed_other, out_weight, other_out, gain2, bias2, up_weight, hidden_grad,
        scratch=[vm((tok, full), BF16), vm((tok, full), F32)], scalars=1, mib=24,
        grid=(hidden_width // tile,),
        in_specs=[None] * 8 + [wide_tile, tok_tile],
        out_specs=(None, None, tok_tile, tok_tile, None), us=10.8)
    got2 = swapped(part2)
    rows = full // seqs
    up_width = hidden_width + width
    down_keep, down_send, ffn_own, ffn_send = run(
        down_kernel,
        half_shapes(seqs, rows, hidden_width) + (shape((tok, width), F32), shape((tok, width), BF16)),
        place, grad_full, hidden, down_weight, resid, scalars=1,
        scratch=[vm((seqs, rows, hidden_width), BF16), vm((tok, full), F32)], mib=24, us=2.46)
    ffn_other = swapped(ffn_send)
    got2 = after(got2, ffn_own)
    resid_grad, branch, g_low, sums2, message = run(
        norm2_kernel,
        (shape((tok, width), F32), shape((tok, full), BF16), shape((tok, width), BF16), shape((8, full), F32),
         shape((STEP + 16, width), BF16)),
        place, part2, got2, resid, grad_full, gain2, out_weight, query, first_w, gate_w,
        scratch=[vm((tok, full), F32)], scalars=1, us=2.34)
    before = ()
    got = scan_send(message, 0, True)
    up_keep, up_send, block_output = run(
        functools.partial(up_kernel, (0, hidden_width)),
        half_shapes(seqs, rows, up_width) + (shape((tok, width), BF16),),
        place, after(normed2, message), branch, pre_grad, mixed, ffn_own, ffn_other, scalars=1,
        scratch=[vm((seqs, rows, up_width), BF16)], mib=24, us=1.92)
    got = [after(g, block_output) for g in got]
    for at in range(len(stages) - 1):
        before, message = scan_link(place, got, before, at, True)
        got = scan_send(message, at + 1, True)
    up_got = mirrored(after(up_send, message), 0)
    down_got = mirrored(after(down_send, message), 0, True)
    query_late = after(query, message)
    query_grad, dk_part, dv_part = run(
        back_kernel, (shape((tok, width), BF16), shape((tok, width), F32), shape((tok, width), F32)),
        query_late, scaled, value, g_low, lamr, lamc, docr, docc, first_w, state,
        grid=(count,),
        in_specs=[pair_spec] * 4 + [lamr_spec, lamc_spec, None, None, pair_spec, state_spec],
        out_specs=(pair_spec,) * 3, us=1.28)
    got = [after(g, query_grad) for g in got]
    value_grad, shifted_grad, edge, sums, ahead = run(
        functools.partial(carry_kernel, stages[-1]),
        (shape((tok, width), BF16), shape((count, tok + 2 * STEP, LANES), F32), shape((STEP, width), BF16),
         shape((count, STEP, 8, LANES), F32), shape((tok + STEP, LANES), F32)),
        place, dk_part, dv_part, scaled, value, last_w, beta_w, docr, docc, shift_kernel, prev_tail,
        *got, *before, scalars=1,
        scratch=[vm((count, STEP, LANES), F32), vm((count, STEP, LANES), F32)], us=1.5)
    got_edge = passed_along(edge, -1)
    mix_keep, mix_send = run(
        functools.partial(grads_kernel, (0, width)), half_shapes(seqs, rows, 2 * width),
        place, normed1, normed1, query_grad, after(value_grad, edge), scalars=1,
        scratch=[vm((seqs, rows, 2 * width), BF16)], us=1.14)
    mix_got = mirrored(mix_send, 0)
    up_keep, up_send = folded(place, up_keep, after(up_got, mix_keep), 0, (), 8)
    up_got = mirrored(up_send, 1)
    key_rows, taps_grad = run(
        filter_back_kernel, (shape((tok, width), F32), shape((STEP, width), F32)),
        shifted_grad, key, ahead, shift_kernel, after(sums, up_keep),
        scratch=[vm((count, tok + STEP, LANES), F32), vm((count, STEP, LANES), F32),
                 vm((count, STEP, 8, LANES), F32)], us=7.05)
    key_grad, part1 = run(
        out_kernel, (shape((tok, width), BF16), shape((tok + 8, full), BF16)),
        place, key_rows, after(got_edge, key_rows), docc, query_grad, value_grad, q_weight, k_weight, v_weight,
        block_input, other_input,
        scratch=[vm((tok, full), BF16), vm((tok, full), F32), vm((8, full), F32)], scalars=1, us=2.16)
    got1 = swapped(part1)
    up_keep, up_send = folded(place, up_keep, after(up_got, key_grad), 1, (), 0.5)
    up_got = mirrored(up_send, 2)
    mix_keep, mix_send = folded(place, mix_keep, after(mix_got, up_keep), 0, (), 1)
    mix_got = mirrored(mix_send, 1)
    down_keep, down_send = folded(place, down_keep, after(down_got, mix_keep), 0, (), 1, True)
    down_got = mirrored(down_send, 1, True)
    key_keep, key_send = run(
        key_grads_kernel, (shape((seqs // 2 * rows + STEP + 8, width), BF16),) * 2,
        place, normed1, key_grad, taps_grad, sums2, part1, after(got1, down_keep), scalars=1,
        scratch=[vm((seqs, rows, width), BF16), vm((STEP + 8, width), F32)], us=0.78)
    key_got = mirrored(key_send, 0)
    input_grad = run(
        input_kernel, shape((tok, width), BF16),
        place, part1, after(got1, key_keep), block_input, other_input, gain1, resid_grad, scalars=1,
        scratch=[vm((tok, full), BF16), vm((tok, full), F32)], us=0.89)
    mix_keep, mix_send = folded(place, mix_keep, after(mix_got, input_grad), 1, (), 8)
    mix_got = mirrored(mix_send, 2)
    down_keep, down_send = folded(place, down_keep, after(down_got, mix_keep), 1, (), 1, True)
    down_got = mirrored(down_send, 2, True)
    up_keep, up_send = folded(place, up_keep, after(up_got, down_keep), 2, (), 0.2)
    up_got = mirrored(up_send, 3)
    key_keep, key_send = folded_message(place, key_keep, after(key_got, up_keep), 0, rows, 4)
    key_got = mirrored(key_send, 1)
    down_keep, down_send = folded(place, down_keep, after(down_got, key_keep), 2, (), 4, True)
    down_got = mirrored(down_send, 3, True)
    mix_keep, mix_send = folded(place, mix_keep, after(mix_got, down_keep), 2, (), 4)
    mix_got = mirrored(mix_send, 3)
    key_keep, key_send = folded_message(place, key_keep, after(key_got, mix_keep), 1, rows, 2)
    key_got = mirrored(key_send, 2)
    up_total, out_total = folded_last(place, up_keep, after(up_got, key_keep), 3, (hidden_width, width), 1)
    key_keep, key_send = folded_message(place, key_keep, after(key_got, up_total), 2, rows, 8)
    key_got = mirrored(key_send, 3)
    (down_total,) = folded_last(place, down_keep, after(down_got, key_keep), 3, (hidden_width,), 0.2, True)
    key_got = after(key_got, down_total)
    for at in range(3, len(strides_of(seqs)) - 1):
        key_keep, key_send = folded_message(place, key_keep, key_got, at, rows, 8)
        key_got = mirrored(key_send, at + 1)
    k_total, taps_total, vectors = folded_message(
        place, key_keep, key_got, len(strides_of(seqs)) - 1, rows, 0.5)
    other_vectors = swapped(vectors)
    q_total, v_total = folded_last(place, mix_keep, after(mix_got, vectors), 3, (width, width), 0.5)
    gain1_grad, bias1_grad, gain2_grad, bias2_grad = run(
        vector_kernel, (shape((full,), F32),) * 4, place, vectors, after(other_vectors, q_total), scalars=1, us=0.7)
    return (block_output, input_grad, gain1_grad, bias1_grad, q_total, k_total, v_total, taps_total, out_total,
            gain2_grad, bias2_grad, up_total, down_total)


def solution(mesh):
    both, head = P("seq", "head"), P(None, "head")
    in_specs = (both, P("seq"), P("head", "seq"), P(), P(), head, head, head, head, head, P(), P(), head, head, both)
    out_specs = (both, both, P(), P(), both, both, both, head, both, P(), P(), both, both)
    return jax.shard_map(local, mesh=mesh, in_specs=in_specs, out_specs=out_specs, check_vma=False)
```

```python
import functools

import jax
import jax.numpy as jnp
from jax import lax
from jax.experimental import pallas as pl
from jax.experimental.pallas import tpu as pltpu
from jax.sharding import PartitionSpec as P

NORM_EPS = 1e-05
RATE_CAP = 0.05
LANES = 128
STEP = 64
SPAN = 32
FAR = float(1 << 20)
GELU_SCALE = 0.7978845608028654
GELU_CUBE = 0.044715
F32 = jnp.float32
BF16 = jnp.bfloat16

NN = (((1,), (0,)), ((), ()))
NT = (((1,), (1,)), ((), ()))
TN = (((0,), (0,)), ((), ()))


def mm(a, b, dims=NN):
    return lax.dot_general(a, b, dims, preferred_element_type=F32)


def shape(dims, kind):
    return pltpu.HBM(dims, kind)


def shape(dims, kind):
    return jax.ShapeDtypeStruct(dims, kind)


FEW = pl.BlockSpec(memory_space=pltpu.SMEM)


def whole(array):
    dims = array.shape
    return pl.BlockSpec(dims, lambda *_: (0,) * len(dims), pipeline_mode=pl.Buffered(1))


def run(body, outs, *ins, scratch=(), scalars=0, grid=(1,), in_specs=None, out_specs=None, mib=16,
        us=1.0, far=()):
    many = isinstance(outs, (tuple, list))
    held = [pltpu.with_memory_space_constraint(x, pltpu.HBM) if i in far else x for i, x in enumerate(ins)]
    if in_specs is None:
        in_specs = [None] * (len(ins) - scalars)
    if out_specs is None:
        out_specs = (None,) * len(outs) if many else None
    in_specs = [spec or whole(x) for spec, x in zip(in_specs, ins[scalars:])]
    pick = lambda spec, x: spec or whole(x)
    out_specs = tuple(map(pick, out_specs, outs)) if many else pick(out_specs, outs)
    return pl.pallas_call(
        body, out_shape=outs, grid=grid, in_specs=[FEW] * scalars + list(in_specs), out_specs=out_specs,
        scratch_shapes=list(scratch), compiler_params=pltpu.CompilerParams(vmem_limit_bytes=mib << 20),
        cost_estimate=pl.CostEstimate(flops=int(us * 1e9), transcendentals=0, bytes_accessed=int(us * 3e6)))(*held)


def after(value, *first):
    return lax.optimization_barrier((value,) + first)[0]


def lanes(width):
    return range(0, width, LANES)


def half_of(ref, h, width):
    return ref.at[:, pl.ds(pl.multiple_of(h * width, LANES), width)]


def digits_of(count):
    digits, stride = [], 1
    while count > 1:
        radix = 4 if count % 4 == 0 else (2 if count % 2 == 0 else count)
        digits.append((stride, radix))
        stride, count = stride * radix, count // radix
    return digits


def turned(array, stride, radix, by):
    pairs = []
    for i in range(lax.axis_size("seq")):
        member = i // stride % radix
        pairs.append((i, i + ((member + by) % radix - member) * stride))
    return lax.ppermute(array, "seq", pairs)


def crossed(array, stride, radix, mask):
    pairs = []
    for i in range(lax.axis_size("seq")):
        member = i // stride % radix
        pairs.append((i, i + ((member ^ mask) - member) * stride))
    return lax.ppermute(array, "seq", pairs)


def swapped(array):
    count = lax.axis_size("head")
    return lax.ppermute(array, "head", [(i, (i + 1) % count) for i in range(count)])


def passed_along(array, by):
    count = lax.axis_size("seq")
    return lax.ppermute(array, "seq", [(i, i + by) for i in range(count) if 0 <= i + by < count])


def member_at(place_ref, stride, radix):
    return lax.rem(lax.div(place_ref[0], stride), radix)


def strides_of(count, z_first=False):
    bits = [1 << k for k in range(count.bit_length() - 1)]
    if z_first and len(bits) > 3:
        x, y, low, high = bits[:4]
        return [(low, high), (x, y), (y, x), (high, low)] + [(b, b) for b in bits[4:]]
    order = []
    for k in range(0, len(bits) - 1, 2):
        order += [(bits[k], bits[k + 1]), (bits[k + 1], bits[k])]
    return order + [(b, b) for b in bits[len(order) :]]


def mirrored(array, at, z_first=False):
    count, cores = lax.axis_size("seq"), lax.axis_size("head")
    strides = strides_of(count, z_first)[at]
    pairs = [(i * cores + h, (i ^ strides[h % 2]) * cores + h) for i in range(count) for h in range(cores)]
    return lax.ppermute(array, ("seq", "head"), pairs)


def pick(place_ref, first, second):
    return jnp.where(place_ref[1] == 0, first, second)


def halved(place_ref, at, count, z_first=False):
    pairs = strides_of(count, z_first)
    lows = []
    for h in range(2):
        left = sorted(set(p[h] for p in pairs) - set(p[h] for p in pairs[:at]))
        lows.append(1 << left.index(pairs[at][h]))
    bit = pick(place_ref, *(lax.rem(lax.div(place_ref[0], stride), 2) for stride in pairs[at]))
    places = []
    for g in range((count >> at) // 2):
        bases = [g // low * 2 * low + g % low for low in lows]
        base, low = pick(place_ref, *bases), pick(place_ref, *lows)
        places.append((base + bit * low, base + (1 - bit) * low))
    return places


def put_halves(place_ref, at, count, total, keep, send, z_first=False):
    for g, (mine, other) in enumerate(halved(place_ref, at, count, z_first)):
        keep[g] = total[mine].astype(BF16)
        send[g] = total[other].astype(BF16)


def put_rows(total, at, grad):
    rows = total.shape[1]
    for s in range(total.shape[0]):
        total[s, :, at : at + grad.shape[1]] = grad[s * rows : (s + 1) * rows].astype(total.dtype)


def half_shapes(entries, rows, width):
    return (shape((entries // 2, rows, width), BF16),) * 2


def grads_kernel(spans, place_ref, *refs):
    lefts, rights, (keep, send), total = refs[: len(spans)], refs[len(spans) : 2 * len(spans)], refs[-3:-1], refs[-1]
    for left, right, at in zip(lefts, rights, spans):
        put_rows(total, at, mm(left[...], right[...], TN))
    put_halves(place_ref, 0, total.shape[0], total, keep, send)


def up_kernel(spans, place_ref, *refs):
    grads_kernel(spans, place_ref, *refs[:4], *refs[6:8], refs[-1])
    refs[8][...] = (refs[4][...] + refs[5][...].astype(F32)).astype(BF16)


def down_kernel(place_ref, grad_ref, hidden_ref, down_ref, resid_ref, keep, send, own_ref, send_ref, total, part):
    part[...] = mm(hidden_ref[...], down_ref[...], NT)
    width = own_ref.shape[1]
    h = place_ref[1]
    own_ref[...] = half_of(part, h, width)[...] + half_of(resid_ref, h, width)[...]
    send_ref[...] = half_of(part, 1 - h, width)[...].astype(BF16)
    put_rows(total, 0, mm(grad_ref[...], hidden_ref[...], TN))
    put_halves(place_ref, 0, total.shape[0], total, keep, send, True)


def fold_kernel(at, count, z_first, place_ref, keep_ref, got_ref, *refs):
    outs, total = refs[:-1], refs[-1]
    for g in range(total.shape[0]):
        total[g] = (keep_ref[g].astype(F32) + got_ref[g].astype(F32)).astype(total.dtype)
    if total.shape[0] > 1:
        put_halves(place_ref, at + 1, count, total, *outs, z_first)
        return
    begin = 0
    for out in outs:
        out[...] = total[0, :, begin : begin + out.shape[1]]
        begin += out.shape[1]


def folded(place, keep, got, at, widths, us, z_first=False):
    entries, rows, width = keep.shape
    outs = half_shapes(entries, rows, width) if entries > 1 else tuple(shape((rows, w), F32) for w in widths)
    return run(functools.partial(fold_kernel, at, lax.axis_size("seq"), z_first), outs, place, keep, got, scalars=1,
               scratch=[pltpu.VMEM((entries, rows, width), BF16 if entries > 1 else F32)], us=us)


def folded_last(place, keep, got, at, widths, us, z_first=False):
    while True:
        res = folded(place, keep, got, at, widths, us, z_first)
        if keep.shape[0] == 1:
            return res
        keep, got, at = res[0], mirrored(res[1], at + 1, z_first), at + 1


def put_messages(place_ref, at, count, total, shared, keep, send):
    rows = total.shape[1]
    places = halved(place_ref, at, count)
    for g, (mine, other) in enumerate(places):
        keep[g * rows : (g + 1) * rows] = total[mine].astype(BF16)
        send[g * rows : (g + 1) * rows] = total[other].astype(BF16)
    end = len(places) * rows
    keep[end:] = shared.astype(BF16)
    send[end:] = shared.astype(BF16)


def message_kernel(at, count, place_ref, keep_ref, got_ref, *refs):
    outs, total = refs[:-1], refs[-1]
    entries, rows, _ = total.shape
    for g in range(entries):
        span = slice(g * rows, (g + 1) * rows)
        total[g] = keep_ref[span].astype(F32) + got_ref[span].astype(F32)
    shared = keep_ref[entries * rows :].astype(F32) + got_ref[entries * rows :].astype(F32)
    if entries > 1:
        put_messages(place_ref, at + 1, count, total, shared, *outs)
        return
    outs[0][...] = total[0]
    outs[1][...] = shared[:STEP]
    outs[2][...] = shared[STEP:]


def folded_message(place, keep, got, at, rows, us):
    depth, width = keep.shape
    extra = STEP + 8
    entries = (depth - extra) // rows
    if entries > 1:
        outs = (shape((entries // 2 * rows + extra, width), BF16),) * 2
    else:
        outs = (shape((rows, width), F32), shape((STEP, width), F32), shape((8, width), F32))
    return run(functools.partial(message_kernel, at, lax.axis_size("seq")), outs, place, keep, got, scalars=1,
               scratch=[pltpu.VMEM((entries, rows, width), F32)], us=us)


def end_kernel(widths, place_ref, keep_ref, got_ref, own_ref, other_ref, *outs):
    begin = 0
    for out, width in zip(outs, widths):
        span = slice(begin, begin + width)
        out[...] = keep_ref[0, :, span].astype(F32) + got_ref[0, :, span].astype(F32)
        begin += width
    h = place_ref[1]
    own, other = own_ref[...], other_ref[...]
    width = own.shape[1]
    for k, out in enumerate(outs[len(widths) :]):
        out[:width] = jnp.where(h == 0, own[k], other[k])
        out[width:] = jnp.where(h == 0, other[k], own[k])


def chained(first, second):
    return first[0] * second[0], second[0] * first[1] + second[1]


def link(stage, reverse, place_ref, messages, before, want_total):
    radix = stage[1]
    member = member_at(place_ref, *stage)
    if reverse:
        member = radix - 1 - member
    rows = messages[0].shape[0] - 16
    pairs = []
    for m in messages:
        whole = m[...].astype(F32)
        pairs.append((whole[rows : rows + 1], whole[:rows]))
    none = (jnp.ones_like(pairs[0][0]), jnp.zeros_like(pairs[0][1]))

    def side(use):
        acc = none
        for by in range(radix - 1, 0, -1):
            kept = use(by)
            part = (jnp.where(kept, pairs[by][0], none[0]), jnp.where(kept, pairs[by][1], none[1]))
            acc = chained(acc, part)
        return acc

    lower = side(lambda by: by <= member)
    before = chained(lower, tuple(b[...] for b in before)) if before else lower
    if not want_total:
        return before, None
    return before, chained(chained(lower, pairs[0]), side(lambda by: by > member))


def link_kernel(stage, reverse, place_ref, *refs):
    messages, held, outs = refs[: stage[1]], refs[stage[1] : -3], refs[-3:]
    before, total = link(stage, reverse, place_ref, messages, held, True)
    outs[0][...], outs[1][...] = before
    rows = outs[1].shape[0]
    outs[2][:rows] = total[1].astype(BF16)
    outs[2][rows:] = jnp.broadcast_to(total[0], (outs[2].shape[0] - rows, total[0].shape[1])).astype(BF16)


def scan_send(message, at, reverse):
    stride, radix = digits_of(lax.axis_size("seq"))[at]
    return [message] + [
        turned(message, stride, radix, (radix - by) if reverse else by) for by in range(1, radix)
    ]


def scan_link(place, got, before, at, reverse):
    stage = digits_of(lax.axis_size("seq"))[at]
    rows, width = got[0].shape
    outs = run(functools.partial(link_kernel, stage, reverse),
               (shape((1, width), F32), shape((rows - 16, width), F32), shape((rows, width), BF16)),
               place, *got, *before, scalars=1, us=8)
    return outs[:2], outs[2]


def split_parts(x, count):
    parts = []
    for _ in range(count):
        low = x.astype(BF16)
        parts.append(low)
        x = x - low.astype(F32)
    return parts


def one_less_exp(x):
    acc = jnp.ones_like(x)
    for k in range(7, 1, -1):
        acc = 1.0 - x * (1.0 / k) * acc
    return x * acc


def side_kernel(starts_ref, decay_ref, lamr_ref, lamc_ref, docr_ref, docc_ref, dist_ref,
                beta_out, first_out, last_out, gate_out, tri, same, wide):
    tok = starts_ref.shape[0]
    heads = decay_ref.shape[0]
    head_pairs = lamc_ref.shape[0] // tok
    width = beta_out.shape[1]
    row = lax.broadcasted_iota(jnp.int32, (tok, tok), 0)
    col = lax.broadcasted_iota(jnp.int32, (tok, tok), 1)
    tri[...] = (col <= row).astype(F32).astype(BF16)
    begins = jnp.broadcast_to(row_of(starts_ref).astype(F32), (LANES, tok)).astype(BF16)
    doc_col = mm(tri[...], begins, NT)
    doc_row = mm(begins[:16], tri[...], NT)[:8]
    docr_ref[...] = doc_row
    docc_ref[...] = doc_col
    wide[...] = jnp.zeros_like(wide)
    wide[:heads] = decay_ref[...]
    lam_col = jnp.zeros((tok, LANES), F32)
    lam_row = jnp.zeros((16, tok), F32)
    for part in split_parts(wide[...], 2):
        lam_col = lam_col + mm(tri[...], part, NT)
        lam_row = lam_row + mm(part[:16], tri[...], NT)
    lamr_ref[...] = jnp.zeros_like(lamr_ref)
    for p in range(head_pairs):
        lamr_ref[8 * p : 8 * p + 2] = lam_row[2 * p : 2 * p + 2]
        lamc_ref[p * tok : (p + 1) * tok] = lam_col if p == 0 else pltpu.roll(lam_col, LANES - 2 * p, 1)
    ones = jnp.ones((tok, LANES), BF16)
    alike = doc_col[:, :1] == doc_row[:1]
    same[...] = jnp.where(alike & (col <= row), 1.0, 0.0).astype(BF16)
    behind = mm(same[...], ones)
    dist_ref[...] = jnp.where(doc_col == 0.0, FAR, behind - 1.0)
    lam_end = lam_col[tok - 1 :]
    doc_end = doc_col[tok - 1 :]
    first = jnp.where(doc_col == 0.0, jnp.exp(-lam_col), 0.0)
    last = jnp.where(doc_col == doc_end, jnp.exp(lam_col - lam_end), 0.0)
    spread = (lax.broadcasted_iota(jnp.int32, (LANES, width), 0)
              == lax.broadcasted_iota(jnp.int32, (LANES, width), 1) // (width // heads))
    spread = spread.astype(F32).astype(BF16)
    for ref, value in ((first_out, first), (last_out, last)):
        parts = split_parts(value, 2)
        ref[...] = mm(parts[0], spread) + mm(parts[1], spread)
    wide[:heads] = jnp.sqrt(one_less_exp(2.0 * jnp.minimum(decay_ref[...], RATE_CAP)))
    eye = (row == col).astype(F32).astype(BF16)
    beta_col = jnp.zeros((tok, LANES), F32)
    for part in split_parts(wide[...], 2):
        beta_col = beta_col + mm(eye, part, NT)
    parts = split_parts(beta_col, 2)
    beta_out[...] = mm(parts[0], spread) + mm(parts[1], spread)
    gate_out[...] = jnp.broadcast_to(first_out[tok - 1 :], gate_out.shape).astype(BF16)


def row_of(ref):
    return ref[...].reshape(1, ref.shape[0])


def norm_rows(rows_in):
    count = rows_in.shape[1]
    center = rows_in - jnp.sum(rows_in, axis=1, keepdims=True) * (1.0 / count)
    spread = jnp.sum(center * center, axis=1, keepdims=True) * (1.0 / count)
    inverse = lax.rsqrt(spread + NORM_EPS)
    return center * inverse, inverse


def norm_back(grad_rows, unit_rows, inverse, gain_vec):
    scale = 1.0 / grad_rows.shape[1]
    scaled = grad_rows * gain_vec
    return inverse * (scaled - jnp.sum(scaled, axis=1, keepdims=True) * scale
                      - unit_rows * (jnp.sum(scaled * unit_rows, axis=1, keepdims=True) * scale))


def by_rows(tok, body, size=512):
    def step(i, carry):
        body(pl.ds(pl.multiple_of(i * size, size), size))
        return carry

    lax.fori_loop(0, tok // size, step, 0)


def in_kernel(place_ref, own_ref, other_ref, gain_ref, bias_ref, wq_ref, wk_ref, wv_ref, docc_ref,
              normed_ref, q_ref, k_ref, v_ref, tail_ref, rows):
    h = place_ref[1]
    tok, width = own_ref.shape
    half_of(rows, h, width)[...] = own_ref[...]
    half_of(rows, 1 - h, width)[...] = other_ref[...]

    def norm(at):
        unit, _ = norm_rows(rows[at].astype(F32))
        normed_ref[at] = (unit * row_of(gain_ref) + row_of(bias_ref)).astype(BF16)

    by_rows(tok, norm)
    normed = normed_ref[...]
    k_ref[...] = mm(normed, wk_ref[...]).astype(BF16)
    keep = docc_ref[tok - STEP :] == docc_ref[tok - 1 :]
    for l in lanes(width):
        tail_ref[:, l : l + LANES] = jnp.where(
            keep, k_ref[tok - STEP :, l : l + LANES].astype(F32), 0.0).astype(BF16)
    q_ref[...] = mm(normed, wq_ref[...]).astype(BF16)
    v_ref[...] = mm(normed, wv_ref[...]).astype(BF16)


def filter_chunk(keys, taps, dist, count, t0):
    def group(a, acc):
        acc = list(acc)
        for b in range(32):
            j = a * 32 + b
            keep = dist >= j.astype(F32)
            for l in range(count):
                x = keys[l, pl.ds(STEP + t0 - a * 32 - b, STEP), :]
                acc[l] = acc[l] + jnp.where(keep, x * taps[l, pl.ds(j, 1), :], 0.0)
        return tuple(acc)

    return lax.fori_loop(0, STEP // 32, group, tuple(jnp.zeros((STEP, LANES), F32) for _ in range(count)))


def filter_kernel(k_ref, taps_ref, dist_ref, beta_ref, out_ref, keys, taps):
    tok, width = k_ref.shape
    count = width // LANES
    for l in range(count):
        keys[l, STEP:] = k_ref[:, l * LANES : (l + 1) * LANES].astype(F32)
        taps[l] = taps_ref[:, l * LANES : (l + 1) * LANES].astype(F32)
    out_ref[:STEP] = jnp.zeros((STEP, width), BF16)

    def chunk(c, carry):
        t0 = pl.multiple_of(c * STEP, STEP)
        at = pl.ds(t0, STEP)
        acc = filter_chunk(keys, taps, dist_ref[at], count, t0)
        for l in range(count):
            span = slice(l * LANES, (l + 1) * LANES)
            out_ref[at, span] = (acc[l] * beta_ref[at, span]).astype(BF16)
        return carry

    lax.fori_loop(1, tok // STEP, chunk, 0)


def fold(square, low):
    return jnp.where(low, square[:STEP], square[STEP:])


def unfold(flat, low):
    return jnp.concatenate([jnp.where(low, flat, 0.0), jnp.where(low, 0.0, flat)], axis=0)


def low_lanes(rows):
    return lax.broadcasted_iota(jnp.int32, (rows, LANES), 1) < STEP


def state_kernel(part_ref, tail_ref, k_ref, taps_ref, dist_ref, beta_ref, last_ref, v_ref, gate_ref,
                 sk_ref, message_ref, keys, taps):
    tok, width = part_ref.shape
    count = width // LANES
    for l in range(count):
        span = slice(l * LANES, (l + 1) * LANES)
        keys[l, :STEP] = tail_ref[:, span].astype(F32)
        keys[l, STEP:] = k_ref[:STEP, span].astype(F32)
        taps[l] = taps_ref[:, span].astype(F32)
    sk_ref[...] = part_ref[...]
    acc = filter_chunk(keys, taps, dist_ref[:STEP], count, 0)
    low = low_lanes(STEP)
    for l in range(count):
        span = slice(l * LANES, (l + 1) * LANES)
        sk_ref[:STEP, span] = (acc[l] * beta_ref[:STEP, span]).astype(BF16)
        weighted = (sk_ref[:, span].astype(F32) * last_ref[:, span]).astype(BF16)
        message_ref[:STEP, span] = fold(mm(weighted, v_ref[:, span], TN), low).astype(BF16)
    message_ref[STEP:] = gate_ref[...]


def kept_pairs(docc_ref, docr_ref):
    tok = docc_ref.shape[0]
    order = lax.broadcasted_iota(jnp.int32, (tok, tok), 0) >= lax.broadcasted_iota(jnp.int32, (tok, tok), 1)
    return (docc_ref[:, :1] == docr_ref[:1]) & order


def own_lanes(x, low, e):
    return jnp.where(low if e == 0 else ~low, x.astype(F32), 0.0).astype(BF16)


def decay_of(lamr_ref, lamc_ref, keep, e):
    span = jnp.minimum(lamr_ref[e : e + 1] - lamc_ref[:, e : e + 1], 0.0)
    return jnp.where(keep, jnp.exp(span), 0.0)


def inside_kernel(q_ref, k_ref, v_ref, lamr_ref, lamc_ref, docr_ref, docc_ref, out_ref):
    low = low_lanes(q_ref.shape[0])
    keep = kept_pairs(docc_ref, docr_ref)
    outs = []
    for e in range(2):
        score = mm(own_lanes(q_ref[...], low, e), k_ref[...], NT)
        outs.append(mm((score * decay_of(lamr_ref, lamc_ref, keep, e)).astype(BF16), v_ref[...]))
    out_ref[...] = jnp.where(low, outs[0], outs[1])


def mixed_kernel(stage, place_ref, inside_ref, q_ref, first_ref, *refs):
    (state_ref, mixed_ref) = refs[-2:]
    before, _ = link(stage, False, place_ref, refs[: stage[1]], refs[stage[1] : -2], False)
    state_ref[...] = before[1]
    low = low_lanes(STEP)
    for l in lanes(q_ref.shape[1]):
        span = slice(l, l + LANES)
        square = unfold(state_ref[:, span], low).astype(BF16)
        mixed_ref[:, span] = (0.125 * (inside_ref[:, span] + first_ref[:, span] * mm(q_ref[:, span], square))
                              ).astype(BF16)


def hidden_grad_kernel(place_ref, own_ref, other_ref, down_ref, out_ref, full_ref):
    @pl.when(pl.program_id(0) == 0)
    def _():
        width = own_ref.shape[1]
        half_of(full_ref, place_ref[1], width)[...] = own_ref[...]
        half_of(full_ref, 1 - place_ref[1], width)[...] = other_ref[...]

    out_ref[...] = mm(full_ref[...], down_ref[...]).astype(BF16)


def ffn_kernel(place_ref, own_ref, other_ref, mix_own_ref, mix_other_ref, out_own_ref, out_other_ref, gain_ref,
               bias_ref, up_ref, hg_ref, resid_ref, normed_ref, hidden_ref, pre_ref, part_ref, rows, acc):
    h = place_ref[1]
    step = pl.program_id(0)
    tok, width = own_ref.shape

    @pl.when(step == 0)
    def _():
        half_of(rows, h, width)[...] = own_ref[...]
        half_of(rows, 1 - h, width)[...] = other_ref[...]
        resid_ref[...] = mm(mix_own_ref[...], out_own_ref[...], NT) + mm(mix_other_ref[...], out_other_ref[...], NT)

        def norm(at):
            resid = rows[at].astype(F32) + resid_ref[at]
            resid_ref[at] = resid
            unit, _ = norm_rows(resid)
            normed_ref[at] = (unit * row_of(gain_ref) + row_of(bias_ref)).astype(BF16)

        by_rows(tok, norm)
        acc[...] = jnp.zeros_like(acc)

    pre = mm(normed_ref[...], up_ref[...])
    square = pre * pre
    bent = jnp.tanh(GELU_SCALE * (pre + GELU_CUBE * (square * pre)))
    outer = 0.5 * (1.0 + bent)
    hidden_ref[...] = (pre * outer).astype(BF16)
    slope = outer + 0.5 * pre * (1.0 - bent * bent) * (GELU_SCALE * (1.0 + 3.0 * GELU_CUBE * square))
    pre_ref[...] = (hg_ref[...].astype(F32) * slope).astype(BF16)
    acc[...] += mm(pre_ref[...], up_ref[...], NT)

    @pl.when(step == pl.num_programs(0) - 1)
    def _():
        part_ref[...] = acc[...].astype(BF16)


def norm2_kernel(place_ref, part_ref, got_ref, resid_ref, grad_ref, gain_ref, out_w_ref, q_ref, first_ref,
                 gate_ref, resid_grad_ref, branch_ref, g_ref, sums_ref, message_ref, rows):
    h = place_ref[1]
    tok, width = q_ref.shape
    sums_ref[...] = jnp.zeros_like(sums_ref)

    def norm(at):
        back = part_ref[at].astype(F32) + got_ref[at].astype(F32)
        unit, inverse = norm_rows(resid_ref[at])
        grad = grad_ref[at].astype(F32) + norm_back(back, unit, inverse, row_of(gain_ref))
        rows[at] = grad
        branch_ref[at] = grad.astype(BF16)
        sums_ref[0:1] += jnp.sum(back * unit, axis=0, keepdims=True)
        sums_ref[1:2] += jnp.sum(back, axis=0, keepdims=True)

    by_rows(tok, norm)
    resid_grad_ref[...] = half_of(rows, h, width)[...]
    g_ref[...] = (0.125 * mm(branch_ref[...], out_w_ref[...]).astype(BF16).astype(F32)).astype(BF16)
    low = low_lanes(STEP)
    for l in lanes(width):
        span = slice(l, l + LANES)
        weighted = (q_ref[:, span].astype(F32) * first_ref[:, span]).astype(BF16)
        message_ref[:STEP, span] = fold(mm(weighted, g_ref[:, span], TN), low).astype(BF16)
    message_ref[STEP:] = gate_ref[...]


def back_kernel(q_ref, k_ref, v_ref, g_ref, lamr_ref, lamc_ref, docr_ref, docc_ref, first_ref, state_ref,
                dq_ref, dk_ref, dv_ref):
    low = low_lanes(q_ref.shape[0])
    keep = kept_pairs(docc_ref, docr_ref)
    square = unfold(state_ref[...], low_lanes(STEP)).astype(BF16)
    outs = []
    for e in range(2):
        decay = decay_of(lamr_ref, lamc_ref, keep, e)
        prob = (mm(own_lanes(q_ref[...], low, e), k_ref[...], NT) * decay).astype(BF16)
        score = (mm(own_lanes(g_ref[...], low, e), v_ref[...], NT) * decay).astype(BF16)
        outs.append((mm(score, k_ref[...]), mm(score, q_ref[...], TN), mm(prob, g_ref[...], TN)))
    from_state = first_ref[...] * mm(g_ref[...], square, NT)
    dq_ref[...] = (jnp.where(low, outs[0][0], outs[1][0]) + from_state).astype(BF16)
    dk_ref[...] = jnp.where(low, outs[0][1], outs[1][1])
    dv_ref[...] = jnp.where(low, outs[0][2], outs[1][2])


def filter_back_chunk(sg, keys, taps, ahead, sums, count, s0):
    held = [keys[l, pl.ds(s0, SPAN), :] for l in range(count)]

    def group(a, acc):
        acc = list(acc)
        for b in range(16):
            j = a * 16 + b
            keep = ahead > j.astype(F32)
            for l in range(count):
                u = jnp.where(keep, sg[l, pl.ds(s0 + a * 16 + b, SPAN), :], 0.0)
                acc[l] = acc[l] + u * taps[l, pl.ds(j, 1), :]
                sums[l, j] += jnp.sum((held[l] * u).reshape(SPAN // 8, 8, LANES), axis=0)
        return tuple(acc)

    return lax.fori_loop(0, STEP // 16, group, tuple(jnp.zeros((SPAN, LANES), F32) for _ in range(count)))


def reach(docr_ref, docc_ref, ahead_ref):
    tok = docc_ref.shape[0]
    order = lax.broadcasted_iota(jnp.int32, (tok, tok), 0) <= lax.broadcasted_iota(jnp.int32, (tok, tok), 1)
    same = jnp.where((docc_ref[:, :1] == docr_ref[:1]) & order, 1.0, 0.0).astype(BF16)
    ahead_ref[STEP:] = mm(same, jnp.ones((tok, LANES), BF16))
    unbroken = jnp.sum(jnp.where(docr_ref[:1] == 0.0, 1.0, 0.0), axis=1, keepdims=True)
    ahead_ref[:STEP] = unbroken + STEP - lax.broadcasted_iota(jnp.int32, (STEP, LANES), 0).astype(F32)


def carry_kernel(stage, place_ref, dk_ref, dv_ref, k_ref, v_ref, last_ref, beta_ref, docr_ref, docc_ref, taps_ref,
                 tail_ref, *refs):
    value_ref, sg_ref, edge_ref, sums, ahead_ref, taps, keys = refs[-7:]
    reach(docr_ref, docc_ref, ahead_ref)
    before, _ = link(stage, True, place_ref, refs[: stage[1]], refs[stage[1] : -7], False)
    state = before[1]
    tok, width = dk_ref.shape
    count = width // LANES
    low = low_lanes(STEP)
    for l in range(count):
        span = slice(l * LANES, (l + 1) * LANES)
        square = unfold(state[:, span], low).astype(BF16)
        last = last_ref[:, span]
        value_ref[:, span] = (dv_ref[:, span] + last * mm(k_ref[:, span], square)).astype(BF16)
        sg_ref[l, :STEP] = jnp.zeros((STEP, LANES), F32)
        sg_ref[l, STEP : STEP + tok] = beta_ref[:, span] * (
            dk_ref[:, span] + last * mm(v_ref[:, span], square, NT))
        sg_ref[l, STEP + tok :] = jnp.zeros((STEP, LANES), F32)
        keys[l] = tail_ref[:, span].astype(F32)
        taps[l] = taps_ref[:, span].astype(F32)
    sums[...] = jnp.zeros_like(sums)
    for s0 in range(0, STEP, SPAN):
        at = slice(s0, s0 + SPAN)
        acc = filter_back_chunk(sg_ref, keys, taps, ahead_ref[at], sums, count, s0)
        for l in range(count):
            edge_ref[at, l * LANES : (l + 1) * LANES] = acc[l].astype(BF16)


def filter_back_kernel(sg_ref, k_ref, ahead_ref, taps_ref, sums_in, grad_ref, taps_grad_ref, keys, taps, sums):
    tok, width = k_ref.shape
    count = width // LANES
    for l in range(count):
        span = slice(l * LANES, (l + 1) * LANES)
        keys[l, STEP:] = k_ref[:, span].astype(F32)
        taps[l] = taps_ref[:, span].astype(F32)
    sums[...] = sums_in[...]

    def chunk(c, carry):
        s0 = pl.multiple_of(c * SPAN, SPAN)
        acc = filter_back_chunk(sg_ref, keys, taps, ahead_ref[pl.ds(s0, SPAN)], sums, count, s0)
        for l in range(count):
            grad_ref[pl.ds(s0 - STEP, SPAN), l * LANES : (l + 1) * LANES] = acc[l]
        return carry

    lax.fori_loop(STEP // SPAN, (tok + STEP) // SPAN, chunk, 0)
    for l in range(count):
        taps_grad_ref[:, l * LANES : (l + 1) * LANES] = jnp.sum(sums[l], axis=1)


def out_kernel(place_ref, grad_ref, edge_ref, docc_ref, dq_ref, dv_ref, wq_ref, wk_ref, wv_ref, own_ref, other_ref,
               key_ref, part_ref, rows, total, sums_ref):
    h = place_ref[1]
    tok, width = own_ref.shape
    keep = docc_ref[tok - STEP :] == docc_ref[tok - 1 :]
    key_ref[: tok - STEP] = grad_ref[: tok - STEP].astype(BF16)
    for l in lanes(width):
        span = slice(l, l + LANES)
        edge = jnp.where(keep, edge_ref[:, span].astype(F32), 0.0)
        key_ref[tok - STEP :, span] = (grad_ref[tok - STEP :, span] + edge).astype(BF16)
    total[...] = (mm(dq_ref[...], wq_ref[...], NT) + mm(dv_ref[...], wv_ref[...], NT)
                  + mm(key_ref[...], wk_ref[...], NT))
    part_ref[:tok] = total[...].astype(BF16)
    half_of(rows, h, width)[...] = own_ref[...]
    half_of(rows, 1 - h, width)[...] = other_ref[...]
    sums_ref[...] = jnp.zeros_like(sums_ref)

    def norm(at):
        unit, _ = norm_rows(rows[at].astype(F32))
        sums_ref[0:1] += jnp.sum(total[at] * unit, axis=0, keepdims=True)
        sums_ref[1:2] += jnp.sum(total[at], axis=0, keepdims=True)

    by_rows(tok, norm)
    part_ref[tok:] = sums_ref[...].astype(BF16)


def key_grads_kernel(place_ref, normed_ref, key_ref, taps_ref, sums2_ref, part_ref, got_ref, keep, send, total, shared):
    put_rows(total, 0, mm(normed_ref[...], key_ref[...], TN))
    tok, width = key_ref.shape
    shared[STEP:] = jnp.zeros_like(shared[STEP:])
    shared[:STEP] = taps_ref[...]
    sums1 = part_ref[tok:].astype(F32) + got_ref[tok:].astype(F32)
    for at, sums in ((STEP, sums1), (STEP + 2, sums2_ref[...])):
        shared[at : at + 2] = jnp.where(place_ref[1] == 0, sums[:2, :width], sums[:2, width:])
    put_messages(place_ref, 0, total.shape[0], total, shared[...], keep, send)


def input_kernel(place_ref, part_ref, got_ref, own_ref, other_ref, gain_ref, resid_grad_ref, out_ref, rows, back):
    h = place_ref[1]
    tok, width = own_ref.shape
    half_of(rows, h, width)[...] = own_ref[...]
    half_of(rows, 1 - h, width)[...] = other_ref[...]

    def norm(at):
        unit, inverse = norm_rows(rows[at].astype(F32))
        grad = part_ref[at].astype(F32) + got_ref[at].astype(F32)
        back[at] = norm_back(grad, unit, inverse, row_of(gain_ref))

    by_rows(tok, norm)
    out_ref[...] = (half_of(back, h, width)[...] + resid_grad_ref[...]).astype(BF16)


def local(block_input, starts, decay_rate, norm1_gain, norm1_bias, q_weight, k_weight, v_weight,
          shift_kernel, out_weight, norm2_gain, norm2_bias, up_weight, down_weight, out_grad):
    tok, width = block_input.shape
    heads = decay_rate.shape[0]
    full = 2 * width
    hidden_width = up_weight.shape[1]
    count = width // LANES
    seqs = lax.axis_size("seq")
    place = jnp.stack([lax.axis_index("seq"), lax.axis_index("head")]).astype(jnp.int32)
    gain1, bias1, gain2, bias2 = norm1_gain, norm1_bias, norm2_gain, norm2_bias
    vm = pltpu.VMEM

    stages = digits_of(seqs)
    other_input = swapped(block_input)
    other_grad = swapped(out_grad)
    other_out = swapped(out_weight)
    lamr, lamc, docr, docc, dist, beta_w, first_w, last_w, gate_w = run(
        side_kernel,
        (shape((8 * count, tok), F32), shape((count * tok, LANES), F32), shape((8, tok), F32),
         shape((tok, LANES), F32), shape((tok, LANES), F32),
         shape((tok, width), F32), shape((tok, width), F32), shape((tok, width), F32), shape((16, width), BF16)),
        starts, decay_rate, far=(0, 1),
        scratch=[vm((tok, tok), BF16), vm((tok, tok), BF16), vm((LANES, tok), F32)], us=2.7)
    other_input = after(other_input, docc)
    normed1, query, key, value, tail = run(
        in_kernel,
        (shape((tok, full), BF16),) + (shape((tok, width), BF16),) * 3 + (shape((STEP, width), BF16),),
        place, block_input, other_input, gain1, bias1, q_weight, k_weight, v_weight, docc,
        scratch=[vm((tok, full), BF16)], scalars=1, us=3.0)
    prev_tail = passed_along(tail, 1)
    scaled_part = run(
        filter_kernel, shape((tok, width), BF16), key, shift_kernel, dist, beta_w,
        scratch=[vm((count, tok + STEP, LANES), F32), vm((count, STEP, LANES), F32)], us=5.4)
    prev_tail = after(prev_tail, scaled_part)
    scaled, message = run(
        state_kernel, (shape((tok, width), BF16), shape((STEP + 16, width), BF16)),
        scaled_part, prev_tail, key, shift_kernel, dist, beta_w, last_w, value, gate_w,
        scratch=[vm((count, 2 * STEP, LANES), F32), vm((count, STEP, LANES), F32)], us=1.7)
    pair_spec = pl.BlockSpec((tok, LANES), lambda p: (0, p))
    lamr_spec = pl.BlockSpec((8, tok), lambda p: (p, 0))
    lamc_spec = pl.BlockSpec((tok, LANES), lambda p: (p, 0))
    state_spec = pl.BlockSpec((STEP, LANES), lambda p: (0, p))
    tile = 768

    before = ()
    got = scan_send(message, 0, False)
    hidden_grad, grad_full = run(
        hidden_grad_kernel, (shape((tok, hidden_width), BF16), shape((tok, full), BF16)),
        place, out_grad, after(other_grad, message), down_weight, scalars=1,
        grid=(hidden_width // tile,), in_specs=[None, None, pl.BlockSpec((full, tile), lambda i: (0, i))],
        out_specs=(pl.BlockSpec((tok, tile), lambda i: (0, i)), None), us=2.5)
    last_got = [after(g, hidden_grad) for g in got]
    for at in range(len(stages) - 1):
        before, message = scan_link(place, last_got, before, at, False)
        last_got = scan_send(message, at + 1, False)
    query_late = after(query, message)
    inside = run(
        inside_kernel, shape((tok, width), F32), query_late, scaled, value, lamr, lamc, docr, docc,
        grid=(count,),
        in_specs=[pair_spec] * 3 + [lamr_spec, lamc_spec, None, None], out_specs=pair_spec, us=3.5)
    last_got = [after(g, inside) for g in last_got]
    state, mixed = run(
        functools.partial(mixed_kernel, stages[-1]), (shape((STEP, width), F32), shape((tok, width), BF16)),
        place, inside, query, first_w, *last_got, *before, scalars=1, us=1.2)
    mixed_other = swapped(mixed)

    wide_tile = pl.BlockSpec((full, tile), lambda i: (0, i))
    tok_tile = pl.BlockSpec((tok, tile), lambda i: (0, i))
    resid, normed2, hidden, pre_grad, part2 = run(
        ffn_kernel,
        (shape((tok, full), F32), shape((tok, full), BF16), shape((tok, hidden_width), BF16),
         shape((tok, hidden_width), BF16), shape((tok, full), BF16)),
        place, block_input, other_input, mixed, mixed_other, out_weight, other_out, gain2, bias2, up_weight, hidden_grad,
        scratch=[vm((tok, full), BF16), vm((tok, full), F32)], scalars=1, mib=24,
        grid=(hidden_width // tile,),
        in_specs=[None] * 8 + [wide_tile, tok_tile],
        out_specs=(None, None, tok_tile, tok_tile, None), us=10.8)
    got2 = swapped(part2)
    rows = full // seqs
    up_width = hidden_width + width
    down_keep, down_send, ffn_own, ffn_send = run(
        down_kernel,
        half_shapes(seqs, rows, hidden_width) + (shape((tok, width), F32), shape((tok, width), BF16)),
        place, grad_full, hidden, down_weight, resid, scalars=1,
        scratch=[vm((seqs, rows, hidden_width), BF16), vm((tok, full), F32)], mib=24, us=2.46)
    ffn_other = swapped(ffn_send)
    got2 = after(got2, ffn_own)
    resid_grad, branch, g_low, sums2, message = run(
        norm2_kernel,
        (shape((tok, width), F32), shape((tok, full), BF16), shape((tok, width), BF16), shape((8, full), F32),
         shape((STEP + 16, width), BF16)),
        place, part2, got2, resid, grad_full, gain2, out_weight, query, first_w, gate_w,
        scratch=[vm((tok, full), F32)], scalars=1, us=2.34)
    before = ()
    got = scan_send(message, 0, True)
    up_keep, up_send, block_output = run(
        functools.partial(up_kernel, (0, hidden_width)),
        half_shapes(seqs, rows, up_width) + (shape((tok, width), BF16),),
        place, after(normed2, message), branch, pre_grad, mixed, ffn_own, ffn_other, scalars=1,
        scratch=[vm((seqs, rows, up_width), BF16)], mib=24, us=1.92)
    got = [after(g, block_output) for g in got]
    for at in range(len(stages) - 1):
        before, message = scan_link(place, got, before, at, True)
        got = scan_send(message, at + 1, True)
    up_got = mirrored(after(up_send, message), 0)
    down_got = mirrored(after(down_send, message), 0, True)
    query_late = after(query, message)
    query_grad, dk_part, dv_part = run(
        back_kernel, (shape((tok, width), BF16), shape((tok, width), F32), shape((tok, width), F32)),
        query_late, scaled, value, g_low, lamr, lamc, docr, docc, first_w, state,
        grid=(count,),
        in_specs=[pair_spec] * 4 + [lamr_spec, lamc_spec, None, None, pair_spec, state_spec],
        out_specs=(pair_spec,) * 3, us=1.28)
    got = [after(g, query_grad) for g in got]
    value_grad, shifted_grad, edge, sums, ahead = run(
        functools.partial(carry_kernel, stages[-1]),
        (shape((tok, width), BF16), shape((count, tok + 2 * STEP, LANES), F32), shape((STEP, width), BF16),
         shape((count, STEP, 8, LANES), F32), shape((tok + STEP, LANES), F32)),
        place, dk_part, dv_part, scaled, value, last_w, beta_w, docr, docc, shift_kernel, prev_tail,
        *got, *before, scalars=1,
        scratch=[vm((count, STEP, LANES), F32), vm((count, STEP, LANES), F32)], us=1.5)
    got_edge = passed_along(edge, -1)
    mix_keep, mix_send = run(
        functools.partial(grads_kernel, (0, width)), half_shapes(seqs, rows, 2 * width),
        place, normed1, normed1, query_grad, after(value_grad, edge), scalars=1,
        scratch=[vm((seqs, rows, 2 * width), BF16)], us=1.14)
    mix_got = mirrored(mix_send, 0)
    up_keep, up_send = folded(place, up_keep, after(up_got, mix_keep), 0, (), 8)
    up_got = mirrored(up_send, 1)
    key_rows, taps_grad = run(
        filter_back_kernel, (shape((tok, width), F32), shape((STEP, width), F32)),
        shifted_grad, key, ahead, shift_kernel, after(sums, up_keep),
        scratch=[vm((count, tok + STEP, LANES), F32), vm((count, STEP, LANES), F32),
                 vm((count, STEP, 8, LANES), F32)], us=7.05)
    key_grad, part1 = run(
        out_kernel, (shape((tok, width), BF16), shape((tok + 8, full), BF16)),
        place, key_rows, after(got_edge, key_rows), docc, query_grad, value_grad, q_weight, k_weight, v_weight,
        block_input, other_input,
        scratch=[vm((tok, full), BF16), vm((tok, full), F32), vm((8, full), F32)], scalars=1, us=2.16)
    got1 = swapped(part1)
    up_keep, up_send = folded(place, up_keep, after(up_got, key_grad), 1, (), 0.5)
    up_got = mirrored(up_send, 2)
    mix_keep, mix_send = folded(place, mix_keep, after(mix_got, up_keep), 0, (), 1)
    mix_got = mirrored(mix_send, 1)
    down_keep, down_send = folded(place, down_keep, after(down_got, mix_keep), 0, (), 1, True)
    down_got = mirrored(down_send, 1, True)
    key_keep, key_send = run(
        key_grads_kernel, (shape((seqs // 2 * rows + STEP + 8, width), BF16),) * 2,
        place, normed1, key_grad, taps_grad, sums2, part1, after(got1, down_keep), scalars=1,
        scratch=[vm((seqs, rows, width), BF16), vm((STEP + 8, width), F32)], us=0.78)
    key_got = mirrored(key_send, 0)
    input_grad = run(
        input_kernel, shape((tok, width), BF16),
        place, part1, after(got1, key_keep), block_input, other_input, gain1, resid_grad, scalars=1,
        scratch=[vm((tok, full), BF16), vm((tok, full), F32)], us=0.89)
    mix_keep, mix_send = folded(place, mix_keep, after(mix_got, input_grad), 1, (), 8)
    mix_got = mirrored(mix_send, 2)
    down_keep, down_send = folded(place, down_keep, after(down_got, mix_keep), 1, (), 1, True)
    down_got = mirrored(down_send, 2, True)
    up_keep, up_send = folded(place, up_keep, after(up_got, down_keep), 2, (), 0.2)
    up_got = mirrored(up_send, 3)
    key_keep, key_send = folded_message(place, key_keep, after(key_got, up_keep), 0, rows, 4)
    key_got = mirrored(key_send, 1)
    down_keep, down_send = folded(place, down_keep, after(down_got, key_keep), 2, (), 4, True)
    down_got = mirrored(down_send, 3, True)
    mix_keep, mix_send = folded(place, mix_keep, after(mix_got, down_keep), 2, (), 4)
    mix_got = mirrored(mix_send, 3)
    key_keep, key_send = folded_message(place, key_keep, after(key_got, mix_keep), 1, rows, 2)
    key_got = mirrored(key_send, 2)
    up_total, out_total = folded_last(place, up_keep, after(up_got, key_keep), 3, (hidden_width, width), 1)
    key_keep, key_send = folded_message(place, key_keep, after(key_got, up_total), 2, rows, 8)
    key_got = mirrored(key_send, 3)
    (down_total,) = folded_last(place, down_keep, after(down_got, key_keep), 3, (hidden_width,), 0.2, True)
    key_got = after(key_got, down_total)
    for at in range(3, len(strides_of(seqs)) - 1):
        key_keep, key_send = folded_message(place, key_keep, key_got, at, rows, 8)
        key_got = mirrored(key_send, at + 1)
    k_total, taps_total, vectors = folded_message(
        place, key_keep, key_got, len(strides_of(seqs)) - 1, rows, 0.5)
    other_vectors = swapped(vectors)
    mix_got = after(mix_got, vectors)
    for at in range(3, len(strides_of(seqs)) - 1):
        mix_keep, mix_send = folded(place, mix_keep, mix_got, at, (), 0.5)
        mix_got = mirrored(mix_send, at + 1)
    q_total, v_total, gain1_grad, bias1_grad, gain2_grad, bias2_grad = run(
        functools.partial(end_kernel, (width, width)), (shape((rows, width), F32),) * 2 + (shape((full,), F32),) * 4,
        place, mix_keep, mix_got, vectors, other_vectors, scalars=1, us=0.5)
    return (block_output, input_grad, gain1_grad, bias1_grad, q_total, k_total, v_total, taps_total, out_total,
            gain2_grad, bias2_grad, up_total, down_total)


def solution(mesh):
    both, head = P("seq", "head"), P(None, "head")
    in_specs = (both, P("seq"), P("head", "seq"), P(), P(), head, head, head, head, head, P(), P(), head, head, both)
    out_specs = (both, both, P(), P(), both, both, both, head, both, P(), P(), both, both)
    return jax.shard_map(local, mesh=mesh, in_specs=in_specs, out_specs=out_specs, check_vma=False)
```

```python
import functools

import jax
import jax.numpy as jnp
from jax import lax
from jax.experimental import pallas as pl
from jax.experimental.pallas import tpu as pltpu
from jax.sharding import PartitionSpec as P

NORM_EPS = 1e-05
RATE_CAP = 0.05
LANES = 128
STEP = 64
SPAN = 32
FAR = float(1 << 20)
GELU_SCALE = 0.7978845608028654
GELU_CUBE = 0.044715
F32 = jnp.float32
BF16 = jnp.bfloat16

NN = (((1,), (0,)), ((), ()))
NT = (((1,), (1,)), ((), ()))
TN = (((0,), (0,)), ((), ()))


def mm(a, b, dims=NN):
    return lax.dot_general(a, b, dims, preferred_element_type=F32)


def shape(dims, kind):
    return pltpu.HBM(dims, kind)


def shape(dims, kind):
    return jax.ShapeDtypeStruct(dims, kind)


FEW = pl.BlockSpec(memory_space=pltpu.SMEM)


def whole(array):
    dims = array.shape
    return pl.BlockSpec(dims, lambda *_: (0,) * len(dims), pipeline_mode=pl.Buffered(1))


def run(body, outs, *ins, scratch=(), scalars=0, grid=(1,), in_specs=None, out_specs=None, mib=16,
        us=1.0, far=()):
    many = isinstance(outs, (tuple, list))
    held = [pltpu.with_memory_space_constraint(x, pltpu.HBM) if i in far else x for i, x in enumerate(ins)]
    if in_specs is None:
        in_specs = [None] * (len(ins) - scalars)
    if out_specs is None:
        out_specs = (None,) * len(outs) if many else None
    in_specs = [spec or whole(x) for spec, x in zip(in_specs, ins[scalars:])]
    pick = lambda spec, x: spec or whole(x)
    out_specs = tuple(map(pick, out_specs, outs)) if many else pick(out_specs, outs)
    return pl.pallas_call(
        body, out_shape=outs, grid=grid, in_specs=[FEW] * scalars + list(in_specs), out_specs=out_specs,
        scratch_shapes=list(scratch), compiler_params=pltpu.CompilerParams(vmem_limit_bytes=mib << 20),
        cost_estimate=pl.CostEstimate(flops=int(us * 1e9), transcendentals=0, bytes_accessed=int(us * 3e6)))(*held)


def after(value, *first):
    return lax.optimization_barrier((value,) + first)[0]


def lanes(width):
    return range(0, width, LANES)


def half_of(ref, h, width):
    return ref.at[:, pl.ds(pl.multiple_of(h * width, LANES), width)]


def digits_of(count):
    digits, stride = [], 1
    while count > 1:
        radix = 4 if count % 4 == 0 else (2 if count % 2 == 0 else count)
        digits.append((stride, radix))
        stride, count = stride * radix, count // radix
    return digits


def turned(array, stride, radix, by):
    pairs = []
    for i in range(lax.axis_size("seq")):
        member = i // stride % radix
        pairs.append((i, i + ((member + by) % radix - member) * stride))
    return lax.ppermute(array, "seq", pairs)


def crossed(array, stride, radix, mask):
    pairs = []
    for i in range(lax.axis_size("seq")):
        member = i // stride % radix
        pairs.append((i, i + ((member ^ mask) - member) * stride))
    return lax.ppermute(array, "seq", pairs)


def swapped(array):
    count = lax.axis_size("head")
    return lax.ppermute(array, "head", [(i, (i + 1) % count) for i in range(count)])


def passed_along(array, by):
    count = lax.axis_size("seq")
    return lax.ppermute(array, "seq", [(i, i + by) for i in range(count) if 0 <= i + by < count])


def member_at(place_ref, stride, radix):
    return lax.rem(lax.div(place_ref[0], stride), radix)


def strides_of(count, z_first=False):
    bits = [1 << k for k in range(count.bit_length() - 1)]
    if z_first and len(bits) > 3:
        x, y, low, high = bits[:4]
        return [(low, high), (x, y), (y, x), (high, low)] + [(b, b) for b in bits[4:]]
    order = []
    for k in range(0, len(bits) - 1, 2):
        order += [(bits[k], bits[k + 1]), (bits[k + 1], bits[k])]
    return order + [(b, b) for b in bits[len(order) :]]


def mirrored(array, at, z_first=False):
    count, cores = lax.axis_size("seq"), lax.axis_size("head")
    strides = strides_of(count, z_first)[at]
    pairs = [(i * cores + h, (i ^ strides[h % 2]) * cores + h) for i in range(count) for h in range(cores)]
    return lax.ppermute(array, ("seq", "head"), pairs)


def pick(place_ref, first, second):
    return jnp.where(place_ref[1] == 0, first, second)


def halved(place_ref, at, count, z_first=False):
    pairs = strides_of(count, z_first)
    lows = []
    for h in range(2):
        left = sorted(set(p[h] for p in pairs) - set(p[h] for p in pairs[:at]))
        lows.append(1 << left.index(pairs[at][h]))
    bit = pick(place_ref, *(lax.rem(lax.div(place_ref[0], stride), 2) for stride in pairs[at]))
    places = []
    for g in range((count >> at) // 2):
        bases = [g // low * 2 * low + g % low for low in lows]
        base, low = pick(place_ref, *bases), pick(place_ref, *lows)
        places.append((base + bit * low, base + (1 - bit) * low))
    return places


def put_halves(place_ref, at, count, total, keep, send, z_first=False):
    for g, (mine, other) in enumerate(halved(place_ref, at, count, z_first)):
        keep[g] = total[mine].astype(BF16)
        send[g] = total[other].astype(BF16)


def put_rows(total, at, grad):
    rows = total.shape[1]
    for s in range(total.shape[0]):
        total[s, :, at : at + grad.shape[1]] = grad[s * rows : (s + 1) * rows].astype(total.dtype)


def half_shapes(entries, rows, width):
    return (shape((entries // 2, rows, width), BF16),) * 2


def grads_kernel(spans, place_ref, *refs):
    lefts, rights, (keep, send), total = refs[: len(spans)], refs[len(spans) : 2 * len(spans)], refs[-3:-1], refs[-1]
    for left, right, at in zip(lefts, rights, spans):
        put_rows(total, at, mm(left[...], right[...], TN))
    put_halves(place_ref, 0, total.shape[0], total, keep, send)


def up_kernel(spans, place_ref, *refs):
    grads_kernel(spans, place_ref, *refs[:4], *refs[6:8], refs[-1])
    refs[8][...] = (refs[4][...] + refs[5][...].astype(F32)).astype(BF16)


def down_kernel(place_ref, grad_ref, hidden_ref, down_ref, resid_ref, keep, send, own_ref, send_ref, total, part):
    part[...] = mm(hidden_ref[...], down_ref[...], NT)
    width = own_ref.shape[1]
    h = place_ref[1]
    own_ref[...] = half_of(part, h, width)[...] + half_of(resid_ref, h, width)[...]
    send_ref[...] = half_of(part, 1 - h, width)[...].astype(BF16)
    put_rows(total, 0, mm(grad_ref[...], hidden_ref[...], TN))
    put_halves(place_ref, 0, total.shape[0], total, keep, send, True)


def fold_kernel(at, count, z_first, place_ref, keep_ref, got_ref, *refs):
    outs, total = refs[:-1], refs[-1]
    for g in range(total.shape[0]):
        total[g] = (keep_ref[g].astype(F32) + got_ref[g].astype(F32)).astype(total.dtype)
    if total.shape[0] > 1:
        put_halves(place_ref, at + 1, count, total, *outs, z_first)
        return
    begin = 0
    for out in outs:
        out[...] = total[0, :, begin : begin + out.shape[1]]
        begin += out.shape[1]


def folded(place, keep, got, at, widths, us, z_first=False):
    entries, rows, width = keep.shape
    outs = half_shapes(entries, rows, width) if entries > 1 else tuple(shape((rows, w), F32) for w in widths)
    return run(functools.partial(fold_kernel, at, lax.axis_size("seq"), z_first), outs, place, keep, got, scalars=1,
               scratch=[pltpu.VMEM((entries, rows, width), BF16 if entries > 1 else F32)], us=us)


def folded_last(place, keep, got, at, widths, us, z_first=False):
    while True:
        res = folded(place, keep, got, at, widths, us, z_first)
        if keep.shape[0] == 1:
            return res
        keep, got, at = res[0], mirrored(res[1], at + 1, z_first), at + 1


def put_messages(place_ref, at, count, total, shared, keep, send):
    rows = total.shape[1]
    places = halved(place_ref, at, count)
    for g, (mine, other) in enumerate(places):
        keep[g * rows : (g + 1) * rows] = total[mine].astype(BF16)
        send[g * rows : (g + 1) * rows] = total[other].astype(BF16)
    end = len(places) * rows
    keep[end:] = shared.astype(BF16)
    send[end:] = shared.astype(BF16)


def message_kernel(at, count, place_ref, keep_ref, got_ref, *refs):
    outs, total = refs[:-1], refs[-1]
    entries, rows, _ = total.shape
    for g in range(entries):
        span = slice(g * rows, (g + 1) * rows)
        total[g] = keep_ref[span].astype(F32) + got_ref[span].astype(F32)
    shared = keep_ref[entries * rows :].astype(F32) + got_ref[entries * rows :].astype(F32)
    if entries > 1:
        put_messages(place_ref, at + 1, count, total, shared, *outs)
        return
    outs[0][...] = total[0]
    outs[1][...] = shared[:STEP]
    outs[2][...] = shared[STEP:]


def folded_message(place, keep, got, at, rows, us):
    depth, width = keep.shape
    extra = STEP + 8
    entries = (depth - extra) // rows
    if entries > 1:
        outs = (shape((entries // 2 * rows + extra, width), BF16),) * 2
    else:
        outs = (shape((rows, width), F32), shape((STEP, width), F32), shape((8, width), F32))
    return run(functools.partial(message_kernel, at, lax.axis_size("seq")), outs, place, keep, got, scalars=1,
               scratch=[pltpu.VMEM((entries, rows, width), F32)], us=us)


def end_kernel(widths, place_ref, keep_ref, got_ref, own_ref, other_ref, *outs):
    begin = 0
    for out, width in zip(outs, widths):
        span = slice(begin, begin + width)
        out[...] = keep_ref[0, :, span].astype(F32) + got_ref[0, :, span].astype(F32)
        begin += width
    h = place_ref[1]
    own, other = own_ref[...], other_ref[...]
    width = own.shape[1]
    for k, out in enumerate(outs[len(widths) :]):
        out[:width] = jnp.where(h == 0, own[k], other[k])
        out[width:] = jnp.where(h == 0, other[k], own[k])


def chained(first, second):
    return first[0] * second[0], second[0] * first[1] + second[1]


def link(stage, reverse, place_ref, messages, before, want_total):
    radix = stage[1]
    member = member_at(place_ref, *stage)
    if reverse:
        member = radix - 1 - member
    rows = messages[0].shape[0] - 16
    pairs = []
    for m in messages:
        whole = m[...].astype(F32)
        pairs.append((whole[rows : rows + 1], whole[:rows]))
    none = (jnp.ones_like(pairs[0][0]), jnp.zeros_like(pairs[0][1]))

    def side(use):
        acc = none
        for by in range(radix - 1, 0, -1):
            kept = use(by)
            part = (jnp.where(kept, pairs[by][0], none[0]), jnp.where(kept, pairs[by][1], none[1]))
            acc = chained(acc, part)
        return acc

    lower = side(lambda by: by <= member)
    before = chained(lower, tuple(b[...] for b in before)) if before else lower
    if not want_total:
        return before, None
    return before, chained(chained(lower, pairs[0]), side(lambda by: by > member))


def link_kernel(stage, reverse, place_ref, *refs):
    messages, held, outs = refs[: stage[1]], refs[stage[1] : -3], refs[-3:]
    before, total = link(stage, reverse, place_ref, messages, held, True)
    outs[0][...], outs[1][...] = before
    rows = outs[1].shape[0]
    outs[2][:rows] = total[1].astype(BF16)
    outs[2][rows:] = jnp.broadcast_to(total[0], (outs[2].shape[0] - rows, total[0].shape[1])).astype(BF16)


def scan_send(message, at, reverse):
    stride, radix = digits_of(lax.axis_size("seq"))[at]
    return [message] + [
        turned(message, stride, radix, (radix - by) if reverse else by) for by in range(1, radix)
    ]


def scan_link(place, got, before, at, reverse):
    stage = digits_of(lax.axis_size("seq"))[at]
    rows, width = got[0].shape
    outs = run(functools.partial(link_kernel, stage, reverse),
               (shape((1, width), F32), shape((rows - 16, width), F32), shape((rows, width), BF16)),
               place, *got, *before, scalars=1, us=8)
    return outs[:2], outs[2]


def split_parts(x, count):
    parts = []
    for _ in range(count):
        low = x.astype(BF16)
        parts.append(low)
        x = x - low.astype(F32)
    return parts


def one_less_exp(x):
    acc = jnp.ones_like(x)
    for k in range(7, 1, -1):
        acc = 1.0 - x * (1.0 / k) * acc
    return x * acc


def side_kernel(starts_ref, decay_ref, lamr_ref, lamc_ref, docr_ref, docc_ref, dist_ref,
                beta_out, first_out, last_out, gate_out, tri, same, wide):
    tok = starts_ref.shape[0]
    heads = decay_ref.shape[0]
    head_pairs = lamc_ref.shape[0] // tok
    width = beta_out.shape[1]
    row = lax.broadcasted_iota(jnp.int32, (tok, tok), 0)
    col = lax.broadcasted_iota(jnp.int32, (tok, tok), 1)
    tri[...] = (col <= row).astype(F32).astype(BF16)
    begins = jnp.broadcast_to(row_of(starts_ref).astype(F32), (LANES, tok)).astype(BF16)
    doc_col = mm(tri[...], begins, NT)
    doc_row = mm(begins[:16], tri[...], NT)[:8]
    docr_ref[...] = doc_row
    docc_ref[...] = doc_col
    wide[...] = jnp.zeros_like(wide)
    wide[:heads] = decay_ref[...]
    lam_col = jnp.zeros((tok, LANES), F32)
    lam_row = jnp.zeros((16, tok), F32)
    for part in split_parts(wide[...], 2):
        lam_col = lam_col + mm(tri[...], part, NT)
        lam_row = lam_row + mm(part[:16], tri[...], NT)
    lamr_ref[...] = jnp.zeros_like(lamr_ref)
    for p in range(head_pairs):
        lamr_ref[8 * p : 8 * p + 2] = lam_row[2 * p : 2 * p + 2]
        lamc_ref[p * tok : (p + 1) * tok] = lam_col if p == 0 else pltpu.roll(lam_col, LANES - 2 * p, 1)
    ones = jnp.ones((tok, LANES), BF16)
    alike = doc_col[:, :1] == doc_row[:1]
    same[...] = jnp.where(alike & (col <= row), 1.0, 0.0).astype(BF16)
    behind = mm(same[...], ones)
    dist_ref[...] = jnp.where(doc_col == 0.0, FAR, behind - 1.0)
    lam_end = lam_col[tok - 1 :]
    doc_end = doc_col[tok - 1 :]
    first = jnp.where(doc_col == 0.0, jnp.exp(-lam_col), 0.0)
    last = jnp.where(doc_col == doc_end, jnp.exp(lam_col - lam_end), 0.0)
    spread = (lax.broadcasted_iota(jnp.int32, (LANES, width), 0)
              == lax.broadcasted_iota(jnp.int32, (LANES, width), 1) // (width // heads))
    spread = spread.astype(F32).astype(BF16)
    for ref, value in ((first_out, first), (last_out, last)):
        parts = split_parts(value, 2)
        ref[...] = mm(parts[0], spread) + mm(parts[1], spread)
    wide[:heads] = jnp.sqrt(one_less_exp(2.0 * jnp.minimum(decay_ref[...], RATE_CAP)))
    eye = (row == col).astype(F32).astype(BF16)
    beta_col = jnp.zeros((tok, LANES), F32)
    for part in split_parts(wide[...], 2):
        beta_col = beta_col + mm(eye, part, NT)
    parts = split_parts(beta_col, 2)
    beta_out[...] = mm(parts[0], spread) + mm(parts[1], spread)
    gate_out[...] = jnp.broadcast_to(first_out[tok - 1 :], gate_out.shape).astype(BF16)


def row_of(ref):
    return ref[...].reshape(1, ref.shape[0])


def norm_rows(rows_in):
    count = rows_in.shape[1]
    center = rows_in - jnp.sum(rows_in, axis=1, keepdims=True) * (1.0 / count)
    spread = jnp.sum(center * center, axis=1, keepdims=True) * (1.0 / count)
    inverse = lax.rsqrt(spread + NORM_EPS)
    return center * inverse, inverse


def norm_back(grad_rows, unit_rows, inverse, gain_vec):
    scale = 1.0 / grad_rows.shape[1]
    scaled = grad_rows * gain_vec
    return inverse * (scaled - jnp.sum(scaled, axis=1, keepdims=True) * scale
                      - unit_rows * (jnp.sum(scaled * unit_rows, axis=1, keepdims=True) * scale))


def by_rows(tok, body, size=512):
    def step(i, carry):
        body(pl.ds(pl.multiple_of(i * size, size), size))
        return carry

    lax.fori_loop(0, tok // size, step, 0)


def in_kernel(place_ref, own_ref, other_ref, gain_ref, bias_ref, wq_ref, wk_ref, wv_ref, docc_ref,
              normed_ref, q_ref, k_ref, v_ref, tail_ref, rows):
    h = place_ref[1]
    tok, width = own_ref.shape
    half_of(rows, h, width)[...] = own_ref[...]
    half_of(rows, 1 - h, width)[...] = other_ref[...]

    def norm(at):
        unit, _ = norm_rows(rows[at].astype(F32))
        normed_ref[at] = (unit * row_of(gain_ref) + row_of(bias_ref)).astype(BF16)

    by_rows(tok, norm)
    normed = normed_ref[...]
    k_ref[...] = mm(normed, wk_ref[...]).astype(BF16)
    keep = docc_ref[tok - STEP :] == docc_ref[tok - 1 :]
    for l in lanes(width):
        tail_ref[:, l : l + LANES] = jnp.where(
            keep, k_ref[tok - STEP :, l : l + LANES].astype(F32), 0.0).astype(BF16)
    q_ref[...] = mm(normed, wq_ref[...]).astype(BF16)
    v_ref[...] = mm(normed, wv_ref[...]).astype(BF16)


def filter_chunk(keys, taps, dist, count, t0):
    def group(a, acc):
        acc = list(acc)
        for b in range(32):
            j = a * 32 + b
            keep = dist >= j.astype(F32)
            for l in range(count):
                x = keys[l, pl.ds(STEP + t0 - a * 32 - b, STEP), :]
                acc[l] = acc[l] + jnp.where(keep, x * taps[l, pl.ds(j, 1), :], 0.0)
        return tuple(acc)

    return lax.fori_loop(0, STEP // 32, group, tuple(jnp.zeros((STEP, LANES), F32) for _ in range(count)))


def filter_kernel(k_ref, taps_ref, dist_ref, beta_ref, out_ref, keys, taps):
    tok, width = k_ref.shape
    count = width // LANES
    for l in range(count):
        keys[l, STEP:] = k_ref[:, l * LANES : (l + 1) * LANES].astype(F32)
        taps[l] = taps_ref[:, l * LANES : (l + 1) * LANES].astype(F32)
    out_ref[:STEP] = jnp.zeros((STEP, width), BF16)

    def chunk(c, carry):
        t0 = pl.multiple_of(c * STEP, STEP)
        at = pl.ds(t0, STEP)
        acc = filter_chunk(keys, taps, dist_ref[at], count, t0)
        for l in range(count):
            span = slice(l * LANES, (l + 1) * LANES)
            out_ref[at, span] = (acc[l] * beta_ref[at, span]).astype(BF16)
        return carry

    lax.fori_loop(1, tok // STEP, chunk, 0)


def fold(square, low):
    return jnp.where(low, square[:STEP], square[STEP:])


def unfold(flat, low):
    return jnp.concatenate([jnp.where(low, flat, 0.0), jnp.where(low, 0.0, flat)], axis=0)


def low_lanes(rows):
    return lax.broadcasted_iota(jnp.int32, (rows, LANES), 1) < STEP


def state_kernel(part_ref, tail_ref, k_ref, taps_ref, dist_ref, beta_ref, last_ref, v_ref, gate_ref,
                 sk_ref, message_ref, keys, taps):
    tok, width = part_ref.shape
    count = width // LANES
    for l in range(count):
        span = slice(l * LANES, (l + 1) * LANES)
        keys[l, :STEP] = tail_ref[:, span].astype(F32)
        keys[l, STEP:] = k_ref[:STEP, span].astype(F32)
        taps[l] = taps_ref[:, span].astype(F32)
    sk_ref[...] = part_ref[...]
    acc = filter_chunk(keys, taps, dist_ref[:STEP], count, 0)
    low = low_lanes(STEP)
    for l in range(count):
        span = slice(l * LANES, (l + 1) * LANES)
        sk_ref[:STEP, span] = (acc[l] * beta_ref[:STEP, span]).astype(BF16)
        weighted = (sk_ref[:, span].astype(F32) * last_ref[:, span]).astype(BF16)
        message_ref[:STEP, span] = fold(mm(weighted, v_ref[:, span], TN), low).astype(BF16)
    message_ref[STEP:] = gate_ref[...]


def kept_pairs(docc_ref, docr_ref):
    tok = docc_ref.shape[0]
    order = lax.broadcasted_iota(jnp.int32, (tok, tok), 0) >= lax.broadcasted_iota(jnp.int32, (tok, tok), 1)
    return (docc_ref[:, :1] == docr_ref[:1]) & order


def own_lanes(x, low, e):
    return jnp.where(low if e == 0 else ~low, x.astype(F32), 0.0).astype(BF16)


def decay_of(lamr_ref, lamc_ref, keep, e):
    span = jnp.minimum(lamr_ref[e : e + 1] - lamc_ref[:, e : e + 1], 0.0)
    return jnp.where(keep, jnp.exp(span), 0.0)


def inside_kernel(q_ref, k_ref, v_ref, lamr_ref, lamc_ref, docr_ref, docc_ref, out_ref):
    low = low_lanes(q_ref.shape[0])
    keep = kept_pairs(docc_ref, docr_ref)
    outs = []
    for e in range(2):
        score = mm(own_lanes(q_ref[...], low, e), k_ref[...], NT)
        outs.append(mm((score * decay_of(lamr_ref, lamc_ref, keep, e)).astype(BF16), v_ref[...]))
    out_ref[...] = jnp.where(low, outs[0], outs[1])


def mixed_kernel(stage, place_ref, inside_ref, q_ref, first_ref, *refs):
    (state_ref, mixed_ref) = refs[-2:]
    before, _ = link(stage, False, place_ref, refs[: stage[1]], refs[stage[1] : -2], False)
    state_ref[...] = before[1]
    low = low_lanes(STEP)
    for l in lanes(q_ref.shape[1]):
        span = slice(l, l + LANES)
        square = unfold(state_ref[:, span], low).astype(BF16)
        mixed_ref[:, span] = (0.125 * (inside_ref[:, span] + first_ref[:, span] * mm(q_ref[:, span], square))
                              ).astype(BF16)


def hidden_grad_kernel(place_ref, own_ref, other_ref, down_ref, out_ref, full_ref):
    @pl.when(pl.program_id(0) == 0)
    def _():
        width = own_ref.shape[1]
        half_of(full_ref, place_ref[1], width)[...] = own_ref[...]
        half_of(full_ref, 1 - place_ref[1], width)[...] = other_ref[...]

    out_ref[...] = mm(full_ref[...], down_ref[...]).astype(BF16)


def ffn_kernel(place_ref, own_ref, other_ref, mix_own_ref, mix_other_ref, out_own_ref, out_other_ref, gain_ref,
               bias_ref, up_ref, hg_ref, resid_ref, normed_ref, hidden_ref, pre_ref, part_ref, rows, acc):
    h = place_ref[1]
    step = pl.program_id(0)
    tok, width = own_ref.shape

    @pl.when(step == 0)
    def _():
        half_of(rows, h, width)[...] = own_ref[...]
        half_of(rows, 1 - h, width)[...] = other_ref[...]
        resid_ref[...] = mm(mix_own_ref[...], out_own_ref[...], NT) + mm(mix_other_ref[...], out_other_ref[...], NT)

        def norm(at):
            resid = rows[at].astype(F32) + resid_ref[at]
            resid_ref[at] = resid
            unit, _ = norm_rows(resid)
            normed_ref[at] = (unit * row_of(gain_ref) + row_of(bias_ref)).astype(BF16)

        by_rows(tok, norm)
        acc[...] = jnp.zeros_like(acc)

    pre = mm(normed_ref[...], up_ref[...])
    square = pre * pre
    bent = jnp.tanh(GELU_SCALE * (pre + GELU_CUBE * (square * pre)))
    outer = 0.5 * (1.0 + bent)
    hidden_ref[...] = (pre * outer).astype(BF16)
    slope = outer + 0.5 * pre * (1.0 - bent * bent) * (GELU_SCALE * (1.0 + 3.0 * GELU_CUBE * square))
    pre_ref[...] = (hg_ref[...].astype(F32) * slope).astype(BF16)
    acc[...] += mm(pre_ref[...], up_ref[...], NT)

    @pl.when(step == pl.num_programs(0) - 1)
    def _():
        part_ref[...] = acc[...].astype(BF16)


def norm2_kernel(place_ref, part_ref, got_ref, resid_ref, grad_ref, gain_ref, out_w_ref, q_ref, first_ref,
                 gate_ref, resid_grad_ref, branch_ref, g_ref, sums_ref, message_ref, rows):
    h = place_ref[1]
    tok, width = q_ref.shape
    sums_ref[...] = jnp.zeros_like(sums_ref)

    def norm(at):
        back = part_ref[at].astype(F32) + got_ref[at].astype(F32)
        unit, inverse = norm_rows(resid_ref[at])
        grad = grad_ref[at].astype(F32) + norm_back(back, unit, inverse, row_of(gain_ref))
        rows[at] = grad
        branch_ref[at] = grad.astype(BF16)
        sums_ref[0:1] += jnp.sum(back * unit, axis=0, keepdims=True)
        sums_ref[1:2] += jnp.sum(back, axis=0, keepdims=True)

    by_rows(tok, norm)
    resid_grad_ref[...] = half_of(rows, h, width)[...]
    g_ref[...] = (0.125 * mm(branch_ref[...], out_w_ref[...]).astype(BF16).astype(F32)).astype(BF16)
    low = low_lanes(STEP)
    for l in lanes(width):
        span = slice(l, l + LANES)
        weighted = (q_ref[:, span].astype(F32) * first_ref[:, span]).astype(BF16)
        message_ref[:STEP, span] = fold(mm(weighted, g_ref[:, span], TN), low).astype(BF16)
    message_ref[STEP:] = gate_ref[...]


def back_kernel(q_ref, k_ref, v_ref, g_ref, lamr_ref, lamc_ref, docr_ref, docc_ref, first_ref, state_ref,
                dq_ref, dk_ref, dv_ref):
    low = low_lanes(q_ref.shape[0])
    keep = kept_pairs(docc_ref, docr_ref)
    square = unfold(state_ref[...], low_lanes(STEP)).astype(BF16)
    outs = []
    for e in range(2):
        decay = decay_of(lamr_ref, lamc_ref, keep, e)
        prob = (mm(own_lanes(q_ref[...], low, e), k_ref[...], NT) * decay).astype(BF16)
        score = (mm(own_lanes(g_ref[...], low, e), v_ref[...], NT) * decay).astype(BF16)
        outs.append((mm(score, k_ref[...]), mm(score, q_ref[...], TN), mm(prob, g_ref[...], TN)))
    from_state = first_ref[...] * mm(g_ref[...], square, NT)
    dq_ref[...] = (jnp.where(low, outs[0][0], outs[1][0]) + from_state).astype(BF16)
    dk_ref[...] = jnp.where(low, outs[0][1], outs[1][1])
    dv_ref[...] = jnp.where(low, outs[0][2], outs[1][2])


def filter_back_chunk(sg, keys, taps, ahead, sums, count, s0):
    held = [keys[l, pl.ds(s0, SPAN), :] for l in range(count)]

    def group(a, acc):
        acc = list(acc)
        for b in range(32):
            j = a * 32 + b
            keep = ahead > j.astype(F32)
            for l in range(count):
                u = jnp.where(keep, sg[l, pl.ds(s0 + a * 32 + b, SPAN), :], 0.0)
                acc[l] = acc[l] + u * taps[l, pl.ds(j, 1), :]
                sums[l, j] += jnp.sum((held[l] * u).reshape(SPAN // 8, 8, LANES), axis=0)
        return tuple(acc)

    return lax.fori_loop(0, STEP // 32, group, tuple(jnp.zeros((SPAN, LANES), F32) for _ in range(count)))


def reach(docr_ref, docc_ref, ahead_ref):
    tok = docc_ref.shape[0]
    order = lax.broadcasted_iota(jnp.int32, (tok, tok), 0) <= lax.broadcasted_iota(jnp.int32, (tok, tok), 1)
    same = jnp.where((docc_ref[:, :1] == docr_ref[:1]) & order, 1.0, 0.0).astype(BF16)
    ahead_ref[STEP:] = mm(same, jnp.ones((tok, LANES), BF16))
    unbroken = jnp.sum(jnp.where(docr_ref[:1] == 0.0, 1.0, 0.0), axis=1, keepdims=True)
    ahead_ref[:STEP] = unbroken + STEP - lax.broadcasted_iota(jnp.int32, (STEP, LANES), 0).astype(F32)


def carry_kernel(stage, place_ref, dk_ref, dv_ref, k_ref, v_ref, last_ref, beta_ref, docr_ref, docc_ref, taps_ref,
                 tail_ref, *refs):
    value_ref, sg_ref, edge_ref, sums, ahead_ref, taps, keys = refs[-7:]
    reach(docr_ref, docc_ref, ahead_ref)
    before, _ = link(stage, True, place_ref, refs[: stage[1]], refs[stage[1] : -7], False)
    state = before[1]
    tok, width = dk_ref.shape
    count = width // LANES
    low = low_lanes(STEP)
    for l in range(count):
        span = slice(l * LANES, (l + 1) * LANES)
        square = unfold(state[:, span], low).astype(BF16)
        last = last_ref[:, span]
        value_ref[:, span] = (dv_ref[:, span] + last * mm(k_ref[:, span], square)).astype(BF16)
        sg_ref[l, :STEP] = jnp.zeros((STEP, LANES), F32)
        sg_ref[l, STEP : STEP + tok] = beta_ref[:, span] * (
            dk_ref[:, span] + last * mm(v_ref[:, span], square, NT))
        sg_ref[l, STEP + tok :] = jnp.zeros((STEP, LANES), F32)
        keys[l] = tail_ref[:, span].astype(F32)
        taps[l] = taps_ref[:, span].astype(F32)
    sums[...] = jnp.zeros_like(sums)
    for s0 in range(0, STEP, SPAN):
        at = slice(s0, s0 + SPAN)
        acc = filter_back_chunk(sg_ref, keys, taps, ahead_ref[at], sums, count, s0)
        for l in range(count):
            edge_ref[at, l * LANES : (l + 1) * LANES] = acc[l].astype(BF16)


def filter_back_kernel(sg_ref, k_ref, ahead_ref, taps_ref, sums_in, grad_ref, taps_grad_ref, keys, taps, sums):
    tok, width = k_ref.shape
    count = width // LANES
    for l in range(count):
        span = slice(l * LANES, (l + 1) * LANES)
        keys[l, STEP:] = k_ref[:, span].astype(F32)
        taps[l] = taps_ref[:, span].astype(F32)
    sums[...] = sums_in[...]

    def chunk(c, carry):
        s0 = pl.multiple_of(c * SPAN, SPAN)
        acc = filter_back_chunk(sg_ref, keys, taps, ahead_ref[pl.ds(s0, SPAN)], sums, count, s0)
        for l in range(count):
            grad_ref[pl.ds(s0 - STEP, SPAN), l * LANES : (l + 1) * LANES] = acc[l]
        return carry

    lax.fori_loop(STEP // SPAN, (tok + STEP) // SPAN, chunk, 0)
    for l in range(count):
        taps_grad_ref[:, l * LANES : (l + 1) * LANES] = jnp.sum(sums[l], axis=1)


def out_kernel(place_ref, grad_ref, edge_ref, docc_ref, dq_ref, dv_ref, wq_ref, wk_ref, wv_ref, own_ref, other_ref,
               key_ref, part_ref, rows, total, sums_ref):
    h = place_ref[1]
    tok, width = own_ref.shape
    keep = docc_ref[tok - STEP :] == docc_ref[tok - 1 :]
    key_ref[: tok - STEP] = grad_ref[: tok - STEP].astype(BF16)
    for l in lanes(width):
        span = slice(l, l + LANES)
        edge = jnp.where(keep, edge_ref[:, span].astype(F32), 0.0)
        key_ref[tok - STEP :, span] = (grad_ref[tok - STEP :, span] + edge).astype(BF16)
    total[...] = (mm(dq_ref[...], wq_ref[...], NT) + mm(dv_ref[...], wv_ref[...], NT)
                  + mm(key_ref[...], wk_ref[...], NT))
    part_ref[:tok] = total[...].astype(BF16)
    half_of(rows, h, width)[...] = own_ref[...]
    half_of(rows, 1 - h, width)[...] = other_ref[...]
    sums_ref[...] = jnp.zeros_like(sums_ref)

    def norm(at):
        unit, _ = norm_rows(rows[at].astype(F32))
        sums_ref[0:1] += jnp.sum(total[at] * unit, axis=0, keepdims=True)
        sums_ref[1:2] += jnp.sum(total[at], axis=0, keepdims=True)

    by_rows(tok, norm)
    part_ref[tok:] = sums_ref[...].astype(BF16)


def key_grads_kernel(place_ref, normed_ref, key_ref, taps_ref, sums2_ref, part_ref, got_ref, keep, send, total, shared):
    put_rows(total, 0, mm(normed_ref[...], key_ref[...], TN))
    tok, width = key_ref.shape
    shared[STEP:] = jnp.zeros_like(shared[STEP:])
    shared[:STEP] = taps_ref[...]
    sums1 = part_ref[tok:].astype(F32) + got_ref[tok:].astype(F32)
    for at, sums in ((STEP, sums1), (STEP + 2, sums2_ref[...])):
        shared[at : at + 2] = jnp.where(place_ref[1] == 0, sums[:2, :width], sums[:2, width:])
    put_messages(place_ref, 0, total.shape[0], total, shared[...], keep, send)


def input_kernel(place_ref, part_ref, got_ref, own_ref, other_ref, gain_ref, resid_grad_ref, out_ref, rows, back):
    h = place_ref[1]
    tok, width = own_ref.shape
    half_of(rows, h, width)[...] = own_ref[...]
    half_of(rows, 1 - h, width)[...] = other_ref[...]

    def norm(at):
        unit, inverse = norm_rows(rows[at].astype(F32))
        grad = part_ref[at].astype(F32) + got_ref[at].astype(F32)
        back[at] = norm_back(grad, unit, inverse, row_of(gain_ref))

    by_rows(tok, norm)
    out_ref[...] = (half_of(back, h, width)[...] + resid_grad_ref[...]).astype(BF16)


def local(block_input, starts, decay_rate, norm1_gain, norm1_bias, q_weight, k_weight, v_weight,
          shift_kernel, out_weight, norm2_gain, norm2_bias, up_weight, down_weight, out_grad):
    tok, width = block_input.shape
    heads = decay_rate.shape[0]
    full = 2 * width
    hidden_width = up_weight.shape[1]
    count = width // LANES
    seqs = lax.axis_size("seq")
    place = jnp.stack([lax.axis_index("seq"), lax.axis_index("head")]).astype(jnp.int32)
    gain1, bias1, gain2, bias2 = norm1_gain, norm1_bias, norm2_gain, norm2_bias
    vm = pltpu.VMEM

    stages = digits_of(seqs)
    other_input = swapped(block_input)
    other_grad = swapped(out_grad)
    other_out = swapped(out_weight)
    lamr, lamc, docr, docc, dist, beta_w, first_w, last_w, gate_w = run(
        side_kernel,
        (shape((8 * count, tok), F32), shape((count * tok, LANES), F32), shape((8, tok), F32),
         shape((tok, LANES), F32), shape((tok, LANES), F32),
         shape((tok, width), F32), shape((tok, width), F32), shape((tok, width), F32), shape((16, width), BF16)),
        starts, decay_rate, far=(0, 1),
        scratch=[vm((tok, tok), BF16), vm((tok, tok), BF16), vm((LANES, tok), F32)], us=2.7)
    other_input = after(other_input, docc)
    normed1, query, key, value, tail = run(
        in_kernel,
        (shape((tok, full), BF16),) + (shape((tok, width), BF16),) * 3 + (shape((STEP, width), BF16),),
        place, block_input, other_input, gain1, bias1, q_weight, k_weight, v_weight, docc,
        scratch=[vm((tok, full), BF16)], scalars=1, us=3.0)
    prev_tail = passed_along(tail, 1)
    scaled_part = run(
        filter_kernel, shape((tok, width), BF16), key, shift_kernel, dist, beta_w,
        scratch=[vm((count, tok + STEP, LANES), F32), vm((count, STEP, LANES), F32)], us=5.4)
    prev_tail = after(prev_tail, scaled_part)
    scaled, message = run(
        state_kernel, (shape((tok, width), BF16), shape((STEP + 16, width), BF16)),
        scaled_part, prev_tail, key, shift_kernel, dist, beta_w, last_w, value, gate_w,
        scratch=[vm((count, 2 * STEP, LANES), F32), vm((count, STEP, LANES), F32)], us=1.7)
    pair_spec = pl.BlockSpec((tok, LANES), lambda p: (0, p))
    lamr_spec = pl.BlockSpec((8, tok), lambda p: (p, 0))
    lamc_spec = pl.BlockSpec((tok, LANES), lambda p: (p, 0))
    state_spec = pl.BlockSpec((STEP, LANES), lambda p: (0, p))
    tile = 768

    before = ()
    got = scan_send(message, 0, False)
    hidden_grad, grad_full = run(
        hidden_grad_kernel, (shape((tok, hidden_width), BF16), shape((tok, full), BF16)),
        place, out_grad, after(other_grad, message), down_weight, scalars=1,
        grid=(hidden_width // tile,), in_specs=[None, None, pl.BlockSpec((full, tile), lambda i: (0, i))],
        out_specs=(pl.BlockSpec((tok, tile), lambda i: (0, i)), None), us=2.5)
    last_got = [after(g, hidden_grad) for g in got]
    for at in range(len(stages) - 1):
        before, message = scan_link(place, last_got, before, at, False)
        last_got = scan_send(message, at + 1, False)
    query_late = after(query, message)
    inside = run(
        inside_kernel, shape((tok, width), F32), query_late, scaled, value, lamr, lamc, docr, docc,
        grid=(count,),
        in_specs=[pair_spec] * 3 + [lamr_spec, lamc_spec, None, None], out_specs=pair_spec, us=3.5)
    last_got = [after(g, inside) for g in last_got]
    state, mixed = run(
        functools.partial(mixed_kernel, stages[-1]), (shape((STEP, width), F32), shape((tok, width), BF16)),
        place, inside, query, first_w, *last_got, *before, scalars=1, us=1.2)
    mixed_other = swapped(mixed)

    wide_tile = pl.BlockSpec((full, tile), lambda i: (0, i))
    tok_tile = pl.BlockSpec((tok, tile), lambda i: (0, i))
    resid, normed2, hidden, pre_grad, part2 = run(
        ffn_kernel,
        (shape((tok, full), F32), shape((tok, full), BF16), shape((tok, hidden_width), BF16),
         shape((tok, hidden_width), BF16), shape((tok, full), BF16)),
        place, block_input, other_input, mixed, mixed_other, out_weight, other_out, gain2, bias2, up_weight, hidden_grad,
        scratch=[vm((tok, full), BF16), vm((tok, full), F32)], scalars=1, mib=24,
        grid=(hidden_width // tile,),
        in_specs=[None] * 8 + [wide_tile, tok_tile],
        out_specs=(None, None, tok_tile, tok_tile, None), us=10.8)
    got2 = swapped(part2)
    rows = full // seqs
    up_width = hidden_width + width
    down_keep, down_send, ffn_own, ffn_send = run(
        down_kernel,
        half_shapes(seqs, rows, hidden_width) + (shape((tok, width), F32), shape((tok, width), BF16)),
        place, grad_full, hidden, down_weight, resid, scalars=1,
        scratch=[vm((seqs, rows, hidden_width), BF16), vm((tok, full), F32)], mib=24, us=2.46)
    ffn_other = swapped(ffn_send)
    got2 = after(got2, ffn_own)
    resid_grad, branch, g_low, sums2, message = run(
        norm2_kernel,
        (shape((tok, width), F32), shape((tok, full), BF16), shape((tok, width), BF16), shape((8, full), F32),
         shape((STEP + 16, width), BF16)),
        place, part2, got2, resid, grad_full, gain2, out_weight, query, first_w, gate_w,
        scratch=[vm((tok, full), F32)], scalars=1, us=2.34)
    before = ()
    got = scan_send(message, 0, True)
    up_keep, up_send, block_output = run(
        functools.partial(up_kernel, (0, hidden_width)),
        half_shapes(seqs, rows, up_width) + (shape((tok, width), BF16),),
        place, after(normed2, message), branch, pre_grad, mixed, ffn_own, ffn_other, scalars=1,
        scratch=[vm((seqs, rows, up_width), BF16)], mib=24, us=1.92)
    got = [after(g, block_output) for g in got]
    for at in range(len(stages) - 1):
        before, message = scan_link(place, got, before, at, True)
        got = scan_send(message, at + 1, True)
    up_got = mirrored(after(up_send, message), 0)
    down_got = mirrored(after(down_send, message), 0, True)
    query_late = after(query, message)
    query_grad, dk_part, dv_part = run(
        back_kernel, (shape((tok, width), BF16), shape((tok, width), F32), shape((tok, width), F32)),
        query_late, scaled, value, g_low, lamr, lamc, docr, docc, first_w, state,
        grid=(count,),
        in_specs=[pair_spec] * 4 + [lamr_spec, lamc_spec, None, None, pair_spec, state_spec],
        out_specs=(pair_spec,) * 3, us=1.28)
    got = [after(g, query_grad) for g in got]
    value_grad, shifted_grad, edge, sums, ahead = run(
        functools.partial(carry_kernel, stages[-1]),
        (shape((tok, width), BF16), shape((count, tok + 2 * STEP, LANES), F32), shape((STEP, width), BF16),
         shape((count, STEP, 8, LANES), F32), shape((tok + STEP, LANES), F32)),
        place, dk_part, dv_part, scaled, value, last_w, beta_w, docr, docc, shift_kernel, prev_tail,
        *got, *before, scalars=1,
        scratch=[vm((count, STEP, LANES), F32), vm((count, STEP, LANES), F32)], us=1.5)
    got_edge = passed_along(edge, -1)
    mix_keep, mix_send = run(
        functools.partial(grads_kernel, (0, width)), half_shapes(seqs, rows, 2 * width),
        place, normed1, normed1, query_grad, after(value_grad, edge), scalars=1,
        scratch=[vm((seqs, rows, 2 * width), BF16)], us=1.14)
    mix_got = mirrored(mix_send, 0)
    up_keep, up_send = folded(place, up_keep, after(up_got, mix_keep), 0, (), 8)
    up_got = mirrored(up_send, 1)
    key_rows, taps_grad = run(
        filter_back_kernel, (shape((tok, width), F32), shape((STEP, width), F32)),
        shifted_grad, key, ahead, shift_kernel, after(sums, up_keep),
        scratch=[vm((count, tok + STEP, LANES), F32), vm((count, STEP, LANES), F32),
                 vm((count, STEP, 8, LANES), F32)], us=7.05)
    key_grad, part1 = run(
        out_kernel, (shape((tok, width), BF16), shape((tok + 8, full), BF16)),
        place, key_rows, after(got_edge, key_rows), docc, query_grad, value_grad, q_weight, k_weight, v_weight,
        block_input, other_input,
        scratch=[vm((tok, full), BF16), vm((tok, full), F32), vm((8, full), F32)], scalars=1, us=2.16)
    got1 = swapped(part1)
    up_keep, up_send = folded(place, up_keep, after(up_got, key_grad), 1, (), 0.5)
    up_got = mirrored(up_send, 2)
    mix_keep, mix_send = folded(place, mix_keep, after(mix_got, up_keep), 0, (), 1)
    mix_got = mirrored(mix_send, 1)
    down_keep, down_send = folded(place, down_keep, after(down_got, mix_keep), 0, (), 1, True)
    down_got = mirrored(down_send, 1, True)
    key_keep, key_send = run(
        key_grads_kernel, (shape((seqs // 2 * rows + STEP + 8, width), BF16),) * 2,
        place, normed1, key_grad, taps_grad, sums2, part1, after(got1, down_keep), scalars=1,
        scratch=[vm((seqs, rows, width), BF16), vm((STEP + 8, width), F32)], us=0.78)
    key_got = mirrored(key_send, 0)
    input_grad = run(
        input_kernel, shape((tok, width), BF16),
        place, part1, after(got1, key_keep), block_input, other_input, gain1, resid_grad, scalars=1,
        scratch=[vm((tok, full), BF16), vm((tok, full), F32)], us=0.89)
    mix_keep, mix_send = folded(place, mix_keep, after(mix_got, input_grad), 1, (), 8)
    mix_got = mirrored(mix_send, 2)
    down_keep, down_send = folded(place, down_keep, after(down_got, mix_keep), 1, (), 1, True)
    down_got = mirrored(down_send, 2, True)
    up_keep, up_send = folded(place, up_keep, after(up_got, down_keep), 2, (), 0.2)
    up_got = mirrored(up_send, 3)
    key_keep, key_send = folded_message(place, key_keep, after(key_got, up_keep), 0, rows, 4)
    key_got = mirrored(key_send, 1)
    down_keep, down_send = folded(place, down_keep, after(down_got, key_keep), 2, (), 4, True)
    down_got = mirrored(down_send, 3, True)
    mix_keep, mix_send = folded(place, mix_keep, after(mix_got, down_keep), 2, (), 4)
    mix_got = mirrored(mix_send, 3)
    key_keep, key_send = folded_message(place, key_keep, after(key_got, mix_keep), 1, rows, 2)
    key_got = mirrored(key_send, 2)
    up_total, out_total = folded_last(place, up_keep, after(up_got, key_keep), 3, (hidden_width, width), 1)
    key_keep, key_send = folded_message(place, key_keep, after(key_got, up_total), 2, rows, 8)
    key_got = mirrored(key_send, 3)
    (down_total,) = folded_last(place, down_keep, after(down_got, key_keep), 3, (hidden_width,), 0.2, True)
    key_got = after(key_got, down_total)
    for at in range(3, len(strides_of(seqs)) - 1):
        key_keep, key_send = folded_message(place, key_keep, key_got, at, rows, 8)
        key_got = mirrored(key_send, at + 1)
    k_total, taps_total, vectors = folded_message(
        place, key_keep, key_got, len(strides_of(seqs)) - 1, rows, 0.5)
    other_vectors = swapped(vectors)
    mix_got = after(mix_got, vectors)
    for at in range(3, len(strides_of(seqs)) - 1):
        mix_keep, mix_send = folded(place, mix_keep, mix_got, at, (), 0.5)
        mix_got = mirrored(mix_send, at + 1)
    q_total, v_total, gain1_grad, bias1_grad, gain2_grad, bias2_grad = run(
        functools.partial(end_kernel, (width, width)), (shape((rows, width), F32),) * 2 + (shape((full,), F32),) * 4,
        place, mix_keep, mix_got, vectors, other_vectors, scalars=1, us=0.5)
    return (block_output, input_grad, gain1_grad, bias1_grad, q_total, k_total, v_total, taps_total, out_total,
            gain2_grad, bias2_grad, up_total, down_total)


def solution(mesh):
    both, head = P("seq", "head"), P(None, "head")
    in_specs = (both, P("seq"), P("head", "seq"), P(), P(), head, head, head, head, head, P(), P(), head, head, both)
    out_specs = (both, both, P(), P(), both, both, both, head, both, P(), P(), both, both)
    return jax.shard_map(local, mesh=mesh, in_specs=in_specs, out_specs=out_specs, check_vma=False)
```
